32 devices in a mesh: wide: 8 (over z, x), narrow: 4 (over y, core).
Axes of the slice: x: 2, y: 2, z: 4, core: 2. Of those that a mesh axis runs over, the one named last changes fastest.
Arguments:
- images: bfloat16 [128, 50, 1024], P(('wide', 'narrow')), may hold values from -6 to 6
- cotangent: bfloat16 [128, 50, 1024], P(('wide', 'narrow')), may hold values from -6 to 6
- kept_tokens: int32 [128, 50], P('wide'), may hold values from 0 to 1, as said below
- owner_slots: int32 [2, 768], replicated, may hold values from 0 to 767, as said below
- master_blocks: float32 [2, 768, 128, 128], P(None, ('wide', 'narrow')), may hold values from -0.75 to 0.75
- small_params: float32 [2, 12288], P(None, ('wide', 'narrow')), may hold values from -1.2 to 1.4
- left_basis: float32 [2, 768, 128, 128], P(None, ('wide', 'narrow')), may hold values from -0.5 to 0.5
- right_basis: float32 [2, 768, 128, 128], P(None, ('wide', 'narrow')), may hold values from -0.5 to 0.5
- first_moment: float32 [2, 768, 128, 128], P(None, ('wide', 'narrow')), may hold values from -0.0011954564 to 0.0011954564
- second_moment: float32 [2, 768, 128, 128], P(None, ('wide', 'narrow')), may hold values from 1.9848832e-08 to 1.5879066e-07
- small_first: float32 [2, 12288], P(None, ('wide', 'narrow')), may hold values from -0.0047818255 to 0.0047818255
- small_second: float32 [2, 12288], P(None, ('wide', 'narrow')), may hold values from 3.175813e-07 to 2.5406505e-06
Outputs:
- block_output: bfloat16 [128, 50, 1024], P(('wide', 'narrow'))
- input_grad: float32 [128, 50, 1024], P(('wide', 'narrow'))
- grad_norm: float32 [1], replicated
- new_first: float32 [2, 768, 128, 128], P(None, ('wide', 'narrow'))
- new_second: float32 [2, 768, 128, 128], P(None, ('wide', 'narrow'))
- new_master: float32 [2, 768, 128, 128], P(None, ('wide', 'narrow'))
- new_weights_bf16: bfloat16 [2, 768, 128, 128], P(None, ('wide', 'narrow'))
- new_small_first: float32 [2, 12288], P(None, ('wide', 'narrow'))
- new_small_second: float32 [2, 12288], P(None, ('wide', 'narrow'))
- new_small: float32 [2, 12288], P(None, ('wide', 'narrow'))
- new_small_bf16: bfloat16 [2, 12288], P(None, ('wide', 'narrow'))
The draws below stay inside these ranges and needn't reach their ends.
Inputs may be any that keep to these rules, and one draw needn't show every extreme that they name: `kept_tokens`: each image keeps at least 25 of its tokens; some image keeps all of them and some exactly 25. `owner_slots`: each row is a permutation of the slots 0 to 767. Call the share of a tile j, where a QKV tile in column c has j = (c % 8) // 2, an output tile in row r has j = r // 2, an up tile in column c has j = c // 8 and a down tile in row r has j = r // 8. Every tile of share j lies in a slot s with (s // 24) % 4 = j.
All inputs are finite; a program needn't handle non-finite values.
Results may differ from the reference program's by a relative error of at most 0.02.
Values may be sent and summed in bfloat16 or wider, within the bound.
No kernel may reach another device: no remote copies, remote signals or barrier semaphores. Data moves between devices by JAX's collectives and lax.ppermute only.
A program may use at most 192 MiB of HBM per device.

```python
import math
import jax
import jax.numpy as jnp
from jax import lax

D = 1024
HEADS = 16
HEAD_DIM = 64
FF = 4096
S = 50
IMG_DEV = 4
LAYERS = 2
BLK = 128
IMAGES = 128
NBLK = 768
NSMALL = 12288
NPAR = 25190400
N_WIDE = 8
N_NARROW = 4


def tile_ids(shard):
    tile_rows = D // BLK
    shard_cols = D // (N_NARROW * BLK)
    shard_hidden = FF // (N_NARROW * BLK)
    count_qkv = tile_rows * 3 * tile_rows
    start_up = count_qkv + tile_rows * tile_rows
    start_down = start_up + tile_rows * (FF // BLK)
    row_part = jnp.arange(tile_rows)[:, None, None]
    third = jnp.arange(3)[None, :, None]
    column_part = jnp.arange(shard_cols)[None, None, :]
    qkv_ids = (row_part * 3 * tile_rows + third * tile_rows + shard * shard_cols + column_part).reshape(-1)
    out_ids = (count_qkv + (shard * shard_cols + jnp.arange(shard_cols)[:, None]) * tile_rows + jnp.arange(tile_rows)[None, :]).reshape(-1)
    up_ids = (start_up + jnp.arange(tile_rows)[:, None] * (FF // BLK) + shard * shard_hidden + jnp.arange(shard_hidden)[None, :]).reshape(-1)
    down_ids = (start_down + (shard * shard_hidden + jnp.arange(shard_hidden)[:, None]) * tile_rows + jnp.arange(tile_rows)[None, :]).reshape(-1)
    return jnp.concatenate([qkv_ids, out_ids, up_ids, down_ids]).astype(jnp.int32)


def owner_table(key):
    per_device = NBLK // (N_WIDE * N_NARROW)
    share_count = NBLK // N_NARROW
    layer_rows = []
    for which_layer in range(LAYERS):
        owners = jnp.zeros((NBLK,), jnp.int32)
        for shard in range(N_NARROW):
            ids = tile_ids(shard)
            slots = ((jnp.arange(N_WIDE)[:, None] * N_NARROW + shard) * per_device + jnp.arange(per_device)[None, :]).reshape(-1)
            order = jax.random.permutation(jax.random.fold_in(key, 1000 + which_layer * N_NARROW + shard), share_count)
            owners = owners.at[ids].set(jnp.take(slots, order).astype(jnp.int32))
        layer_rows.append(owners)
    return jnp.stack(layer_rows)


def draw_owner_slots(key, part):
    return owner_table(key)


def draw_master_blocks(key, part):
    owners = owner_table(key)
    block_ids = jnp.arange(NBLK)
    count_qkv = D // BLK * (3 * D // BLK)
    count_out = D // BLK * (D // BLK)
    count_up = D // BLK * (FF // BLK)
    scales = jnp.where(block_ids < count_qkv, D ** (-0.5), jnp.where(block_ids < count_qkv + count_out, 4.0 * D ** (-0.5), jnp.where(block_ids < count_qkv + count_out + count_up, D ** (-0.5), FF ** (-0.5))))
    layer_rows = jnp.arange(LAYERS)[:, None]
    slot_scale = jnp.zeros((LAYERS, NBLK), jnp.float32).at[layer_rows, owners].set(jnp.broadcast_to(scales.astype(jnp.float32), (LAYERS, NBLK)))
    noise_draw = jnp.clip(jax.random.normal(jax.random.fold_in(key, 102), (LAYERS, NBLK, BLK, BLK), jnp.float32), -6.0, 6.0)
    return noise_draw * slot_scale[:, :, None, None]


def draw_small_params(key, part):
    position = jnp.arange(NSMALL)[None, :]
    gain_zone = (position < D) | (position >= 5 * D) & (position < 6 * D)
    gains = jax.random.uniform(jax.random.fold_in(key, 103), (LAYERS, NSMALL), jnp.float32, 0.6, 1.4)
    biases = 0.2 * jnp.clip(jax.random.normal(jax.random.fold_in(key, 104), (LAYERS, NSMALL), jnp.float32), -6.0, 6.0)
    return jnp.where(gain_zone, gains, biases)


def draw_kept_tokens(key, part):
    counts = jax.random.randint(jax.random.fold_in(key, 105), (IMAGES,), S // 2, S + 1)
    counts = counts.at[0].set(S).at[1].set(S // 2)
    split_keys = jax.random.split(jax.random.fold_in(key, 106), IMAGES)
    ranking = jax.vmap(lambda sub_key: jax.random.permutation(sub_key, S))(split_keys)
    return (ranking < counts[:, None]).astype(jnp.int32)


def block_scale(own_key, dims, cuts, least, top_value):
    def one(dim, blocks):
        steps = jax.random.uniform(jax.random.fold_in(jax.random.fold_in(own_key, 6), dim), (blocks,), jnp.float32, least / len(cuts), top_value / len(cuts))
        return jnp.repeat(jnp.exp(steps), dims[dim] // blocks).reshape((-1,) + (1,) * (len(dims) - dim - 1))

    gain = one(*cuts[0])
    for cut in cuts[1:]:
        gain = gain * one(*cut)
    return gain


def gaussian(key, extent, width, limit, cuts=(), held_as=jnp.bfloat16):
    array = jax.random.normal(key, extent, jnp.float32) * width
    if len(cuts) > 0:
        array = block_scale(key, extent, cuts, -0.22, 0.18) * array
    return jnp.clip(array, min=-limit, max=limit).astype(held_as)


def setup_inputs(seed: int = 0) -> dict:
    key_of = jax.random.split(jax.random.key(seed), 13)
    return {
        "images": gaussian(key_of[0], (IMAGES, S, D), 1.0, 6.0, ((0, 32),)),
        "cotangent": gaussian(key_of[1], (IMAGES, S, D), 1.0, 6.0, ((0, 32),)),
        "kept_tokens": draw_kept_tokens(jax.random.fold_in(key_of[12], 71), 0),
        "owner_slots": draw_owner_slots(jax.random.fold_in(key_of[12], 71), 0),
        "master_blocks": draw_master_blocks(jax.random.fold_in(key_of[12], 71), 0),
        "small_params": draw_small_params(jax.random.fold_in(key_of[12], 71), 0),
        "left_basis": gaussian(key_of[6], (LAYERS, NBLK, BLK, BLK), BLK ** -0.5, 0.5, ((1, 32),), jnp.float32),
        "right_basis": gaussian(key_of[7], (LAYERS, NBLK, BLK, BLK), BLK ** -0.5, 0.5, ((1, 32),), jnp.float32),
        "first_moment": gaussian(key_of[8], (LAYERS, NBLK, BLK, BLK), (1.0 / NPAR ** 0.5), 0.0011954564, ((1, 32),), jnp.float32),
        "second_moment": jnp.clip(jnp.exp(math.log(1.5879065529134095e-07) - 2.0794415 * jax.random.uniform(key_of[9], (LAYERS, NBLK, BLK, BLK), jnp.float32) ** block_scale(key_of[9], (LAYERS, NBLK, BLK, BLK), ((1, 32),), -0.2, 0.2)), 1.984883191141762e-08, 1.5879065529134095e-07),
        "small_first": gaussian(key_of[10], (LAYERS, NSMALL), (4.0 / NPAR ** 0.5), 0.0047818255, ((1, 32),), jnp.float32),
        "small_second": jnp.clip(jnp.exp(math.log(2.5406504846614553e-06) - 2.0794415 * jax.random.uniform(key_of[11], (LAYERS, NSMALL), jnp.float32) ** block_scale(key_of[11], (LAYERS, NSMALL), ((1, 32),), -0.2, 0.2)), 3.175813105826819e-07, 2.5406504846614553e-06),
    }


@jax.custom_vjp
def low(v):
    return lax.optimization_barrier(v.astype(jnp.bfloat16)).astype(jnp.float32)

@jax.custom_vjp
def low_back(v):
    return v

def low_keep(v):
    return (low(v), None)

def low_pass(kept, grad):
    return (grad,)

def back_keep(v):
    return (v, None)

def back_low(kept, grad):
    return (low(grad),)
low.defvjp(low_keep, low_pass)
low_back.defvjp(back_keep, back_low)
precise = lax.Precision.HIGHEST

def layer_norm(hidden, gain_vec, offset):
    centre = hidden - lax.optimization_barrier(jnp.mean(hidden, axis=-1, keepdims=True))
    spread = lax.optimization_barrier(jnp.mean(centre * centre, axis=-1, keepdims=True))
    return centre * lax.rsqrt(spread + 1e-06) * gain_vec + offset

def round_both(value_in):
    return low(low_back(value_in))

def split_small(small_all):
    pieces = [small_all[piece_index * D:(piece_index + 1) * D] for piece_index in range(8)]
    return pieces + [small_all[8 * D:]]

def from_blocks(blocks, row_count, col_count):
    tiled = blocks.reshape(row_count // BLK, col_count // BLK, BLK, BLK)
    return tiled.transpose(0, 2, 1, 3).reshape(row_count, col_count)

def to_blocks(matrix):
    row_count, col_count = matrix.shape
    tiled = matrix.reshape(row_count // BLK, BLK, col_count // BLK, BLK)
    return tiled.transpose(0, 2, 1, 3).reshape(-1, BLK, BLK)

def matrices(ordered):
    count_qkv = D // BLK * (3 * D // BLK)
    count_out = D // BLK * (D // BLK)
    count_up = D // BLK * (FF // BLK)
    start_up = count_qkv + count_out
    start_down = start_up + count_up
    return (from_blocks(ordered[:count_qkv], D, 3 * D), from_blocks(ordered[count_qkv:start_up], D, D), from_blocks(ordered[start_up:start_down], D, FF), from_blocks(ordered[start_down:], FF, D))

def layer_apply(weights, hidden, kept_keys):
    w_qkv, w_out, w_up, w_down, small_all = weights
    gain_one, offset_one, bias_query, bias_value, bias_out, gain_two, offset_two, bias_down, bias_up = split_small(small_all)
    img_count = hidden.shape[0]
    normed = low(layer_norm(hidden, gain_one, offset_one))
    projected = jnp.einsum('nsd,de->nse', normed, w_qkv, precision=precise)
    queries = round_both(projected[..., :D] + bias_query).reshape(img_count, S, HEADS, HEAD_DIM)
    key_heads = round_both(projected[..., D:2 * D]).reshape(img_count, S, HEADS, HEAD_DIM)
    values = round_both(projected[..., 2 * D:] + bias_value).reshape(img_count, S, HEADS, HEAD_DIM)
    scores = low_back(jnp.einsum('nqhd,nkhd->nhqk', queries, key_heads, precision=precise) * HEAD_DIM ** (-0.5))
    scores = jnp.where(kept_keys[:, None, None, :] > 0, scores, -1e+30)
    attention = jax.nn.softmax(scores, axis=-1)
    attended = jnp.einsum('nhqk,nkhd->nqhd', low(attention), values, precision=precise).reshape(img_count, S, D)
    attended = round_both(attended)
    middle = hidden + low_back(jnp.einsum('nsc,cd->nsd', attended, w_out, precision=precise) + bias_out)
    normed_two = low(layer_norm(middle, gain_two, offset_two))
    upward = low_back(jnp.einsum('nsd,df->nsf', normed_two, w_up, precision=precise) + bias_up)
    activated = low(jax.nn.gelu(upward, approximate=False))
    return middle + low_back(jnp.einsum('nsf,fd->nsd', activated, w_down, precision=precise) + bias_down)

def forward(params, hidden, kept_keys):
    for weights in params:
        hidden = layer_apply(weights, hidden, kept_keys)
    return hidden

def rotate_in(left_basis, grads, right_basis):
    inner = jnp.einsum('lbki,lbkj->lbij', left_basis, grads, precision=precise)
    return jnp.einsum('lbij,lbjm->lbim', inner, right_basis, precision=precise)

def rotate_out(left_basis, update, right_basis):
    inner = jnp.einsum('lbik,lbkj->lbij', left_basis, update, precision=precise)
    return jnp.einsum('lbij,lbmj->lbim', inner, right_basis, precision=precise)

def reference(images, cotangent, kept_tokens, owner_slots, master_blocks, small_params, left_basis, right_basis, first_moment, second_moment, small_first, small_second):
    rounded = master_blocks.astype(jnp.bfloat16).astype(jnp.float32)
    small_round = small_params.astype(jnp.bfloat16).astype(jnp.float32)
    params = tuple((matrices(jnp.take(rounded[which_layer], owner_slots[which_layer], axis=0)) + (small_round[which_layer],) for which_layer in range(LAYERS)))
    group_size = IMG_DEV * N_NARROW
    groups = IMAGES // group_size
    image_groups = images.astype(jnp.float32).reshape(groups, group_size, S, D)
    cotangent_groups = cotangent.astype(jnp.float32).reshape(groups, group_size, S, D)
    kept_groups = kept_tokens.reshape(groups, group_size, S)

    def one_group(running, inputs):
        image_block, cotangent_block, kept_block = inputs

        def apply_all(layer_args, tokens):
            return forward(layer_args, tokens, kept_block)
        produced, back_func = jax.vjp(apply_all, params, image_block)
        param_grad, token_grad = back_func(cotangent_block)
        running = jax.tree.map(jnp.add, running, param_grad)
        return (running, (produced.astype(jnp.bfloat16), token_grad))
    start_grads = jax.tree.map(jnp.zeros_like, params)
    totals, (produced, token_grads) = lax.scan(one_group, start_grads, (image_groups, cotangent_groups, kept_groups))
    block_output = produced.reshape(IMAGES, S, D)
    input_grad = token_grads.reshape(IMAGES, S, D)
    block_list = []
    small_list = []
    for which_layer in range(LAYERS):
        grad_qkv, grad_out, grad_up, grad_down, grad_small = totals[which_layer]
        ordered = jnp.concatenate([to_blocks(grad_qkv), to_blocks(grad_out), to_blocks(grad_up), to_blocks(grad_down)], axis=0)
        slotted = jnp.zeros_like(ordered).at[owner_slots[which_layer]].set(ordered)
        block_list.append(slotted)
        small_list.append(grad_small)
    block_grad = jnp.stack(block_list)
    small_grad = jnp.stack(small_list)
    grad_norm = jnp.sqrt(jnp.sum(block_grad * block_grad) + jnp.sum(small_grad * small_grad))
    clip_factor = 1.0 / jnp.maximum(grad_norm, 1.0)
    rotated = rotate_in(left_basis, clip_factor * block_grad, right_basis)
    new_first = 0.5 * first_moment + 0.5 * rotated
    new_second = 0.5 * second_moment + 0.5 * rotated * rotated
    direction = new_first / (jnp.sqrt(new_second) + 1e-08)
    new_master = master_blocks - 0.02 * rotate_out(left_basis, direction, right_basis)
    clipped_small = clip_factor * small_grad
    new_small_first = 0.5 * small_first + 0.5 * clipped_small
    new_small_second = 0.5 * small_second + 0.5 * clipped_small * clipped_small
    new_small = small_params - 0.3 * new_small_first / (jnp.sqrt(new_small_second) + 1e-08)
    return (block_output, input_grad, grad_norm.reshape(1), new_first, new_second, new_master, new_master.astype(jnp.bfloat16), new_small_first, new_small_second, new_small, new_small.astype(jnp.bfloat16))
```

```python
import functools

import jax
import jax.numpy as jnp
from jax import lax
from jax.experimental import pallas as pl
from jax.experimental.pallas import tpu as pltpu
from jax.sharding import PartitionSpec as P

D = 1024
HEAD_DIM = 64
FF = 4096
S = 50
LAYERS = 2
BLK = 128
NARROW = 4

BF = jnp.bfloat16
F32 = jnp.float32

WID = D // 2
HID = FF // 2
SHARE_TILES = 192
ATT_ROWS = 2 * D
MLP_ROWS = 4 * D

CORE = [(j, j ^ 1) for j in range(NARROW)]
ACROSS = [(j, j ^ 2) for j in range(NARROW)]
ANY = pl.BlockSpec(memory_space=pl.ANY)
SMEM = pl.BlockSpec(memory_space=pltpu.SMEM)
VMEM = pl.BlockSpec(memory_space=pltpu.VMEM)


def params(mib):
    return pltpu.CompilerParams(vmem_limit_bytes=mib << 20)


def cost(flops, nbytes):
    return pl.CostEstimate(flops=flops, bytes_accessed=nbytes, transcendentals=0)


def dot(a, b):
    return jnp.dot(a, b, preferred_element_type=F32)


def dot_nt(a, b):
    return lax.dot_general(a, b, (((1,), (1,)), ((), ())), preferred_element_type=F32)


def dot_tn(a, b):
    return lax.dot_general(a, b, (((0,), (0,)), ((), ())), preferred_element_type=F32)


def stats(x):
    centre = x - jnp.mean(x, axis=-1, keepdims=True)
    spread = jnp.mean(centre * centre, axis=-1, keepdims=True)
    return centre, lax.rsqrt(spread + 1e-06)


def norm_back(grad, xhat, rstd, gain):
    gn = grad * gain
    return rstd * (
        gn
        - jnp.mean(gn, axis=-1, keepdims=True)
        - xhat * jnp.mean(gn * xhat, axis=-1, keepdims=True)
    )


def key_bias(kept_row, rows):
    def image_of(dim):
        pos = lax.broadcasted_iota(jnp.int32, (rows, rows), dim)
        image = jnp.zeros((rows, rows), jnp.int32)
        for edge in range(S, rows, S):
            image = image + (pos >= edge).astype(jnp.int32)
        return image

    allowed = (image_of(0) == image_of(1)) & (kept_row > 0.0)
    return jnp.where(allowed, 0.0, -1e30)


def lane_half(x, half):
    lane = lax.broadcasted_iota(jnp.int32, x.shape, 1)
    keep = (lane < HEAD_DIM) if half == 0 else (lane >= HEAD_DIM)
    return jnp.where(keep, x, jnp.zeros_like(x))


def attention_forward(first, *refs):
    if first:
        x_ref, vecs, kept, weights, n1_ref, qkv_ref, lse_ref, att_ref, part_ref = refs
        hidden = x_ref[...].astype(F32)
    else:
        (mid_ref, own_ref, got_ref, prev, vecs, kept, weights) = refs[:7]
        hidden_ref, n1_ref, qkv_ref, lse_ref, att_ref, part_ref = refs[7:]
        hidden = mid_ref[...] + (
            own_ref[...].astype(F32) + got_ref[...].astype(F32) + prev[6:7, :]
        )
        hidden_ref[...] = hidden
    rows = hidden.shape[0]
    centre, rstd = stats(hidden)
    n1 = (centre * rstd * vecs[0:1, :] + vecs[1:2, :]).astype(BF)
    n1_ref[...] = n1
    qkv_ref[:, 0:WID] = (dot(n1, weights[0:D, 0:WID]) + vecs[2:3, 0:WID]).astype(BF)
    qkv_ref[:, WID : 2 * WID] = dot(n1, weights[0:D, WID:D]).astype(BF)
    qkv_ref[:, 2 * WID :] = (dot(n1, weights[D : 2 * D, 0:WID]) + vecs[2:3, WID:D]).astype(BF)
    bias = key_bias(kept[0:1, :], rows)
    lane = lax.broadcasted_iota(jnp.int32, (rows, BLK), 1)
    lse_all = jnp.zeros((rows, BLK), F32)
    for pair in range(WID // BLK):
        cols = slice(pair * BLK, (pair + 1) * BLK)
        q = qkv_ref[:, cols] * jnp.asarray(0.125, BF)
        k = qkv_ref[:, WID + pair * BLK : WID + (pair + 1) * BLK]
        v = qkv_ref[:, 2 * WID + pair * BLK : 2 * WID + (pair + 1) * BLK]
        outs = []
        for half in range(2):
            scores = dot_nt(lane_half(q, half), k) + bias
            top = jnp.max(scores, axis=-1, keepdims=True)
            raised = jnp.exp(scores - top)
            total = jnp.sum(raised, axis=-1, keepdims=True)
            outs.append(dot((raised * (1.0 / total)).astype(BF), v))
            lse_all = jnp.where(lane == 2 * pair + half, top + jnp.log(total), lse_all)
        att_ref[:, cols] = jnp.where(lane < HEAD_DIM, outs[0], outs[1]).astype(BF)
    lse_ref[...] = lse_all
    att = att_ref[...]
    part_ref[:, 0:WID] = dot(att, weights[D : D + WID, WID:D]).astype(BF)
    part_ref[:, WID:D] = dot(att, weights[D + WID : 2 * D, WID:D]).astype(BF)


def call_attention_forward(first, operands, vecs, kept, weights):
    rows = operands[0].shape[0]
    outs = [
        jax.ShapeDtypeStruct((rows, D), BF),
        jax.ShapeDtypeStruct((rows, 3 * WID), BF),
        jax.ShapeDtypeStruct((rows, BLK), F32),
        jax.ShapeDtypeStruct((rows, WID), BF),
        jax.ShapeDtypeStruct((rows, D), BF),
    ]
    if not first:
        outs = [jax.ShapeDtypeStruct((rows, D), F32)] + outs
    args = list(operands) + [vecs, kept, weights]
    return pl.pallas_call(
        functools.partial(attention_forward, first),
        out_shape=outs,
        grid=(1,),
        in_specs=[full(*a.shape) for a in args[:-1]] + [full(ATT_ROWS, D)],
        out_specs=[full(*o.shape) for o in outs],
        compiler_params=params(32),
        cost_estimate=cost(2 * rows * D * 4 * WID * 2, 6 << 20),
        name="attention_forward",
    )(*args)


STEPS = 4
STEP_HID = HID // STEPS


def mlp_forward(hid_ref, own_ref, got_ref, vecs, up_ref, down_ref, *rest):
    mid_ref, n2_ref, act_ref, slope_ref, part_ref, total = rest
    step = pl.program_id(0)

    @pl.when(step == 0)
    def _():
        middle = hid_ref[...].astype(F32) + (
            own_ref[...].astype(F32) + got_ref[...].astype(F32) + vecs[3:4, :]
        )
        mid_ref[...] = middle
        centre, rstd = stats(middle)
        n2_ref[...] = (centre * rstd * vecs[4:5, :] + vecs[5:6, :]).astype(BF)

    row = 7 + step // 2
    bias = jnp.where(
        step % 2 == 0, vecs[pl.ds(row, 1), 0:STEP_HID], vecs[pl.ds(row, 1), STEP_HID:D]
    )
    upward = dot(n2_ref[...], up_ref[...]) + bias
    cdf = 0.5 + 0.5 * lax.erf(upward * 0.7071067811865476)
    act = (upward * cdf).astype(BF)
    act_ref[...] = act
    slope_ref[...] = (
        cdf + upward * (jnp.exp(-0.5 * upward * upward) * 0.3989422804014327)
    ).astype(BF)
    term = dot(act, down_ref[...])

    @pl.when(step == 0)
    def _():
        total[...] = term

    @pl.when((step > 0) & (step < STEPS - 1))
    def _():
        total[...] += term

    @pl.when(step == STEPS - 1)
    def _():
        part_ref[...] = (total[...] + term).astype(BF)


def full(rows, cols):
    return pl.BlockSpec((rows, cols), lambda s: (0, 0))


def mlp_weight_specs():
    return [
        pl.BlockSpec((D, STEP_HID), lambda s: (2 + s // 2, s % 2)),
        pl.BlockSpec((STEP_HID, D), lambda s: (2 * STEPS + s, 0)),
    ]


def call_mlp_forward(hidden, own, got, vecs, weights):
    rows = hidden.shape[0]
    return pl.pallas_call(
        mlp_forward,
        grid=(STEPS,),
        out_shape=[
            jax.ShapeDtypeStruct((rows, D), F32),
            jax.ShapeDtypeStruct((rows, D), BF),
            jax.ShapeDtypeStruct((rows, HID), BF),
            jax.ShapeDtypeStruct((rows, HID), BF),
            jax.ShapeDtypeStruct((rows, D), BF),
        ],
        in_specs=[full(rows, D), full(rows, D), full(rows, D), full(16, D)] + mlp_weight_specs(),
        out_specs=[
            full(rows, D),
            full(rows, D),
            pl.BlockSpec((rows, STEP_HID), lambda s: (0, s)),
            pl.BlockSpec((rows, STEP_HID), lambda s: (0, s)),
            full(rows, D),
        ],
        scratch_shapes=[pltpu.VMEM((rows, D), F32)],
        compiler_params=params(32),
        cost_estimate=cost(2 * rows * D * 2 * HID * 2, 12 << 20),
        name="mlp_forward",
    )(hidden, own, got, vecs, weights, weights)


def mlp_backward(first, *refs):
    if first:
        grad_ref, mid_ref, slope_ref, vecs, down_ref, up_ref = refs[:6]
        gd_ref, gu_ref, part_ref, sums_ref, total = refs[6:]
    else:
        (gm_ref, own_ref, got_ref, hid_ref, above) = refs[:5]
        mid_ref, slope_ref, vecs, down_ref, up_ref = refs[5:10]
        grad_out_ref, gd_ref, gu_ref, part_ref, sums_ref, total = refs[10:]
    step = pl.program_id(0)

    @pl.when(step == 0)
    def _():
        if first:
            gd_ref[...] = grad_ref[...]
        else:
            centre, rstd = stats(hid_ref[...])
            grad = own_ref[...].astype(F32) + got_ref[...].astype(F32)
            grad_hidden = gm_ref[...] + norm_back(grad, centre * rstd, rstd, above[0:1, :])
            grad_out_ref[...] = grad_hidden
            gd_ref[...] = grad_hidden.astype(BF)
        sums_ref[...] = jnp.zeros_like(sums_ref)
        sums_ref[2:3, :] = jnp.sum(gd_ref[...].astype(F32), axis=0, keepdims=True)

    grad_up = (slope_ref[...].astype(F32) * dot_nt(gd_ref[...], down_ref[...])).astype(BF)
    gu_ref[...] = grad_up
    sums = jnp.sum(grad_up.astype(F32), axis=0, keepdims=True)
    for at in range(STEPS):

        @pl.when(step == at)
        def _():
            sums_ref[3 + at // 2 : 4 + at // 2, (at % 2) * STEP_HID : (at % 2 + 1) * STEP_HID] = (
                sums
            )

    term = dot_nt(grad_up, up_ref[...])

    @pl.when(step == 0)
    def _():
        total[...] = term

    @pl.when((step > 0) & (step < STEPS - 1))
    def _():
        total[...] += term

    @pl.when(step == STEPS - 1)
    def _():
        grad = total[...] + term
        part_ref[...] = grad.astype(BF)
        centre, rstd = stats(mid_ref[...])
        sums_ref[0:1, :] = jnp.sum(grad * (centre * rstd), axis=0, keepdims=True)
        sums_ref[1:2, :] = jnp.sum(grad, axis=0, keepdims=True)


def call_mlp_backward(first, operands, middle, slope, vecs, weights):
    rows = middle.shape[0]
    specs = [full(rows, D)] if first else [full(rows, D)] * 4 + [full(16, D)]
    outs = [
        jax.ShapeDtypeStruct((rows, D), BF),
        jax.ShapeDtypeStruct((rows, HID), BF),
        jax.ShapeDtypeStruct((rows, D), BF),
        jax.ShapeDtypeStruct((8, D), F32),
    ]
    out_specs = [
        full(rows, D),
        pl.BlockSpec((rows, STEP_HID), lambda s: (0, s)),
        full(rows, D),
        full(8, D),
    ]
    if not first:
        outs = [jax.ShapeDtypeStruct((rows, D), F32)] + outs
        out_specs = [full(rows, D)] + out_specs
    return pl.pallas_call(
        functools.partial(mlp_backward, first),
        grid=(STEPS,),
        out_shape=outs,
        in_specs=specs
        + [full(rows, D), pl.BlockSpec((rows, STEP_HID), lambda s: (0, s)), full(16, D)]
        + mlp_weight_specs()[::-1],
        out_specs=out_specs,
        scratch_shapes=[pltpu.VMEM((rows, D), F32)],
        compiler_params=params(36),
        cost_estimate=cost(2 * rows * D * 2 * HID * 2, 12 << 20),
        name="mlp_backward",
    )(*operands, middle, slope, vecs, weights, weights)


def attention_backward(
    grad_ref,
    own_ref,
    got_ref,
    mid_ref,
    hid_ref,
    qkv_ref,
    lse_ref,
    vecs,
    kept,
    weights,
    gm_ref,
    gb_ref,
    gp_ref,
    part_ref,
    sums_ref,
):
    rows = grad_ref.shape[0]
    centre, rstd = stats(mid_ref[...])
    grad_two = own_ref[...].astype(F32) + got_ref[...].astype(F32)
    grad_middle = grad_ref[...].astype(F32) + norm_back(
        grad_two, centre * rstd, rstd, vecs[4:5, :]
    )
    gm_ref[...] = grad_middle
    gb = grad_middle.astype(BF)
    gb_ref[...] = gb
    sums_ref[...] = jnp.zeros_like(sums_ref)
    sums_ref[3:4, :] = jnp.sum(gb.astype(F32), axis=0, keepdims=True)
    grad_att = (
        dot_nt(gb[:, 0:WID], weights[D : D + WID, WID:D])
        + dot_nt(gb[:, WID:D], weights[D + WID : 2 * D, WID:D])
    ).astype(BF)
    bias = key_bias(kept[0:1, :], rows)
    lane = lax.broadcasted_iota(jnp.int32, (rows, BLK), 1)
    for pair in range(WID // BLK):
        cols = slice(pair * BLK, (pair + 1) * BLK)
        key_cols = slice(WID + pair * BLK, WID + (pair + 1) * BLK)
        value_cols = slice(2 * WID + pair * BLK, 2 * WID + (pair + 1) * BLK)
        q = qkv_ref[:, cols] * jnp.asarray(0.125, BF)
        k = qkv_ref[:, key_cols]
        v = qkv_ref[:, value_cols]
        g = grad_att[:, cols]
        got = []
        for half in range(2):
            head = 2 * pair + half
            scores = dot_nt(lane_half(q, half), k) + bias
            att = jnp.exp(scores - lse_ref[:, head : head + 1])
            grad_a = dot_nt(lane_half(g, half), v)
            inner = jnp.sum(att * grad_a, axis=-1, keepdims=True)
            grad_s = (att * (grad_a - inner)).astype(BF)
            got.append((dot(grad_s, k) * 0.125, dot_tn(grad_s, q), dot_tn(att.astype(BF), g)))
        for at, where in enumerate((cols, key_cols, value_cols)):
            gp_ref[:, where] = jnp.where(lane < HEAD_DIM, got[0][at], got[1][at]).astype(BF)
    sums_ref[2:3, 0:WID] = jnp.sum(gp_ref[:, 0:WID].astype(F32), axis=0, keepdims=True)
    sums_ref[2:3, WID:D] = jnp.sum(gp_ref[:, 2 * WID :].astype(F32), axis=0, keepdims=True)
    grad = (
        dot_nt(gp_ref[:, 0:WID], weights[0:D, 0:WID])
        + dot_nt(gp_ref[:, WID : 2 * WID], weights[0:D, WID:D])
        + dot_nt(gp_ref[:, 2 * WID :], weights[D : 2 * D, 0:WID])
    )
    part_ref[...] = grad.astype(BF)
    centre, rstd = stats(hid_ref[...].astype(F32))
    sums_ref[0:1, :] = jnp.sum(grad * (centre * rstd), axis=0, keepdims=True)
    sums_ref[1:2, :] = jnp.sum(grad, axis=0, keepdims=True)


def call_attention_backward(*args):
    rows = args[0].shape[0]
    outs = [
        jax.ShapeDtypeStruct((rows, D), F32),
        jax.ShapeDtypeStruct((rows, D), BF),
        jax.ShapeDtypeStruct((rows, 3 * WID), BF),
        jax.ShapeDtypeStruct((rows, D), BF),
        jax.ShapeDtypeStruct((8, D), F32),
    ]
    return pl.pallas_call(
        attention_backward,
        grid=(1,),
        out_shape=outs,
        in_specs=[full(*a.shape) for a in args[:-1]] + [full(ATT_ROWS, D)],
        out_specs=[full(*o.shape) for o in outs],
        compiler_params=params(40),
        cost_estimate=cost(2 * rows * D * 4 * WID * 3, 8 << 20),
        name="attention_backward",
    )(*args)


def mlp_grads(slot_own, slot_par, *refs):
    acts, gds, n2s, gus = refs[0:2], refs[2:4], refs[4:6], refs[6:8]
    own_ref, par_ref, down_buf, up_buf, sems = refs[8:]
    step = pl.program_id(0)
    at = lax.rem(step, 2)
    tiles = STEP_HID // 2 // BLK

    def copies(of_step, act_on):
        part = lax.rem(of_step, 2)
        first = lax.rem(of_step, STEPS) * tiles

        def one(index, carry):
            tile = lax.div(index, 8)
            block = lax.rem(index, 8)
            down_id = 128 + (first + tile) * 8 + block
            up_id = 64 + block * 8 + first + tile
            for slots, out in ((slot_own, own_ref), (slot_par, par_ref)):
                mine = (of_step < STEPS) if out is own_ref else (of_step >= STEPS)

                @pl.when(mine)
                def _():
                    down_row = pl.multiple_of(slots[down_id] * BLK, BLK)
                    up_row = pl.multiple_of(slots[up_id] * BLK, BLK)
                    tile_row = pl.multiple_of(tile * BLK, BLK)
                    block_row = pl.multiple_of(block * BLK, BLK)
                    act_on(
                        pltpu.make_async_copy(
                            down_buf.at[part, pl.ds(tile_row, BLK), pl.ds(block_row, BLK)],
                            out.at[pl.ds(down_row, BLK), :],
                            sems.at[part],
                        )
                    )
                    act_on(
                        pltpu.make_async_copy(
                            up_buf.at[part, pl.ds(block_row, BLK), pl.ds(tile_row, BLK)],
                            out.at[pl.ds(up_row, BLK), :],
                            sems.at[part],
                        )
                    )

            return carry

        lax.fori_loop(0, tiles * 8, one, 0)

    @pl.when(step >= 2)
    def _():
        copies(step - 2, lambda c: c.wait())

    down_buf[at] = sum(dot_tn(a[...], g[...]) for a, g in zip(acts, gds)).astype(BF)
    up_buf[at] = sum(dot_tn(n[...], g[...]) for n, g in zip(n2s, gus)).astype(BF)
    copies(step, lambda c: c.start())

    @pl.when(step == 2 * STEPS - 1)
    def _():
        copies(step - 1, lambda c: c.wait())
        copies(step, lambda c: c.wait())


def call_mlp_grads(slots, acts, gds, n2s, gus):
    rows = gds[0].shape[0]
    wide = STEP_HID // 2
    by_hidden = pl.BlockSpec((rows, wide), lambda s, a, b: (0, s))
    whole = pl.BlockSpec((rows, D), lambda s, a, b: (0, 0))
    buffer = jax.ShapeDtypeStruct((SHARE_TILES * BLK, BLK), BF)
    return pl.pallas_call(
        mlp_grads,
        grid_spec=pltpu.PrefetchScalarGridSpec(
            num_scalar_prefetch=2,
            grid=(2 * STEPS,),
            in_specs=[by_hidden] * 2 + [whole] * 4 + [by_hidden] * 2,
            out_specs=[ANY, ANY],
            scratch_shapes=[
                pltpu.VMEM((2, wide, D), BF),
                pltpu.VMEM((2, D, wide), BF),
                pltpu.SemaphoreType.DMA((2,)),
            ],
        ),
        out_shape=[buffer, buffer],
        compiler_params=params(32),
        cost_estimate=cost(2 * 2 * rows * D * 2 * HID * 2, 16 << 20),
        name="mlp_grads",
    )(*slots, *acts, *gds, *n2s, *gus)


def attention_grads(slot_own, slot_par, *refs):
    atts, gbs, n1s, gqs, gks, gvs = (refs[2 * i : 2 * i + 2] for i in range(6))
    own_ref, par_ref, out_buf, qkv_buf, sems = refs[14:]
    step = pl.program_id(0)
    at = lax.rem(step, 2)
    per_share = D // NARROW // BLK

    def copies(of_step, act_on):
        part = lax.rem(of_step, 2)
        column = lax.rem(of_step, per_share)

        def one(block, carry):
            block_row = pl.multiple_of(block * BLK, BLK)
            for slots, out in ((slot_own, own_ref), (slot_par, par_ref)):
                mine = (of_step < per_share) if out is own_ref else (of_step >= per_share)

                @pl.when(mine)
                def _():
                    row = pl.multiple_of(slots[48 + column * 8 + block] * BLK, BLK)
                    act_on(
                        pltpu.make_async_copy(
                            out_buf.at[part, :, pl.ds(block_row, BLK)],
                            out.at[pl.ds(row, BLK), :],
                            sems.at[part],
                        )
                    )
                    for third in range(3):
                        tile = block * 6 + third * 2 + column
                        row = pl.multiple_of(slots[tile] * BLK, BLK)
                        act_on(
                            pltpu.make_async_copy(
                                qkv_buf.at[part, third, pl.ds(block_row, BLK), :],
                                out.at[pl.ds(row, BLK), :],
                                sems.at[part],
                            )
                        )

            return carry

        lax.fori_loop(0, 8, one, 0)

    @pl.when(step >= 2)
    def _():
        copies(step - 2, lambda c: c.wait())

    out_buf[at] = sum(dot_tn(a[...], g[...]) for a, g in zip(atts, gbs)).astype(BF)
    for third, grads in enumerate((gqs, gks, gvs)):
        qkv_buf[at, third] = sum(dot_tn(n[...], g[...]) for n, g in zip(n1s, grads)).astype(BF)
    copies(step, lambda c: c.start())

    @pl.when(step == 2 * per_share - 1)
    def _():
        copies(step - 1, lambda c: c.wait())
        copies(step, lambda c: c.wait())


def call_attention_grads(slots, atts, gbs, n1s, gps, own, par):
    rows = gbs[0].shape[0]
    steps = WID // BLK
    whole = pl.BlockSpec((rows, D), lambda s, a, b: (0, 0))

    def by_column(third):
        return pl.BlockSpec((rows, BLK), lambda s, a, b: (0, third * steps + s))

    return pl.pallas_call(
        attention_grads,
        grid_spec=pltpu.PrefetchScalarGridSpec(
            num_scalar_prefetch=2,
            grid=(steps,),
            in_specs=[by_column(0)] * 2
            + [whole] * 4
            + [by_column(0)] * 2
            + [by_column(1)] * 2
            + [by_column(2)] * 2
            + [ANY, ANY],
            out_specs=[ANY, ANY],
            scratch_shapes=[
                pltpu.VMEM((2, BLK, D), BF),
                pltpu.VMEM((2, 3, D, BLK), BF),
                pltpu.SemaphoreType.DMA((2,)),
            ],
        ),
        out_shape=[jax.ShapeDtypeStruct(own.shape, BF)] * 2,
        input_output_aliases={14: 0, 15: 1},
        compiler_params=params(24),
        cost_estimate=cost(2 * 2 * rows * D * 4 * WID, 8 << 20),
        name="attention_grads",
    )(*slots, *atts, *gbs, *n1s, *gps, *gps, *gps, own, par)


def place_of(tile, share):
    quarter = WID // 2
    block, rest = tile // 6, tile % 6
    third, column = rest // 2, rest % 2
    qkv_row = jnp.where(third == 2, D, 0) + block * BLK
    qkv_col = jnp.where(third == 1, WID, 0) + share * quarter + column * BLK
    out = tile - 48
    out_block, out_col = out // 8, out % 8
    out_row = D + jnp.where(out_col >= 4, WID, 0) + share * quarter + out_block * BLK
    out_col = WID + (out_col % 4) * BLK
    up = tile - 64
    up_row, up_col = 2 * D + share * D + (up // 8) * BLK, (up % 8) * BLK
    down = tile - 128
    down_row, down_col = 4 * D + share * D + (down // 8) * BLK, (down % 8) * BLK
    kind = (tile >= 48).astype(jnp.int32) + (tile >= 64) + (tile >= 128)
    row = jnp.select([kind == 0, kind == 1, kind == 2], [qkv_row, out_row, up_row], down_row)
    col = jnp.select([kind == 0, kind == 1, kind == 2], [qkv_col, out_col, up_col], down_col)
    return row, col


def assemble_kernel(plan, rows, cols, *refs):
    sources = refs[: len(plan)]
    out_ref, held, in_sems, out_sem = refs[-4:]
    loads, base = [], 0
    for at, (src, (share, first, count)) in enumerate(zip(sources, plan)):
        size = count * BLK
        load = pltpu.make_async_copy(
            src.at[pl.ds(0, size), :], held.at[pl.ds(base * BLK, size), :], in_sems.at[at]
        )
        load.start()
        loads.append((load, base))
        base += count

    def run(at, act_on):
        share, first, count = plan[at]

        def one(i, carry):
            row = pl.multiple_of(rows[share, first + i], BLK)
            col = pl.multiple_of(cols[share, first + i], BLK)
            from_row = pl.multiple_of((loads[at][1] + i) * BLK, BLK)
            act_on(
                pltpu.make_async_copy(
                    held.at[pl.ds(from_row, BLK), :],
                    out_ref.at[pl.ds(row, BLK), pl.ds(col, BLK)],
                    out_sem,
                )
            )
            return carry

        lax.fori_loop(0, count, one, 0)

    for at in range(len(plan)):
        loads[at][0].wait()
        run(at, lambda c: c.start())
    for at in range(len(plan)):
        run(at, lambda c: c.wait())


def assemble(table, pieces, weights):
    plan = [piece[:3] for piece in pieces]
    arrays = [piece[3] for piece in pieces]
    total = sum(piece[2] for piece in pieces)
    shape = jax.ShapeDtypeStruct((6 * D, D), BF)
    alias = {} if weights is None else {2 + len(arrays): 0}
    args = list(table) + arrays + ([] if weights is None else [weights])
    return pl.pallas_call(
        functools.partial(assemble_kernel, plan),
        out_shape=shape,
        in_specs=[SMEM, SMEM] + [ANY] * (len(args) - 2),
        out_specs=ANY,
        scratch_shapes=[
            pltpu.VMEM((total * BLK, BLK), BF),
            pltpu.SemaphoreType.DMA((len(arrays),)),
            pltpu.SemaphoreType.DMA,
        ],
        input_output_aliases=alias,
        compiler_params=params(16),
        cost_estimate=cost(0, total * BLK * BLK * 8),
        name="assemble",
    )(*args)


def ring(size):
    order = list(range(0, size, 2)) + list(range(size - 1, 0, -2))
    ahead = [(order[i], order[(i + 1) % size]) for i in range(size)]
    position = [order.index(i) for i in range(size)]
    return order, position, ahead, [(b, a) for a, b in ahead]


def ring_gather(unit, size, per_device):
    _, _, ahead, behind = ring(size)
    far = size // 2
    front = per_device // 2
    pieces = []
    up = down = unit
    for step in range(1, far):
        up, down = lax.ppermute(up, "wide", ahead), lax.ppermute(down, "wide", behind)
        pieces.append((size - step, 0, per_device, up))
        pieces.append((step, 0, per_device, down))
    up = lax.ppermute(up[: front * BLK], "wide", ahead)
    down = lax.ppermute(down[front * BLK :], "wide", behind)
    pieces.append((far, 0, front, up))
    pieces.append((far, front, per_device - front, down))
    return pieces


def ring_scatter(unit_of, size, cut):
    _, _, ahead, behind = ring(size)
    far = size // 2

    def send(value, perm):
        return lax.ppermute(value.astype(BF), "wide", perm)

    last = unit_of(far)
    up = send(last[:cut], ahead).astype(F32)
    down = send(last[cut:], behind).astype(F32)
    for step in range(far - 1, 0, -1):
        term_up, term_down = unit_of(step), unit_of(size - step)
        if step == far - 1:
            up = jnp.concatenate([term_up[:cut] + up, term_up[cut:]])
            down = jnp.concatenate([term_down[:cut], term_down[cut:] + down])
        else:
            up, down = term_up + up, term_down + down
        up, down = send(up, ahead).astype(F32), send(down, behind).astype(F32)
    return unit_of(0) + up + down


def tile_ids(share):
    tile_rows = D // BLK
    shard_cols = D // (NARROW * BLK)
    shard_hidden = FF // (NARROW * BLK)
    count_qkv = tile_rows * 3 * tile_rows
    start_up = count_qkv + tile_rows * tile_rows
    start_down = start_up + tile_rows * (FF // BLK)
    row_part = jnp.arange(tile_rows)[:, None, None]
    third = jnp.arange(3)[None, :, None]
    column_part = jnp.arange(shard_cols)[None, None, :]
    qkv_ids = (
        row_part * 3 * tile_rows + third * tile_rows + share * shard_cols + column_part
    ).reshape(-1)
    out_ids = (
        count_qkv
        + (share * shard_cols + jnp.arange(shard_cols)[:, None]) * tile_rows
        + jnp.arange(tile_rows)[None, :]
    ).reshape(-1)
    up_ids = (
        start_up
        + jnp.arange(tile_rows)[:, None] * (FF // BLK)
        + share * shard_hidden
        + jnp.arange(shard_hidden)[None, :]
    ).reshape(-1)
    down_ids = (
        start_down
        + (share * shard_hidden + jnp.arange(shard_hidden)[:, None]) * tile_rows
        + jnp.arange(tile_rows)[None, :]
    ).reshape(-1)
    return jnp.concatenate([qkv_ids, out_ids, up_ids, down_ids])


def share_vectors(small_all, me):
    pieces = [small_all[i * D : (i + 1) * D] for i in range(8)]
    bias_up = small_all[8 * D :]

    def both(vector, width):
        own = lax.dynamic_slice_in_dim(vector, me * width, width)
        par = lax.dynamic_slice_in_dim(vector, (me ^ 1) * width, width)
        return jnp.concatenate([own, par])

    quarter = D // NARROW
    heads = jnp.concatenate([both(pieces[2], quarter), both(pieces[3], quarter)])
    rows = [pieces[0], pieces[1], heads, pieces[4], pieces[5], pieces[6], pieces[7]]
    up = both(bias_up, FF // NARROW)
    rows = rows + [up[0:D], up[D:]]
    return jnp.pad(jnp.stack(rows), ((0, 7), (0, 0)))


def small_vector(mlp_sums, att_sums, me):
    half = me // 2
    mine = [(half == t).astype(F32) for t in range(2)]
    mlp = mlp_sums[0] + mlp_sums[1]
    att = att_sums[0] + att_sums[1]
    bias_down = mine[0] * mlp_sums[0][2] + mine[1] * mlp_sums[1][2]
    bias_out = mine[0] * att_sums[0][3] + mine[1] * att_sums[1][3]
    odd = (me % 2) == 1

    def spread(own, par):
        placed = jnp.where(odd, jnp.concatenate([par, own]), jnp.concatenate([own, par]))
        return [jnp.where(half == 0, placed, 0.0), jnp.where(half == 1, placed, 0.0)]

    quarter = D // NARROW
    heads = att[2]
    return jnp.concatenate(
        [att[0], att[1]]
        + spread(heads[0:quarter], heads[quarter : 2 * quarter])
        + spread(heads[2 * quarter : 3 * quarter], heads[3 * quarter :])
        + [bias_out, mlp[0], mlp[1], bias_down]
        + spread(mlp[3], mlp[4])
    )


def total_over_mesh(value):
    value = jnp.broadcast_to(value.reshape(1, 1), (8, BLK))
    for axis in ("narrow", "wide"):
        size = lax.axis_size(axis)
        bit = 1
        while bit < size:
            value = value + lax.ppermute(value, axis, [(i, i ^ bit) for i in range(size)])
            bit *= 2
    return value[0, 0]


def rotate_in_kernel(grad_ref, left_ref, right_ref, out_ref):
    for block in range(out_ref.shape[0]):
        grad = grad_ref[block * BLK : (block + 1) * BLK, :].astype(BF)
        inner = dot_tn(left_ref[0, block].astype(BF), grad)
        out_ref[block] = dot(inner.astype(BF), right_ref[0, block].astype(BF))


def rotate_in(layer, grads, left_basis, right_basis):
    count = left_basis.shape[1]
    group = 6
    spec = pl.BlockSpec((group, BLK, BLK), lambda i: (i, 0, 0))
    flat = pl.BlockSpec((group * BLK, BLK), lambda i: (i, 0))
    basis = pl.BlockSpec((1, group, BLK, BLK), lambda i: (layer, i, 0, 0))
    return pl.pallas_call(
        rotate_in_kernel,
        grid=(count // group,),
        out_shape=jax.ShapeDtypeStruct((count, BLK, BLK), F32),
        in_specs=[flat, basis, basis],
        out_specs=spec,
        compiler_params=params(16),
        cost_estimate=cost(count * 4 * BLK**3, count * BLK * BLK * 14),
        name="rotate_in",
    )(grads, left_basis, right_basis)


def update_kernel(clip_ref, rot0, rot1, left, right, first, second, master, *outs):
    new_first, new_second, new_master, new_weights = outs
    step = pl.program_id(0)
    half = pl.num_programs(0) // 2
    clip = clip_ref[0]
    for block in range(rot0.shape[0]):
        rotated = clip * jnp.where(step < half, rot0[block], rot1[block])
        one = 0.5 * first[0, block] + 0.5 * rotated
        two = 0.5 * second[0, block] + 0.5 * rotated * rotated
        new_first[0, block] = one
        new_second[0, block] = two
        direction = one / (jnp.sqrt(two) + 1e-08)
        inner = dot(left[0, block].astype(BF), direction.astype(BF))
        turned = dot_nt(inner.astype(BF), right[0, block].astype(BF))
        weights = master[0, block] - 0.02 * turned
        new_master[0, block] = weights
        new_weights[0, block] = weights.astype(BF)


def update(clip, rots, left, right, first, second, master):
    count = rots[0].shape[0]
    group = 3
    steps = count // group
    spec = pl.BlockSpec((1, group, BLK, BLK), lambda i: (i // steps, i % steps, 0, 0))
    low = pl.BlockSpec((group, BLK, BLK), lambda i: (jnp.minimum(i, steps - 1), 0, 0))
    high = pl.BlockSpec((group, BLK, BLK), lambda i: (jnp.maximum(i - steps, 0), 0, 0))
    shape = jax.ShapeDtypeStruct(master.shape, F32)
    return pl.pallas_call(
        update_kernel,
        grid=(2 * steps,),
        out_shape=[shape, shape, shape, jax.ShapeDtypeStruct(master.shape, BF)],
        in_specs=[SMEM, low, high] + [spec] * 5,
        out_specs=[spec] * 4,
        compiler_params=params(24),
        cost_estimate=cost(count * 8 * BLK**3, count * BLK * BLK * 2 * 38),
        name="update",
    )(clip, *rots, left, right, first, second, master)


def shards(
    images,
    cotangent,
    kept_tokens,
    owner_slots,
    master_blocks,
    small_params,
    left_basis,
    right_basis,
    first_moment,
    second_moment,
    small_first,
    small_second,
):
    me = lax.axis_index("narrow")
    half, core = me // 2, me % 2
    wide = lax.axis_size("wide")
    per_device = master_blocks.shape[1]
    own_small = small_params.shape[1]
    own_images = images.shape[0]
    rows = own_images * S

    small_bf = small_params.astype(BF)
    small_pair = jnp.stack([small_bf, lax.ppermute(small_bf, "narrow", ACROSS)])
    small_rows = -(-small_pair.size // (16 * BLK)) * 16
    small_pad = jnp.pad(small_pair.reshape(-1), (0, small_rows * BLK - small_pair.size))
    small_pad = small_pad.reshape(small_rows, BLK)

    def chunks(own):
        other = lax.ppermute(own, "narrow", ACROSS)
        return [jnp.where(half == t, own, other) for t in range(2)]

    hidden_in = chunks(images.reshape(rows, D))
    cot = chunks(cotangent.reshape(rows, D))
    kept = [
        lax.dynamic_slice_in_dim(kept_tokens, (2 * t + core) * own_images, own_images, 0)
        .reshape(1, rows)
        .astype(F32)
        for t in range(2)
    ]

    order, position, _, _ = ring(wide)
    place = jnp.take(jnp.asarray(position, jnp.int32), lax.axis_index("wide"))
    around = jnp.take(jnp.asarray(order, jnp.int32), (place + jnp.arange(wide)) % wide)

    slots, tables = [], []
    for layer in range(LAYERS):
        owners = owner_slots[layer]
        layer_slots, layer_rows, layer_cols = [], [], []
        for at, share in enumerate((me, me ^ 1)):
            slot = jnp.take(owners, tile_ids(share))
            at_wide, at_pos = slot // per_device // NARROW, slot % per_device
            distance = (jnp.take(jnp.asarray(position, jnp.int32), at_wide) - place) % wide
            relative = distance * per_device + at_pos
            layer_slots.append(relative)
            here = relative[None, :] == jnp.arange(SHARE_TILES)[:, None]
            tile = jnp.sum(jnp.where(here, jnp.arange(SHARE_TILES)[None, :], 0), axis=1)
            row, col = place_of(tile, at)
            layer_rows.append(row)
            layer_cols.append(col)
        slots.append(layer_slots)
        tables.append((jnp.stack(layer_rows), jnp.stack(layer_cols)))

    def core_swap(value):
        return lax.ppermute(value, "narrow", CORE)

    weights, units = [], []
    for layer in range(LAYERS):
        unit = master_blocks[layer].astype(BF).reshape(per_device * BLK, BLK)
        if layer == 0:
            unit = jnp.concatenate([unit, small_pad], axis=0)
        pieces = [(0, 0, per_device, unit)] + ring_gather(unit, wide, per_device)
        pieces = [piece + (core_swap(piece[3]),) for piece in pieces]
        matrix = None
        for group in (pieces[: wide - 3], pieces[wide - 3 : wide - 1], pieces[wide - 1 :]):
            group = [
                (share, distance * per_device + first, count, pair[share])
                for distance, first, count, *pair in group
                for share in range(2)
            ]
            matrix = assemble(tables[layer], group, matrix)
        weights.append(matrix)
        units.append(pieces)

    tails = [[None] * wide, [None] * wide]
    for distance, first, count, *pair in units[0]:
        if first + count == per_device:
            for share in range(2):
                tails[share][distance] = pair[share][count * BLK :]
    tails = [
        jnp.stack(t).reshape(wide, small_rows * BLK)[:, : small_pair.size]
        .reshape(wide, 2, LAYERS, own_small)
        for t in tails
    ]
    by_distance = jnp.stack([tails[0][:, 0], tails[1][:, 0], tails[0][:, 1], tails[1][:, 1]], axis=1)
    to_order = (jnp.asarray(position, jnp.int32) - place) % wide
    in_order = jnp.take(by_distance, to_order, axis=0)
    in_order = jnp.take(in_order, jnp.arange(NARROW) ^ me, axis=1).astype(F32)
    small_all = in_order.transpose(2, 0, 1, 3).reshape(LAYERS, -1)
    vecs = [share_vectors(small_all[layer], me) for layer in range(LAYERS)]

    def exchange(part):
        return lax.ppermute(part, "narrow", ACROSS)

    saved = []
    state = None
    for layer in range(LAYERS):
        att_w = mlp_w = weights[layer]
        kept_layer = []
        for t in range(2):
            if layer == 0:
                out = call_attention_forward(True, (hidden_in[t],), vecs[0], kept[t], att_w)
                hidden = hidden_in[t]
            else:
                hidden, *out = call_attention_forward(
                    False, state[t] + (vecs[layer - 1],), vecs[layer], kept[t], att_w
                )
            n1, qkv, lse, att, part = out
            kept_layer.append([hidden, n1, qkv, lse, att, part, exchange(part)])
        state = []
        for t in range(2):
            hidden, n1, qkv, lse, att, part, got = kept_layer[t]
            middle, n2, act, slope, down_part = call_mlp_forward(
                hidden, part, got, vecs[layer], mlp_w
            )
            kept_layer[t] = (hidden, n1, qkv, lse, att, middle, n2, act, slope)
            if layer < LAYERS - 1:
                state.append((middle, down_part, exchange(down_part)))
            else:
                state.append((middle, down_part))
        saved.append((att_w, mlp_w, kept_layer))

    def mine(pair):
        return jnp.where(half == 0, pair[0], pair[1])

    def theirs(pair):
        return jnp.where(half == 0, pair[1], pair[0])

    down_parts = [state[t][1] for t in range(2)]
    middles = [state[t][0] for t in range(2)]
    final = mine(middles) + (
        mine(down_parts).astype(F32)
        + exchange(theirs(down_parts)).astype(F32)
        + vecs[LAYERS - 1][6]
    )
    block_output = final.astype(BF).reshape(images.shape)

    upstream = None
    reduced = [None] * LAYERS
    small_terms = [None] * LAYERS
    for layer in reversed(range(LAYERS)):
        att_w, mlp_w, kept_layer = saved[layer]
        top = layer == LAYERS - 1
        work = []
        for t in range(2):
            hidden, n1, qkv, lse, att, middle, n2, act, slope = kept_layer[t]
            if top:
                grad = cot[t]
                gd, gu, part, sums = call_mlp_backward(
                    True, (grad,), middle, slope, vecs[layer], mlp_w
                )
            else:
                grad, gd, gu, part, sums = call_mlp_backward(
                    False, upstream[t] + (vecs[layer + 1],), middle, slope, vecs[layer], mlp_w
                )
            work.append([grad, gd, gu, part, sums, exchange(part)])
        own, par = call_mlp_grads(
            slots[layer],
            [k[7] for k in kept_layer],
            [w[1] for w in work],
            [k[6] for k in kept_layer],
            [w[2] for w in work],
        )
        back = []
        for t in range(2):
            hidden, n1, qkv, lse, att, middle, n2, act, slope = kept_layer[t]
            grad, gd, gu, part, sums, got = work[t]
            gm, gb, gp, att_part, att_sums = call_attention_backward(
                grad, part, got, middle, hidden, qkv, lse, vecs[layer], kept[t], att_w
            )
            back.append((gm, gb, gp, att_part, att_sums))
        if layer > 0:
            upstream = [
                (back[t][0], back[t][3], exchange(back[t][3]), kept_layer[t][0]) for t in range(2)
            ]
        own, par = call_attention_grads(
            slots[layer],
            [k[4] for k in kept_layer],
            [b[1] for b in back],
            [k[1] for k in kept_layer],
            [b[2] for b in back],
            own,
            par,
        )
        terms = small_vector([w[4] for w in work], [b[4] for b in back], me)
        terms = jnp.take(terms.reshape(wide, NARROW, own_small), around, axis=0)
        terms = jnp.take(terms, jnp.arange(NARROW) ^ me, axis=1)
        near = terms[:, 0:2] + exchange(terms[:, 2:4])
        small_sum = near[:, 0] + core_swap(near[:, 1])
        tail_rows = -(-own_small // (16 * BLK)) * 16
        small_tail = jnp.pad(small_sum, ((0, 0), (0, tail_rows * BLK - own_small)))
        small_tail = small_tail.reshape(wide, tail_rows, BLK)
        unit_len = per_device * BLK

        def unit_of(distance, own=own, par=par, small_tail=small_tail, unit_len=unit_len):
            at = slice(distance * unit_len, (distance + 1) * unit_len)
            term = own[at].astype(F32) + core_swap(par[at]).astype(F32)
            return jnp.concatenate([term, small_tail[distance]])

        reduced[layer] = ring_scatter(unit_of, wide, (per_device // 2) * BLK)
        if layer == 0:
            parts = [b[3] for b in back]
            hidden = mine([k[0] for k in kept_layer]).astype(F32)
            centre, rstd = stats(hidden)
            grad = mine(parts).astype(F32) + exchange(theirs(parts)).astype(F32)
            lower = norm_back(grad, centre * rstd, rstd, vecs[0][0:1])
            input_grad = (mine([b[0] for b in back]) + lower).reshape(images.shape)

    tail = per_device * BLK
    grad_small = jnp.stack([r[tail:].reshape(-1)[:own_small] for r in reduced])
    local_sum = jnp.sum(grad_small * grad_small)
    for grads in reduced:
        local_sum = local_sum + jnp.sum(grads[:tail] * grads[:tail])
    grad_norm = jnp.sqrt(total_over_mesh(local_sum))
    clip_factor = 1.0 / jnp.maximum(grad_norm, 1.0)
    rots = [
        rotate_in(layer, reduced[layer], left_basis, right_basis) for layer in range(LAYERS)
    ]
    new_first, new_second, new_master, new_weights = update(
        clip_factor.reshape(1),
        rots,
        left_basis,
        right_basis,
        first_moment,
        second_moment,
        master_blocks,
    )
    clipped_small = clip_factor * grad_small
    new_small_first = 0.5 * small_first + 0.5 * clipped_small
    new_small_second = 0.5 * small_second + 0.5 * clipped_small * clipped_small
    new_small = small_params - 0.3 * new_small_first / (jnp.sqrt(new_small_second) + 1e-08)
    return (
        block_output,
        input_grad,
        grad_norm.reshape(1),
        new_first,
        new_second,
        new_master,
        new_weights,
        new_small_first,
        new_small_second,
        new_small,
        new_small.astype(BF),
    )


def solution(mesh):
    both = ("wide", "narrow")
    rows = P(both, None, None)
    blocks = P(None, both, None, None)
    small = P(None, both)
    in_specs = (
        rows,
        rows,
        P("wide", None),
        P(),
        blocks,
        small,
        blocks,
        blocks,
        blocks,
        blocks,
        small,
        small,
    )
    out_specs = (rows, rows, P(), blocks, blocks, blocks, blocks, small, small, small, small)
    return jax.shard_map(shards, mesh=mesh, in_specs=in_specs, out_specs=out_specs, check_vma=False)
```

```python
import functools

import jax
import jax.numpy as jnp
from jax import lax
from jax.experimental import pallas as pl
from jax.experimental.pallas import tpu as pltpu
from jax.sharding import PartitionSpec as P

D = 1024
HEAD_DIM = 64
FF = 4096
S = 50
LAYERS = 2
BLK = 128
NARROW = 4

BF = jnp.bfloat16
F32 = jnp.float32

WID = D // 2
HID = FF // 2
SHARE_TILES = 192
ATT_ROWS = 2 * D
MLP_ROWS = 4 * D

CORE = [(j, j ^ 1) for j in range(NARROW)]
ACROSS = [(j, j ^ 2) for j in range(NARROW)]
ANY = pl.BlockSpec(memory_space=pl.ANY)
SMEM = pl.BlockSpec(memory_space=pltpu.SMEM)
VMEM = pl.BlockSpec(memory_space=pltpu.VMEM)
HBM = pl.BlockSpec(memory_space=pltpu.HBM)


def params(mib=30):
    return pltpu.CompilerParams(vmem_limit_bytes=mib << 20)


def cost(flops, nbytes):
    return pl.CostEstimate(flops=flops, bytes_accessed=nbytes, transcendentals=0)


def dot(a, b):
    return jnp.dot(a, b, preferred_element_type=F32)


def dot_nt(a, b):
    return lax.dot_general(a, b, (((1,), (1,)), ((), ())), preferred_element_type=F32)


def dot_tn(a, b):
    return lax.dot_general(a, b, (((0,), (0,)), ((), ())), preferred_element_type=F32)


def stats(x):
    centre = x - jnp.mean(x, axis=-1, keepdims=True)
    spread = jnp.mean(centre * centre, axis=-1, keepdims=True)
    return centre, lax.rsqrt(spread + 1e-06)


def norm_back(grad, xhat, rstd, gain):
    gn = grad * gain
    return rstd * (
        gn
        - jnp.mean(gn, axis=-1, keepdims=True)
        - xhat * jnp.mean(gn * xhat, axis=-1, keepdims=True)
    )


def key_bias(kept_row, rows):
    def image_of(dim):
        pos = lax.broadcasted_iota(jnp.int32, (rows, rows), dim)
        image = jnp.zeros((rows, rows), jnp.int32)
        for edge in range(S, rows, S):
            image = image + (pos >= edge).astype(jnp.int32)
        return image

    allowed = (image_of(0) == image_of(1)) & (kept_row > 0.0)
    return jnp.where(allowed, 0.0, -1e30)


def lane_half(x, half):
    lane = lax.broadcasted_iota(jnp.int32, x.shape, 1)
    keep = (lane < HEAD_DIM) if half == 0 else (lane >= HEAD_DIM)
    return jnp.where(keep, x, jnp.zeros_like(x))


def attention_forward(first, *refs):
    if first:
        x_ref, vecs, kept, weights, n1_ref, qkv_ref, lse_ref, att_ref, part_ref = refs
        hidden = x_ref[...].astype(F32)
    else:
        (mid_ref, own_ref, got_ref, prev, vecs, kept, weights) = refs[:7]
        hidden_ref, n1_ref, qkv_ref, lse_ref, att_ref, part_ref = refs[7:]
        hidden = mid_ref[...] + (
            own_ref[...].astype(F32) + got_ref[...].astype(F32) + prev[6:7, :]
        )
        hidden_ref[...] = hidden
    rows = hidden.shape[0]
    centre, rstd = stats(hidden)
    n1 = (centre * rstd * vecs[0:1, :] + vecs[1:2, :]).astype(BF)
    n1_ref[...] = n1
    qkv_ref[:, 0:WID] = (dot(n1, weights[0:D, 0:WID]) + vecs[2:3, 0:WID]).astype(BF)
    qkv_ref[:, WID : 2 * WID] = dot(n1, weights[0:D, WID:D]).astype(BF)
    qkv_ref[:, 2 * WID :] = (dot(n1, weights[D : 2 * D, 0:WID]) + vecs[2:3, WID:D]).astype(BF)
    bias = key_bias(kept[0:1, :], rows)
    lane = lax.broadcasted_iota(jnp.int32, (rows, BLK), 1)
    lse_all = jnp.zeros((rows, BLK), F32)
    for pair in range(WID // BLK):
        cols = slice(pair * BLK, (pair + 1) * BLK)
        q = qkv_ref[:, cols] * jnp.asarray(0.125, BF)
        k = qkv_ref[:, WID + pair * BLK : WID + (pair + 1) * BLK]
        v = qkv_ref[:, 2 * WID + pair * BLK : 2 * WID + (pair + 1) * BLK]
        outs = []
        for half in range(2):
            scores = dot_nt(lane_half(q, half), k) + bias
            top = jnp.max(scores, axis=-1, keepdims=True)
            raised = jnp.exp(scores - top)
            total = jnp.sum(raised, axis=-1, keepdims=True)
            outs.append(dot((raised * (1.0 / total)).astype(BF), v))
            lse_all = jnp.where(lane == 2 * pair + half, top + jnp.log(total), lse_all)
        att_ref[:, cols] = jnp.where(lane < HEAD_DIM, outs[0], outs[1]).astype(BF)
    lse_ref[...] = lse_all
    att = att_ref[...]
    part_ref[:, 0:WID] = dot(att, weights[D : D + WID, WID:D]).astype(BF)
    part_ref[:, WID:D] = dot(att, weights[D + WID : 2 * D, WID:D]).astype(BF)


def call_attention_forward(first, operands, vecs, kept, weights):
    rows = operands[0].shape[0]
    outs = [
        jax.ShapeDtypeStruct((rows, D), BF),
        jax.ShapeDtypeStruct((rows, 3 * WID), BF),
        jax.ShapeDtypeStruct((rows, BLK), F32),
        jax.ShapeDtypeStruct((rows, WID), BF),
        jax.ShapeDtypeStruct((rows, D), BF),
    ]
    if not first:
        outs = [jax.ShapeDtypeStruct((rows, D), F32)] + outs
    args = list(operands) + [vecs, kept, weights]
    return pl.pallas_call(
        functools.partial(attention_forward, first),
        out_shape=outs,
        grid=(1,),
        in_specs=[full(*a.shape) for a in args[:-1]] + [VMEM],
        out_specs=[full(*o.shape) for o in outs],
        compiler_params=params(),
        cost_estimate=cost(2 * rows * D * 4 * WID * 2, 6 << 20),
        name="attention_forward",
    )(*args)


STEPS = 4
STEP_HID = HID // STEPS


def mlp_forward(hid_ref, own_ref, got_ref, vecs, weights, *rest):
    mid_ref, n2_ref, act_ref, slope_ref, part_ref, total = rest
    step = pl.program_id(0)

    @pl.when(step == 0)
    def _():
        middle = hid_ref[...].astype(F32) + (
            own_ref[...].astype(F32) + got_ref[...].astype(F32) + vecs[3:4, :]
        )
        mid_ref[...] = middle
        centre, rstd = stats(middle)
        n2_ref[...] = (centre * rstd * vecs[4:5, :] + vecs[5:6, :]).astype(BF)

    row = 7 + step // 2
    bias = jnp.where(
        step % 2 == 0, vecs[pl.ds(row, 1), 0:STEP_HID], vecs[pl.ds(row, 1), STEP_HID:D]
    )
    upward = dot(n2_ref[...], up_part(weights, step)) + bias
    cdf = 0.5 + 0.5 * lax.erf(upward * 0.7071067811865476)
    act = (upward * cdf).astype(BF)
    act_ref[...] = act
    slope_ref[...] = (
        cdf + upward * (jnp.exp(-0.5 * upward * upward) * 0.3989422804014327)
    ).astype(BF)
    term = dot(act, down_part(weights, step))

    @pl.when(step == 0)
    def _():
        total[...] = term

    @pl.when((step > 0) & (step < STEPS - 1))
    def _():
        total[...] += term

    @pl.when(step == STEPS - 1)
    def _():
        part_ref[...] = (total[...] + term).astype(BF)


def full(rows, cols):
    return pl.BlockSpec((rows, cols), lambda s: (0, 0))


def up_part(weights, step):
    rows = pl.ds(pl.multiple_of(2 * D + step // 2 * D, D), D)
    return weights[rows, pl.ds(pl.multiple_of(step % 2 * STEP_HID, STEP_HID), STEP_HID)]


def down_part(weights, step):
    return weights[pl.ds(pl.multiple_of(4 * D + step * STEP_HID, STEP_HID), STEP_HID), :]


def call_mlp_forward(hidden, own, got, vecs, weights):
    rows = hidden.shape[0]
    return pl.pallas_call(
        mlp_forward,
        grid=(STEPS,),
        out_shape=[
            jax.ShapeDtypeStruct((rows, D), F32),
            jax.ShapeDtypeStruct((rows, D), BF),
            jax.ShapeDtypeStruct((rows, HID), BF),
            jax.ShapeDtypeStruct((rows, HID), BF),
            jax.ShapeDtypeStruct((rows, D), BF),
        ],
        in_specs=[full(rows, D), full(rows, D), full(rows, D), full(16, D), VMEM],
        out_specs=[
            full(rows, D),
            full(rows, D),
            pl.BlockSpec((rows, STEP_HID), lambda s: (0, s)),
            pl.BlockSpec((rows, STEP_HID), lambda s: (0, s)),
            full(rows, D),
        ],
        scratch_shapes=[pltpu.VMEM((rows, D), F32)],
        compiler_params=params(),
        cost_estimate=cost(2 * rows * D * 2 * HID * 2, 12 << 20),
        name="mlp_forward",
    )(hidden, own, got, vecs, weights)


def mlp_backward(first, *refs):
    if first:
        grad_ref, mid_ref, slope_ref, vecs, weights = refs[:5]
        gd_ref, gu_ref, part_ref, sums_ref, total = refs[5:]
    else:
        (gm_ref, own_ref, got_ref, hid_ref, above) = refs[:5]
        mid_ref, slope_ref, vecs, weights = refs[5:9]
        grad_out_ref, gd_ref, gu_ref, part_ref, sums_ref, total = refs[9:]
    step = pl.program_id(0)

    @pl.when(step == 0)
    def _():
        if first:
            gd_ref[...] = grad_ref[...]
        else:
            centre, rstd = stats(hid_ref[...])
            grad = own_ref[...].astype(F32) + got_ref[...].astype(F32)
            grad_hidden = gm_ref[...] + norm_back(grad, centre * rstd, rstd, above[0:1, :])
            grad_out_ref[...] = grad_hidden
            gd_ref[...] = grad_hidden.astype(BF)
        sums_ref[...] = jnp.zeros_like(sums_ref)
        sums_ref[2:3, :] = jnp.sum(gd_ref[...].astype(F32), axis=0, keepdims=True)

    grad_up = (slope_ref[...].astype(F32) * dot_nt(gd_ref[...], down_part(weights, step))).astype(BF)
    gu_ref[...] = grad_up
    sums = jnp.sum(grad_up.astype(F32), axis=0, keepdims=True)
    for at in range(STEPS):

        @pl.when(step == at)
        def _():
            sums_ref[3 + at // 2 : 4 + at // 2, (at % 2) * STEP_HID : (at % 2 + 1) * STEP_HID] = (
                sums
            )

    term = dot_nt(grad_up, up_part(weights, step))

    @pl.when(step == 0)
    def _():
        total[...] = term

    @pl.when((step > 0) & (step < STEPS - 1))
    def _():
        total[...] += term

    @pl.when(step == STEPS - 1)
    def _():
        grad = total[...] + term
        part_ref[...] = grad.astype(BF)
        centre, rstd = stats(mid_ref[...])
        sums_ref[0:1, :] = jnp.sum(grad * (centre * rstd), axis=0, keepdims=True)
        sums_ref[1:2, :] = jnp.sum(grad, axis=0, keepdims=True)


def call_mlp_backward(first, operands, middle, slope, vecs, weights):
    rows = middle.shape[0]
    specs = [full(rows, D)] if first else [full(rows, D)] * 4 + [full(16, D)]
    outs = [
        jax.ShapeDtypeStruct((rows, D), BF),
        jax.ShapeDtypeStruct((rows, HID), BF),
        jax.ShapeDtypeStruct((rows, D), BF),
        jax.ShapeDtypeStruct((8, D), F32),
    ]
    out_specs = [
        full(rows, D),
        pl.BlockSpec((rows, STEP_HID), lambda s: (0, s)),
        full(rows, D),
        full(8, D),
    ]
    if not first:
        outs = [jax.ShapeDtypeStruct((rows, D), F32)] + outs
        out_specs = [full(rows, D)] + out_specs
    return pl.pallas_call(
        functools.partial(mlp_backward, first),
        grid=(STEPS,),
        out_shape=outs,
        in_specs=specs
        + [full(rows, D), pl.BlockSpec((rows, STEP_HID), lambda s: (0, s)), full(16, D), VMEM],
        out_specs=out_specs,
        scratch_shapes=[pltpu.VMEM((rows, D), F32)],
        compiler_params=params(),
        cost_estimate=cost(2 * rows * D * 2 * HID * 2, 12 << 20),
        name="mlp_backward",
    )(*operands, middle, slope, vecs, weights)


def attention_backward(
    grad_ref,
    own_ref,
    got_ref,
    mid_ref,
    hid_ref,
    qkv_ref,
    lse_ref,
    vecs,
    kept,
    weights,
    gm_ref,
    gb_ref,
    gp_ref,
    part_ref,
    sums_ref,
):
    rows = grad_ref.shape[0]
    centre, rstd = stats(mid_ref[...])
    grad_two = own_ref[...].astype(F32) + got_ref[...].astype(F32)
    grad_middle = grad_ref[...].astype(F32) + norm_back(
        grad_two, centre * rstd, rstd, vecs[4:5, :]
    )
    gm_ref[...] = grad_middle
    gb = grad_middle.astype(BF)
    gb_ref[...] = gb
    sums_ref[...] = jnp.zeros_like(sums_ref)
    sums_ref[3:4, :] = jnp.sum(gb.astype(F32), axis=0, keepdims=True)
    grad_att = (
        dot_nt(gb[:, 0:WID], weights[D : D + WID, WID:D])
        + dot_nt(gb[:, WID:D], weights[D + WID : 2 * D, WID:D])
    ).astype(BF)
    bias = key_bias(kept[0:1, :], rows)
    lane = lax.broadcasted_iota(jnp.int32, (rows, BLK), 1)
    for pair in range(WID // BLK):
        cols = slice(pair * BLK, (pair + 1) * BLK)
        key_cols = slice(WID + pair * BLK, WID + (pair + 1) * BLK)
        value_cols = slice(2 * WID + pair * BLK, 2 * WID + (pair + 1) * BLK)
        q = qkv_ref[:, cols] * jnp.asarray(0.125, BF)
        k = qkv_ref[:, key_cols]
        v = qkv_ref[:, value_cols]
        g = grad_att[:, cols]
        got = []
        for half in range(2):
            head = 2 * pair + half
            scores = dot_nt(lane_half(q, half), k) + bias
            att = jnp.exp(scores - lse_ref[:, head : head + 1])
            grad_a = dot_nt(lane_half(g, half), v)
            inner = jnp.sum(att * grad_a, axis=-1, keepdims=True)
            grad_s = (att * (grad_a - inner)).astype(BF)
            got.append((dot(grad_s, k) * 0.125, dot_tn(grad_s, q), dot_tn(att.astype(BF), g)))
        for at, where in enumerate((cols, key_cols, value_cols)):
            gp_ref[:, where] = jnp.where(lane < HEAD_DIM, got[0][at], got[1][at]).astype(BF)
    sums_ref[2:3, 0:WID] = jnp.sum(gp_ref[:, 0:WID].astype(F32), axis=0, keepdims=True)
    sums_ref[2:3, WID:D] = jnp.sum(gp_ref[:, 2 * WID :].astype(F32), axis=0, keepdims=True)
    grad = (
        dot_nt(gp_ref[:, 0:WID], weights[0:D, 0:WID])
        + dot_nt(gp_ref[:, WID : 2 * WID], weights[0:D, WID:D])
        + dot_nt(gp_ref[:, 2 * WID :], weights[D : 2 * D, 0:WID])
    )
    part_ref[...] = grad.astype(BF)
    centre, rstd = stats(hid_ref[...].astype(F32))
    sums_ref[0:1, :] = jnp.sum(grad * (centre * rstd), axis=0, keepdims=True)
    sums_ref[1:2, :] = jnp.sum(grad, axis=0, keepdims=True)


def call_attention_backward(*args):
    rows = args[0].shape[0]
    outs = [
        jax.ShapeDtypeStruct((rows, D), F32),
        jax.ShapeDtypeStruct((rows, D), BF),
        jax.ShapeDtypeStruct((rows, 3 * WID), BF),
        jax.ShapeDtypeStruct((rows, D), BF),
        jax.ShapeDtypeStruct((8, D), F32),
    ]
    return pl.pallas_call(
        attention_backward,
        grid=(1,),
        out_shape=outs,
        in_specs=[full(*a.shape) for a in args[:-1]] + [VMEM],
        out_specs=[full(*o.shape) for o in outs],
        compiler_params=params(),
        cost_estimate=cost(2 * rows * D * 4 * WID * 3, 8 << 20),
        name="attention_backward",
    )(*args)


def mlp_grads(slot_own, slot_par, *refs):
    acts, gds, n2s, gus = refs[0:2], refs[2:4], refs[4:6], refs[6:8]
    own_ref, par_ref, down_buf, up_buf, sems = refs[8:]
    step = pl.program_id(0)
    at = lax.rem(step, 2)
    tiles = STEP_HID // 2 // BLK

    def copies(of_step, act_on):
        part = lax.rem(of_step, 2)
        first = lax.rem(of_step, STEPS) * tiles

        def one(index, carry):
            tile = lax.div(index, 8)
            block = lax.rem(index, 8)
            down_id = 128 + (first + tile) * 8 + block
            up_id = 64 + block * 8 + first + tile
            for slots, out in ((slot_own, own_ref), (slot_par, par_ref)):
                mine = (of_step < STEPS) if out is own_ref else (of_step >= STEPS)

                @pl.when(mine)
                def _():
                    down_row = pl.multiple_of(slots[down_id] * BLK, BLK)
                    up_row = pl.multiple_of(slots[up_id] * BLK, BLK)
                    tile_row = pl.multiple_of(tile * BLK, BLK)
                    block_row = pl.multiple_of(block * BLK, BLK)
                    act_on(
                        pltpu.make_async_copy(
                            down_buf.at[part, pl.ds(tile_row, BLK), pl.ds(block_row, BLK)],
                            out.at[pl.ds(down_row, BLK), :],
                            sems.at[part],
                        )
                    )
                    act_on(
                        pltpu.make_async_copy(
                            up_buf.at[part, pl.ds(block_row, BLK), pl.ds(tile_row, BLK)],
                            out.at[pl.ds(up_row, BLK), :],
                            sems.at[part],
                        )
                    )

            return carry

        lax.fori_loop(0, tiles * 8, one, 0)

    @pl.when(step >= 2)
    def _():
        copies(step - 2, lambda c: c.wait())

    down_buf[at] = sum(dot_tn(a[...], g[...]) for a, g in zip(acts, gds)).astype(BF)
    up_buf[at] = sum(dot_tn(n[...], g[...]) for n, g in zip(n2s, gus)).astype(BF)
    copies(step, lambda c: c.start())

    @pl.when(step == 2 * STEPS - 1)
    def _():
        copies(step - 1, lambda c: c.wait())
        copies(step, lambda c: c.wait())


def call_mlp_grads(slots, acts, gds, n2s, gus):
    rows = gds[0].shape[0]
    wide = STEP_HID // 2
    by_hidden = pl.BlockSpec((rows, wide), lambda s, a, b: (0, s))
    whole = pl.BlockSpec((rows, D), lambda s, a, b: (0, 0))
    buffer = jax.ShapeDtypeStruct((SHARE_TILES * BLK, BLK), BF)
    return pl.pallas_call(
        mlp_grads,
        grid_spec=pltpu.PrefetchScalarGridSpec(
            num_scalar_prefetch=2,
            grid=(2 * STEPS,),
            in_specs=[by_hidden] * 2 + [whole] * 4 + [by_hidden] * 2,
            out_specs=[ANY, ANY],
            scratch_shapes=[
                pltpu.VMEM((2, wide, D), BF),
                pltpu.VMEM((2, D, wide), BF),
                pltpu.SemaphoreType.DMA((2,)),
            ],
        ),
        out_shape=[buffer, buffer],
        compiler_params=params(),
        cost_estimate=cost(2 * 2 * rows * D * 2 * HID * 2, 16 << 20),
        name="mlp_grads",
    )(*slots, *acts, *gds, *n2s, *gus)


def attention_grads(slot_own, slot_par, *refs):
    atts, gbs, n1s, gqs, gks, gvs = (refs[2 * i : 2 * i + 2] for i in range(6))
    own_ref, par_ref, out_buf, qkv_buf, sems = refs[14:]
    step = pl.program_id(0)
    at = lax.rem(step, 2)
    per_share = D // NARROW // BLK

    def copies(of_step, act_on):
        part = lax.rem(of_step, 2)
        column = lax.rem(of_step, per_share)

        def one(block, carry):
            block_row = pl.multiple_of(block * BLK, BLK)
            for slots, out in ((slot_own, own_ref), (slot_par, par_ref)):
                mine = (of_step < per_share) if out is own_ref else (of_step >= per_share)

                @pl.when(mine)
                def _():
                    row = pl.multiple_of(slots[48 + column * 8 + block] * BLK, BLK)
                    act_on(
                        pltpu.make_async_copy(
                            out_buf.at[part, :, pl.ds(block_row, BLK)],
                            out.at[pl.ds(row, BLK), :],
                            sems.at[part],
                        )
                    )
                    for third in range(3):
                        tile = block * 6 + third * 2 + column
                        row = pl.multiple_of(slots[tile] * BLK, BLK)
                        act_on(
                            pltpu.make_async_copy(
                                qkv_buf.at[part, third, pl.ds(block_row, BLK), :],
                                out.at[pl.ds(row, BLK), :],
                                sems.at[part],
                            )
                        )

            return carry

        lax.fori_loop(0, 8, one, 0)

    @pl.when(step >= 2)
    def _():
        copies(step - 2, lambda c: c.wait())

    out_buf[at] = sum(dot_tn(a[...], g[...]) for a, g in zip(atts, gbs)).astype(BF)
    for third, grads in enumerate((gqs, gks, gvs)):
        qkv_buf[at, third] = sum(dot_tn(n[...], g[...]) for n, g in zip(n1s, grads)).astype(BF)
    copies(step, lambda c: c.start())

    @pl.when(step == 2 * per_share - 1)
    def _():
        copies(step - 1, lambda c: c.wait())
        copies(step, lambda c: c.wait())


def call_attention_grads(slots, atts, gbs, n1s, gps, own, par):
    rows = gbs[0].shape[0]
    steps = WID // BLK
    whole = pl.BlockSpec((rows, D), lambda s, a, b: (0, 0))

    def by_column(third):
        return pl.BlockSpec((rows, BLK), lambda s, a, b: (0, third * steps + s))

    return pl.pallas_call(
        attention_grads,
        grid_spec=pltpu.PrefetchScalarGridSpec(
            num_scalar_prefetch=2,
            grid=(steps,),
            in_specs=[by_column(0)] * 2
            + [whole] * 4
            + [by_column(0)] * 2
            + [by_column(1)] * 2
            + [by_column(2)] * 2
            + [ANY, ANY],
            out_specs=[ANY, ANY],
            scratch_shapes=[
                pltpu.VMEM((2, BLK, D), BF),
                pltpu.VMEM((2, 3, D, BLK), BF),
                pltpu.SemaphoreType.DMA((2,)),
            ],
        ),
        out_shape=[jax.ShapeDtypeStruct(own.shape, BF)] * 2,
        input_output_aliases={14: 0, 15: 1},
        compiler_params=params(),
        cost_estimate=cost(2 * 2 * rows * D * 4 * WID, 8 << 20),
        name="attention_grads",
    )(*slots, *atts, *gbs, *n1s, *gps, *gps, *gps, own, par)


def place_of(tile, share):
    quarter = WID // 2
    block, rest = tile // 6, tile % 6
    third, column = rest // 2, rest % 2
    qkv_row = jnp.where(third == 2, D, 0) + block * BLK
    qkv_col = jnp.where(third == 1, WID, 0) + share * quarter + column * BLK
    out = tile - 48
    out_block, out_col = out // 8, out % 8
    out_row = D + jnp.where(out_col >= 4, WID, 0) + share * quarter + out_block * BLK
    out_col = WID + (out_col % 4) * BLK
    up = tile - 64
    up_row, up_col = 2 * D + share * D + (up // 8) * BLK, (up % 8) * BLK
    down = tile - 128
    down_row, down_col = 4 * D + share * D + (down // 8) * BLK, (down % 8) * BLK
    kind = (tile >= 48).astype(jnp.int32) + (tile >= 64) + (tile >= 128)
    row = jnp.select([kind == 0, kind == 1, kind == 2], [qkv_row, out_row, up_row], down_row)
    col = jnp.select([kind == 0, kind == 1, kind == 2], [qkv_col, out_col, up_col], down_col)
    return row, col


def assemble_kernel(plan, rows, cols, *refs):
    sources = refs[: len(plan)]
    out_ref, sem = refs[-2:]

    def run(at, act_on):
        share, first, count = plan[at]

        def one(i, carry):
            row = pl.multiple_of(rows[share, first + i], BLK)
            col = pl.multiple_of(cols[share, first + i], BLK)
            from_row = pl.multiple_of(i * BLK, BLK)
            act_on(
                pltpu.make_async_copy(
                    sources[at].at[pl.ds(from_row, BLK), :],
                    out_ref.at[pl.ds(row, BLK), pl.ds(col, BLK)],
                    sem,
                )
            )
            return carry

        lax.fori_loop(0, count, one, 0)

    for at in range(len(plan)):
        run(at, lambda c: c.start())
    for at in range(len(plan)):
        run(at, lambda c: c.wait())


def assemble(table, pieces, weights):
    plan = [piece[:3] for piece in pieces]
    arrays = [piece[3] for piece in pieces]
    alias = {} if weights is None else {2 + len(arrays): 0}
    args = list(table) + arrays + ([] if weights is None else [weights])
    return pl.pallas_call(
        functools.partial(assemble_kernel, plan),
        out_shape=jax.ShapeDtypeStruct((6 * D, D), BF),
        in_specs=[SMEM, SMEM] + [HBM] * len(arrays) + ([] if weights is None else [VMEM]),
        out_specs=VMEM,
        scratch_shapes=[pltpu.SemaphoreType.DMA],
        input_output_aliases=alias,
        compiler_params=params(),
        cost_estimate=cost(0, BLK),
        name="assemble",
    )(*args)


def ring(size):
    order = list(range(0, size, 2)) + list(range(size - 1, 0, -2))
    ahead = [(order[i], order[(i + 1) % size]) for i in range(size)]
    position = [order.index(i) for i in range(size)]
    return order, position, ahead, [(b, a) for a, b in ahead]


def after(value, *earlier):
    return lax.optimization_barrier((value, *earlier))[0]


def need_order(size):
    far = size // 2
    order = [far]
    for step in range(far - 1, 0, -1):
        order += [step, size - step]
    return order + [0]


class Gather:
    def __init__(self, unit, size, per_device):
        _, _, self.ahead, self.behind = ring(size)
        self.size, self.per_device, self.step_count = size, per_device, 0
        self.up = self.down = unit

    def step(self, *earlier):
        self.step_count += 1
        step, far, front = self.step_count, self.size // 2, self.per_device // 2
        up, down = self.up, self.down
        if step == far:
            up, down = up[: front * BLK], down[front * BLK :]
        up, down, *_ = lax.optimization_barrier((up, down, *earlier))
        self.sent = (up, down)
        self.up = lax.ppermute(up, "wide", self.ahead)
        self.down = lax.ppermute(down, "wide", self.behind)
        if step < far:
            return [
                (self.size - step, 0, self.per_device, self.up),
                (step, 0, self.per_device, self.down),
            ]
        return [
            (far, 0, front, self.up),
            (far, front, self.per_device - front, self.down),
        ]


class Scatter:
    def __init__(self, unit_of, size, cut):
        _, _, self.ahead, self.behind = ring(size)
        self.unit_of, self.size, self.cut, self.left = unit_of, size, cut, size // 2

    def step(self, *earlier):
        cut = self.cut
        if self.left == self.size // 2:
            last = self.unit_of(self.left)
            up, down = last[:cut], last[cut:]
        else:
            up, down = self.unit_of(self.left), self.unit_of(self.size - self.left)
            got_up, got_down = self.up.astype(F32), self.down.astype(F32)
            if self.left == self.size // 2 - 1:
                up = jnp.concatenate([up[:cut] + got_up, up[cut:]])
                down = jnp.concatenate([down[:cut], down[cut:] + got_down])
            else:
                up, down = up + got_up, down + got_down
        up, down = up.astype(BF), down.astype(BF)
        up, down, *_ = lax.optimization_barrier((up, down, *earlier))
        self.sent = (up, down)
        self.up = lax.ppermute(up, "wide", self.ahead)
        self.down = lax.ppermute(down, "wide", self.behind)
        self.left -= 1

    def result(self):
        return self.unit_of(0) + self.up.astype(F32) + self.down.astype(F32)


def mesh_bits():
    out, base = [], 1
    for axis in ("narrow", "wide"):
        size, bit = lax.axis_size(axis), 1
        while bit < size:
            out.append((base * bit, axis, [(i, i ^ bit) for i in range(size)]))
            bit *= 2
        base *= size
    return out


def tile_ids(share):
    tile_rows = D // BLK
    shard_cols = D // (NARROW * BLK)
    shard_hidden = FF // (NARROW * BLK)
    count_qkv = tile_rows * 3 * tile_rows
    start_up = count_qkv + tile_rows * tile_rows
    start_down = start_up + tile_rows * (FF // BLK)
    row_part = jnp.arange(tile_rows)[:, None, None]
    third = jnp.arange(3)[None, :, None]
    column_part = jnp.arange(shard_cols)[None, None, :]
    qkv_ids = (
        row_part * 3 * tile_rows + third * tile_rows + share * shard_cols + column_part
    ).reshape(-1)
    out_ids = (
        count_qkv
        + (share * shard_cols + jnp.arange(shard_cols)[:, None]) * tile_rows
        + jnp.arange(tile_rows)[None, :]
    ).reshape(-1)
    up_ids = (
        start_up
        + jnp.arange(tile_rows)[:, None] * (FF // BLK)
        + share * shard_hidden
        + jnp.arange(shard_hidden)[None, :]
    ).reshape(-1)
    down_ids = (
        start_down
        + (share * shard_hidden + jnp.arange(shard_hidden)[:, None]) * tile_rows
        + jnp.arange(tile_rows)[None, :]
    ).reshape(-1)
    return jnp.concatenate([qkv_ids, out_ids, up_ids, down_ids])


def share_vectors(small_all, me):
    pieces = [small_all[i * D : (i + 1) * D] for i in range(8)]
    bias_up = small_all[8 * D :]

    def both(vector, width):
        own = lax.dynamic_slice_in_dim(vector, me * width, width)
        par = lax.dynamic_slice_in_dim(vector, (me ^ 1) * width, width)
        return jnp.concatenate([own, par])

    quarter = D // NARROW
    heads = jnp.concatenate([both(pieces[2], quarter), both(pieces[3], quarter)])
    rows = [pieces[0], pieces[1], heads, pieces[4], pieces[5], pieces[6], pieces[7]]
    up = both(bias_up, FF // NARROW)
    rows = rows + [up[0:D], up[D:]]
    return jnp.pad(jnp.stack(rows), ((0, 7), (0, 0)))


def small_vector(mlp_sums, att_sums, me):
    half = me // 2
    mine = [(half == t).astype(F32) for t in range(2)]
    mlp = mlp_sums[0] + mlp_sums[1]
    att = att_sums[0] + att_sums[1]
    bias_down = mine[0] * mlp_sums[0][2] + mine[1] * mlp_sums[1][2]
    bias_out = mine[0] * att_sums[0][3] + mine[1] * att_sums[1][3]
    odd = (me % 2) == 1

    def spread(own, par):
        placed = jnp.where(odd, jnp.concatenate([par, own]), jnp.concatenate([own, par]))
        return [jnp.where(half == 0, placed, 0.0), jnp.where(half == 1, placed, 0.0)]

    quarter = D // NARROW
    heads = att[2]
    return jnp.concatenate(
        [att[0], att[1]]
        + spread(heads[0:quarter], heads[quarter : 2 * quarter])
        + spread(heads[2 * quarter : 3 * quarter], heads[3 * quarter :])
        + [bias_out, mlp[0], mlp[1], bias_down]
        + spread(mlp[3], mlp[4])
    )


def total_over_mesh(value):
    value = jnp.broadcast_to(value.reshape(1, 1), (8, BLK))
    for _, axis, perm in mesh_bits():
        value = value + lax.ppermute(value, axis, perm)
    return value[0, 0]


def rotate_in_kernel(grad_ref, left_ref, right_ref, out_ref):
    for block in range(out_ref.shape[0]):
        grad = grad_ref[block * BLK : (block + 1) * BLK, :].astype(BF)
        inner = dot_tn(left_ref[0, block].astype(BF), grad)
        out_ref[block] = dot(inner.astype(BF), right_ref[0, block].astype(BF))


def rotate_in(layer, grads, left_basis, right_basis):
    count = left_basis.shape[1]
    group = 6
    spec = pl.BlockSpec((group, BLK, BLK), lambda i: (i, 0, 0))
    flat = pl.BlockSpec((group * BLK, BLK), lambda i: (i, 0))
    basis = pl.BlockSpec((1, group, BLK, BLK), lambda i: (layer, i, 0, 0))
    return pl.pallas_call(
        rotate_in_kernel,
        grid=(count // group,),
        out_shape=jax.ShapeDtypeStruct((count, BLK, BLK), F32),
        in_specs=[flat, basis, basis],
        out_specs=spec,
        compiler_params=params(10),
        cost_estimate=cost(count * 4 * BLK**3, count * BLK * BLK * 14),
        name="rotate_in",
    )(grads, left_basis, right_basis)


def update_kernel(clip_ref, rot0, rot1, left, right, first, second, master, *outs):
    new_first, new_second, new_master, new_weights = outs
    step = pl.program_id(0)
    half = pl.num_programs(0) // 2
    clip = clip_ref[0]
    for block in range(rot0.shape[0]):
        rotated = clip * jnp.where(step < half, rot0[block], rot1[block])
        one = 0.5 * first[0, block] + 0.5 * rotated
        two = 0.5 * second[0, block] + 0.5 * rotated * rotated
        new_first[0, block] = one
        new_second[0, block] = two
        direction = one / (jnp.sqrt(two) + 1e-08)
        inner = dot(left[0, block].astype(BF), direction.astype(BF))
        turned = dot_nt(inner.astype(BF), right[0, block].astype(BF))
        weights = master[0, block] - 0.02 * turned
        new_master[0, block] = weights
        new_weights[0, block] = weights.astype(BF)


def update(clip, rots, left, right, first, second, master):
    count = rots[0].shape[0]
    group = 3
    steps = count // group
    spec = pl.BlockSpec((1, group, BLK, BLK), lambda i: (i // steps, i % steps, 0, 0))
    low = pl.BlockSpec((group, BLK, BLK), lambda i: (jnp.minimum(i, steps - 1), 0, 0))
    high = pl.BlockSpec((group, BLK, BLK), lambda i: (jnp.maximum(i - steps, 0), 0, 0))
    shape = jax.ShapeDtypeStruct(master.shape, F32)
    return pl.pallas_call(
        update_kernel,
        grid=(2 * steps,),
        out_shape=[shape, shape, shape, jax.ShapeDtypeStruct(master.shape, BF)],
        in_specs=[SMEM, low, high] + [spec] * 5,
        out_specs=[spec] * 4,
        compiler_params=params(10),
        cost_estimate=cost(count * 8 * BLK**3, count * BLK * BLK * 2 * 38),
        name="update",
    )(clip, *rots, left, right, first, second, master)


def shards(
    images,
    cotangent,
    kept_tokens,
    owner_slots,
    master_blocks,
    small_params,
    left_basis,
    right_basis,
    first_moment,
    second_moment,
    small_first,
    small_second,
):
    me = lax.axis_index("narrow")
    half, core = me // 2, me % 2
    wide = lax.axis_size("wide")
    per_device = master_blocks.shape[1]
    own_small = small_params.shape[1]
    own_images = images.shape[0]
    rows = own_images * S

    device = lax.axis_index("wide") * NARROW + me
    by_distance = jnp.arange(wide * NARROW) ^ device

    def chunks(own):
        other = lax.ppermute(own, "narrow", ACROSS)
        return [jnp.where(half == t, own, other) for t in range(2)]

    kept = [
        lax.dynamic_slice_in_dim(kept_tokens, (2 * t + core) * own_images, own_images, 0)
        .reshape(1, rows)
        .astype(F32)
        for t in range(2)
    ]

    order, position, _, _ = ring(wide)
    place = jnp.take(jnp.asarray(position, jnp.int32), lax.axis_index("wide"))
    around = jnp.take(jnp.asarray(order, jnp.int32), (place + jnp.arange(wide)) % wide)

    needed = need_order(wide)
    turns = [needed.index(distance) for distance in range(wide)]
    slots, tables = [], []
    for layer in range(LAYERS):
        owners = owner_slots[layer]
        layer_slots, layer_rows, layer_cols = [], [], []
        for at, share in enumerate((me, me ^ 1)):
            slot = jnp.take(owners, tile_ids(share))
            at_wide, at_pos = slot // per_device // NARROW, slot % per_device
            distance = (jnp.take(jnp.asarray(position, jnp.int32), at_wide) - place) % wide
            relative = distance * per_device + at_pos
            turn = jnp.take(jnp.asarray(turns, jnp.int32), distance)
            layer_slots.append(turn * per_device + at_pos)
            here = relative[None, :] == jnp.arange(SHARE_TILES)[:, None]
            tile = jnp.sum(jnp.where(here, jnp.arange(SHARE_TILES)[None, :], 0), axis=1)
            row, col = place_of(tile, at)
            layer_rows.append(row)
            layer_cols.append(col)
        slots.append(layer_slots)
        tables.append((jnp.stack(layer_rows), jnp.stack(layer_cols)))

    def core_swap(value):
        return lax.ppermute(value, "narrow", CORE)

    def exchange(part):
        return lax.ppermute(part, "narrow", ACROSS)

    units = [
        master_blocks[layer].astype(BF).reshape(per_device * BLK, BLK) for layer in range(LAYERS)
    ]

    def swapped(pieces):
        return [piece + (core_swap(piece[3]),) for piece in pieces]

    def place_pieces(layer, pieces, matrix):
        group = [
            (share, distance * per_device + first, count, pair[share])
            for distance, first, count, *pair in pieces
            for share in range(2)
        ]
        return assemble(tables[layer], group, matrix)

    steps = wide // 2
    own_small_rows = small_params.astype(BF).reshape(1, -1)
    small_rows = own_small_rows
    bits = mesh_bits()
    near_bits, far_bits = bits[:2], bits[2:]
    per_window = -(-len(far_bits) // max(steps - 1, 1))

    def grow(rows, some_bits):
        for _, axis, perm in some_bits:
            rows = jnp.concatenate([rows, lax.ppermute(rows, axis, perm)])
        return rows

    gather = Gather(units[0], wide, per_device)
    arrived = [(0, 0, per_device, units[0])] + gather.step()
    small_rows = grow(small_rows, near_bits)
    placed, inputs, extra = [], [images, cotangent], [small_rows]
    brought = []
    for step in range(2, steps + 1):
        latest = swapped(arrived)
        arrived = gather.step(*extra)
        extra = [piece[4] for piece in latest]
        placed = placed + latest
        if inputs:
            brought.append(chunks(after(inputs.pop(0).reshape(rows, D), *gather.sent)))
            extra += brought[-1]
        at = (step - 2) * per_window
        small_rows = grow(small_rows, far_bits[at : at + per_window])
        if step < steps:
            extra.append(small_rows)
    while inputs:
        brought.append(chunks(inputs.pop(0).reshape(rows, D)))
    hidden_in, cot = brought
    next_unit = after(units[1], gather.up, gather.down)
    gather_next = Gather(next_unit, wide, per_device)
    arrived_next = [(0, 0, per_device, next_unit)] + gather_next.step()
    last = [piece[:3] + (after(piece[3], *gather_next.sent),) for piece in arrived]
    weights = [place_pieces(0, placed + swapped(last), None)]

    in_order = jnp.take(small_rows, by_distance, axis=0).astype(F32)
    small_all = in_order.reshape(-1, LAYERS, own_small).transpose(1, 0, 2).reshape(LAYERS, -1)
    vecs = [share_vectors(small_all[layer], me) for layer in range(LAYERS)]

    saved = []
    state = None
    for layer in range(LAYERS):
        att_w = mlp_w = weights[layer]
        kept_layer = []
        for t in range(2):
            if layer == 0:
                out = call_attention_forward(True, (hidden_in[t],), vecs[0], kept[t], att_w)
                hidden = hidden_in[t]
            else:
                hidden, *out = call_attention_forward(
                    False, state[t] + (vecs[layer - 1],), vecs[layer], kept[t], att_w
                )
            n1, qkv, lse, att, part = out
            kept_layer.append([hidden, n1, qkv, lse, att, part, exchange(part)])
        kept_layer[0][5] = after(kept_layer[0][5], kept_layer[1][5])
        state = []
        for t in range(2):
            hidden, n1, qkv, lse, att, part, got = kept_layer[t]
            if layer == 0 and t == 0:
                placed = swapped(arrived_next)
                arrived_next = gather_next.step(part)
                part = after(part, *gather_next.sent)
            middle, n2, act, slope, down_part = call_mlp_forward(
                hidden, part, got, vecs[layer], mlp_w
            )
            kept_layer[t] = (hidden, n1, qkv, lse, att, middle, n2, act, slope)
            if layer < LAYERS - 1:
                state.append((middle, down_part, exchange(down_part)))
            else:
                state.append((middle, down_part))
        saved.append((att_w, mlp_w, kept_layer))
        if layer == 0:
            gates = [down_part] + [piece[4] for piece in placed]
            for step in range(3, steps + 1):
                latest = swapped(arrived_next)
                arrived_next = gather_next.step(*gates)
                gates = [piece[4] for piece in latest]
                placed = placed + latest
            weights.append(place_pieces(1, placed + swapped(arrived_next), None))

    def mine(pair):
        return jnp.where(half == 0, pair[0], pair[1])

    def theirs(pair):
        return jnp.where(half == 0, pair[1], pair[0])

    down_parts = [state[t][1] for t in range(2)]
    middles = [state[t][0] for t in range(2)]
    final = mine(middles) + (
        mine(down_parts).astype(F32)
        + exchange(theirs(down_parts)).astype(F32)
        + vecs[LAYERS - 1][6]
    )
    block_output = final.astype(BF).reshape(images.shape)

    upstream = None
    reduced = [None] * LAYERS
    small_terms = [None] * LAYERS
    pending = None
    for layer in reversed(range(LAYERS)):
        att_w, mlp_w, kept_layer = saved[layer]
        top = layer == LAYERS - 1
        work = []
        for t in range(2):
            hidden, n1, qkv, lse, att, middle, n2, act, slope = kept_layer[t]
            if top:
                grad = cot[t]
                gd, gu, part, sums = call_mlp_backward(
                    True, (grad,), middle, slope, vecs[layer], mlp_w
                )
            else:
                state = upstream[t]
                state = (after(state[0], *pending.sent),) + state[1:]
                grad, gd, gu, part, sums = call_mlp_backward(
                    False, state + (vecs[layer + 1],), middle, slope, vecs[layer], mlp_w
                )
                if t == 0:
                    pending.step(part)
            work.append([grad, gd, gu, part, sums, exchange(part)])
        gds = [w[1] for w in work]
        if pending is not None:
            gds[0] = after(gds[0], *pending.sent)
        own, par = call_mlp_grads(
            slots[layer],
            [k[7] for k in kept_layer],
            gds,
            [k[6] for k in kept_layer],
            [w[2] for w in work],
        )
        if pending is not None:
            pending.step(own)
        back = []
        for t in range(2):
            hidden, n1, qkv, lse, att, middle, n2, act, slope = kept_layer[t]
            grad, gd, gu, part, sums, got = work[t]
            if pending is not None:
                part = after(part, *pending.sent)
            gm, gb, gp, att_part, att_sums = call_attention_backward(
                grad, part, got, middle, hidden, qkv, lse, vecs[layer], kept[t], att_w
            )
            back.append((gm, gb, gp, att_part, att_sums))
        if pending is not None:
            pending.step(back[1][3])
            while pending.left > 0:
                pending.step()
            own = after(own, *pending.sent)
            reduced[layer + 1] = pending.result()
            arrivals = [pending.up, pending.down]
        if layer > 0:
            upstream = [
                (back[t][0], back[t][3], exchange(back[t][3]), kept_layer[t][0]) for t in range(2)
            ]
        own, par = call_attention_grads(
            slots[layer],
            [k[4] for k in kept_layer],
            [b[1] for b in back],
            [k[1] for k in kept_layer],
            [b[2] for b in back],
            own,
            par,
        )
        terms = small_vector([w[4] for w in work], [b[4] for b in back], me)
        small_terms[layer] = terms.reshape(-1, own_small)
        unit_len = per_device * BLK

        first_got = core_swap(par[:unit_len])
        earlier = pending
        pending = Scatter(None, wide, (per_device // 2) * BLK)

        def first_unit(distance, own=own, got=first_got, unit_len=unit_len):
            return own[:unit_len].astype(F32) + got.astype(F32)

        pending.unit_of = first_unit
        pending.step()
        rest = core_swap(after(par, *pending.sent))

        def unit_of(distance, own=own, rest=rest, unit_len=unit_len):
            at = turns[distance] * unit_len
            return own[at : at + unit_len].astype(F32) + rest[at : at + unit_len].astype(F32)

        pending.unit_of = unit_of

    parts = [b[3] for b in back]
    last_part = exchange(after(theirs(parts), *pending.sent)).astype(F32)
    small_rows = jnp.take(jnp.concatenate(small_terms, axis=1), by_distance, axis=0)
    small_rows = after(small_rows, *pending.sent)
    backward_bits = mesh_bits()[::-1]
    while pending.left > 0:
        for bit, axis, perm in backward_bits[:per_window]:
            small_rows = small_rows[:bit] + lax.ppermute(small_rows[bit:], axis, perm)
        backward_bits = backward_bits[per_window:]
        pending.step(small_rows, last_part, *arrivals)
        small_rows = after(small_rows, *pending.sent)
    for bit, axis, perm in backward_bits:
        small_rows = small_rows[:bit] + lax.ppermute(small_rows[bit:], axis, perm)
    reduced[0] = pending.result()
    hidden = mine([k[0] for k in saved[0][2]]).astype(F32)
    centre, rstd = stats(hidden)
    lower = norm_back(mine(parts).astype(F32) + last_part, centre * rstd, rstd, vecs[0][0:1])
    input_grad = (mine([b[0] for b in back]) + lower).reshape(images.shape)

    grad_small = small_rows.reshape(LAYERS, own_small)
    local_sum = jnp.sum(grad_small * grad_small)
    for grads in reduced[::-1]:
        local_sum = local_sum + jnp.sum(grads * grads)
    grad_norm = jnp.sqrt(total_over_mesh(local_sum))
    clip_factor = 1.0 / jnp.maximum(grad_norm, 1.0)
    rots = [
        rotate_in(layer, reduced[layer], left_basis, right_basis) for layer in range(LAYERS)
    ]
    new_first, new_second, new_master, new_weights = update(
        clip_factor.reshape(1),
        rots,
        left_basis,
        right_basis,
        first_moment,
        second_moment,
        master_blocks,
    )
    clipped_small = clip_factor * grad_small
    new_small_first = 0.5 * small_first + 0.5 * clipped_small
    new_small_second = 0.5 * small_second + 0.5 * clipped_small * clipped_small
    new_small = small_params - 0.3 * new_small_first / (jnp.sqrt(new_small_second) + 1e-08)
    return (
        block_output,
        input_grad,
        grad_norm.reshape(1),
        new_first,
        new_second,
        new_master,
        new_weights,
        new_small_first,
        new_small_second,
        new_small,
        new_small.astype(BF),
    )


def solution(mesh):
    both = ("wide", "narrow")
    rows = P(both, None, None)
    blocks = P(None, both, None, None)
    small = P(None, both)
    in_specs = (
        rows,
        rows,
        P("wide", None),
        P(),
        blocks,
        small,
        blocks,
        blocks,
        blocks,
        blocks,
        small,
        small,
    )
    out_specs = (rows, rows, P(), blocks, blocks, blocks, blocks, small, small, small, small)
    return jax.shard_map(shards, mesh=mesh, in_specs=in_specs, out_specs=out_specs, check_vma=False)
```

```python
import functools

import jax
import jax.numpy as jnp
from jax import lax
from jax.experimental import pallas as pl
from jax.experimental.pallas import tpu as pltpu
from jax.sharding import PartitionSpec as P

D = 1024
HEAD_DIM = 64
FF = 4096
S = 50
LAYERS = 2
BLK = 128
NARROW = 4

BF = jnp.bfloat16
F32 = jnp.float32

WID = D // 2
HID = FF // 2
SHARE_TILES = 192
ATT_ROWS = 2 * D
MLP_ROWS = 4 * D

CORE = [(j, j ^ 1) for j in range(NARROW)]
ACROSS = [(j, j ^ 2) for j in range(NARROW)]
ANY = pl.BlockSpec(memory_space=pl.ANY)
SMEM = pl.BlockSpec(memory_space=pltpu.SMEM)
VMEM = pl.BlockSpec(memory_space=pltpu.VMEM)


def params(mib=16):
    return pltpu.CompilerParams(vmem_limit_bytes=mib << 20)


def cost(flops, nbytes):
    return pl.CostEstimate(flops=flops, bytes_accessed=nbytes, transcendentals=0)


def dot(a, b):
    return jnp.dot(a, b, preferred_element_type=F32)


def dot_nt(a, b):
    return lax.dot_general(a, b, (((1,), (1,)), ((), ())), preferred_element_type=F32)


def dot_tn(a, b):
    return lax.dot_general(a, b, (((0,), (0,)), ((), ())), preferred_element_type=F32)


def stats(x):
    centre = x - jnp.mean(x, axis=-1, keepdims=True)
    spread = jnp.mean(centre * centre, axis=-1, keepdims=True)
    return centre, lax.rsqrt(spread + 1e-06)


def norm_back(grad, xhat, rstd, gain):
    gn = grad * gain
    return rstd * (
        gn
        - jnp.mean(gn, axis=-1, keepdims=True)
        - xhat * jnp.mean(gn * xhat, axis=-1, keepdims=True)
    )


def key_bias(kept_row, rows):
    def image_of(dim):
        return lax.rem(lax.broadcasted_iota(jnp.int32, (rows, rows), dim), rows // S)

    allowed = (image_of(0) == image_of(1)) & (kept_row > 0.0)
    return jnp.where(allowed, 0.0, -1e30)


def lane_half(x, half):
    lane = lax.broadcasted_iota(jnp.int32, x.shape, 1)
    keep = (lane < HEAD_DIM) if half == 0 else (lane >= HEAD_DIM)
    return jnp.where(keep, x, jnp.zeros_like(x))


def attention_forward(first, *refs):
    if first:
        x_ref, vecs, kept, weights, n1_ref, qkv_ref, lse_ref, att_ref, part_ref, _ = refs
        hidden = x_ref[...].astype(F32)
    else:
        (mid_ref, own_ref, got_ref, prev, vecs, kept, weights) = refs[:7]
        hidden_ref, n1_ref, qkv_ref, lse_ref, att_ref, part_ref, _ = refs[7:]
        hidden = mid_ref[...] + (
            own_ref[...].astype(F32) + got_ref[...].astype(F32) + prev[6:7, :]
        )
        hidden_ref[...] = hidden
    rows = hidden.shape[0]
    centre, rstd = stats(hidden)
    n1 = (centre * rstd * vecs[0:1, :] + vecs[1:2, :]).astype(BF)
    n1_ref[...] = n1
    qkv_ref[:, 0:WID] = (dot(n1, weights[0:D, 0:WID]) + vecs[2:3, 0:WID]).astype(BF)
    qkv_ref[:, WID : 2 * WID] = dot(n1, weights[0:D, WID:D]).astype(BF)
    qkv_ref[:, 2 * WID :] = (dot(n1, weights[D : 2 * D, 0:WID]) + vecs[2:3, WID:D]).astype(BF)
    bias = key_bias(kept[0:1, :], rows)
    lane = lax.broadcasted_iota(jnp.int32, (rows, BLK), 1)
    lse_all = jnp.zeros((rows, BLK), F32)
    for pair in range(WID // BLK):
        cols = slice(pair * BLK, (pair + 1) * BLK)
        q = qkv_ref[:, cols] * jnp.asarray(0.125, BF)
        k = qkv_ref[:, WID + pair * BLK : WID + (pair + 1) * BLK]
        v = qkv_ref[:, 2 * WID + pair * BLK : 2 * WID + (pair + 1) * BLK]
        outs = []
        for half in range(2):
            scores = dot_nt(lane_half(q, half), k) + bias
            top = jnp.max(scores, axis=-1, keepdims=True)
            raised = jnp.exp(scores - top)
            total = jnp.sum(raised, axis=-1, keepdims=True)
            outs.append(dot((raised * (1.0 / total)).astype(BF), v))
            lse_all = jnp.where(lane == 2 * pair + half, top + jnp.log(total), lse_all)
        att_ref[:, cols] = jnp.where(lane < HEAD_DIM, outs[0], outs[1]).astype(BF)
    lse_ref[...] = lse_all
    att = att_ref[...]
    part_ref[:, 0:WID] = dot(att, weights[D : D + WID, WID:D]).astype(BF)
    part_ref[:, WID:D] = dot(att, weights[D + WID : 2 * D, WID:D]).astype(BF)


def call_attention_forward(first, operands, vecs, kept, weights):
    rows = operands[0].shape[0]
    outs = [
        jax.ShapeDtypeStruct((rows, D), BF),
        jax.ShapeDtypeStruct((rows, 3 * WID), BF),
        jax.ShapeDtypeStruct((rows, BLK), F32),
        jax.ShapeDtypeStruct((rows, WID), BF),
        jax.ShapeDtypeStruct((rows, D), BF),
    ]
    if not first:
        outs = [jax.ShapeDtypeStruct((rows, D), F32)] + outs
    args = list(operands) + [vecs, kept, weights]
    return pl.pallas_call(
        functools.partial(attention_forward, first),
        out_shape=outs + [jax.ShapeDtypeStruct(weights.shape, BF)],
        grid=(1,),
        in_specs=[full(*a.shape) for a in args[:-1]] + [VMEM],
        out_specs=[full(*o.shape) for o in outs] + [VMEM],
        input_output_aliases={len(args) - 1: len(outs)},
        compiler_params=params(),
        cost_estimate=cost(2 * rows * D * 4 * WID * 2, 6 << 20),
        name="attention_forward",
    )(*args)


STEPS = 4
STEP_HID = HID // STEPS


def mlp_forward(hid_ref, own_ref, got_ref, vecs, weights, *rest):
    mid_ref, n2_ref, act_ref, slope_ref, part_ref, _, total = rest
    step = pl.program_id(0)

    @pl.when(step == 0)
    def _():
        middle = hid_ref[...].astype(F32) + (
            own_ref[...].astype(F32) + got_ref[...].astype(F32) + vecs[3:4, :]
        )
        mid_ref[...] = middle
        centre, rstd = stats(middle)
        n2_ref[...] = (centre * rstd * vecs[4:5, :] + vecs[5:6, :]).astype(BF)

    row = 7 + step // 2
    bias = jnp.where(
        step % 2 == 0, vecs[pl.ds(row, 1), 0:STEP_HID], vecs[pl.ds(row, 1), STEP_HID:D]
    )
    upward = dot(n2_ref[...], up_part(weights, step)) + bias
    cdf = 0.5 + 0.5 * lax.erf(upward * 0.7071067811865476)
    act = (upward * cdf).astype(BF)
    act_ref[...] = act
    slope_ref[...] = (
        cdf + upward * (jnp.exp(-0.5 * upward * upward) * 0.3989422804014327)
    ).astype(BF)
    term = dot(act, down_part(weights, step))

    @pl.when(step == 0)
    def _():
        total[...] = term

    @pl.when((step > 0) & (step < STEPS - 1))
    def _():
        total[...] += term

    @pl.when(step == STEPS - 1)
    def _():
        part_ref[...] = (total[...] + term).astype(BF)


def full(rows, cols):
    return pl.BlockSpec((rows, cols), lambda s: (0, 0))


def up_part(weights, step):
    rows = pl.ds(pl.multiple_of(2 * D + step // 2 * D, D), D)
    return weights[rows, pl.ds(pl.multiple_of(step % 2 * STEP_HID, STEP_HID), STEP_HID)]


def down_part(weights, step):
    return weights[pl.ds(pl.multiple_of(4 * D + step * STEP_HID, STEP_HID), STEP_HID), :]


def call_mlp_forward(hidden, own, got, vecs, weights):
    rows = hidden.shape[0]
    return pl.pallas_call(
        mlp_forward,
        grid=(STEPS,),
        out_shape=[
            jax.ShapeDtypeStruct((rows, D), F32),
            jax.ShapeDtypeStruct((rows, D), BF),
            jax.ShapeDtypeStruct((rows, HID), BF),
            jax.ShapeDtypeStruct((rows, HID), BF),
            jax.ShapeDtypeStruct((rows, D), BF),
            jax.ShapeDtypeStruct(weights.shape, BF),
        ],
        input_output_aliases={4: 5},
        in_specs=[full(rows, D), full(rows, D), full(rows, D), full(16, D), VMEM],
        out_specs=[
            full(rows, D),
            full(rows, D),
            pl.BlockSpec((rows, STEP_HID), lambda s: (0, s)),
            pl.BlockSpec((rows, STEP_HID), lambda s: (0, s)),
            full(rows, D),
            VMEM,
        ],
        scratch_shapes=[pltpu.VMEM((rows, D), F32)],
        compiler_params=params(),
        cost_estimate=cost(2 * rows * D * 2 * HID * 2, 12 << 20),
        name="mlp_forward",
    )(hidden, own, got, vecs, weights)


def mlp_backward(first, *refs):
    if first:
        grad_ref, mid_ref, slope_ref, vecs, weights = refs[:5]
        gd_ref, gu_ref, part_ref, sums_ref, _, total = refs[5:]
    else:
        (gm_ref, own_ref, got_ref, hid_ref, above) = refs[:5]
        mid_ref, slope_ref, vecs, weights = refs[5:9]
        grad_out_ref, gd_ref, gu_ref, part_ref, sums_ref, _, total = refs[9:]
    step = pl.program_id(0)

    @pl.when(step == 0)
    def _():
        if first:
            gd_ref[...] = grad_ref[...]
        else:
            centre, rstd = stats(hid_ref[...])
            grad = own_ref[...].astype(F32) + got_ref[...].astype(F32)
            grad_hidden = gm_ref[...] + norm_back(grad, centre * rstd, rstd, above[0:1, :])
            grad_out_ref[...] = grad_hidden
            gd_ref[...] = grad_hidden.astype(BF)
        sums_ref[...] = jnp.zeros_like(sums_ref)
        sums_ref[2:3, :] = jnp.sum(gd_ref[...].astype(F32), axis=0, keepdims=True)

    grad_up = (slope_ref[...].astype(F32) * dot_nt(gd_ref[...], down_part(weights, step))).astype(BF)
    gu_ref[...] = grad_up
    sums = jnp.sum(grad_up.astype(F32), axis=0, keepdims=True)
    for at in range(STEPS):

        @pl.when(step == at)
        def _():
            sums_ref[3 + at // 2 : 4 + at // 2, (at % 2) * STEP_HID : (at % 2 + 1) * STEP_HID] = (
                sums
            )

    term = dot_nt(grad_up, up_part(weights, step))

    @pl.when(step == 0)
    def _():
        total[...] = term

    @pl.when((step > 0) & (step < STEPS - 1))
    def _():
        total[...] += term

    @pl.when(step == STEPS - 1)
    def _():
        grad = total[...] + term
        part_ref[...] = grad.astype(BF)
        centre, rstd = stats(mid_ref[...])
        sums_ref[0:1, :] = jnp.sum(grad * (centre * rstd), axis=0, keepdims=True)
        sums_ref[1:2, :] = jnp.sum(grad, axis=0, keepdims=True)


def call_mlp_backward(first, operands, middle, slope, vecs, weights):
    rows = middle.shape[0]
    specs = [full(rows, D)] if first else [full(rows, D)] * 4 + [full(16, D)]
    outs = [
        jax.ShapeDtypeStruct((rows, D), BF),
        jax.ShapeDtypeStruct((rows, HID), BF),
        jax.ShapeDtypeStruct((rows, D), BF),
        jax.ShapeDtypeStruct((8, D), F32),
    ]
    out_specs = [
        full(rows, D),
        pl.BlockSpec((rows, STEP_HID), lambda s: (0, s)),
        full(rows, D),
        full(8, D),
    ]
    if not first:
        outs = [jax.ShapeDtypeStruct((rows, D), F32)] + outs
        out_specs = [full(rows, D)] + out_specs
    return pl.pallas_call(
        functools.partial(mlp_backward, first),
        grid=(STEPS,),
        out_shape=outs + [jax.ShapeDtypeStruct(weights.shape, BF)],
        input_output_aliases={len(specs) + 3: len(outs)},
        in_specs=specs
        + [full(rows, D), pl.BlockSpec((rows, STEP_HID), lambda s: (0, s)), full(16, D), VMEM],
        out_specs=out_specs + [VMEM],
        scratch_shapes=[pltpu.VMEM((rows, D), F32)],
        compiler_params=params(),
        cost_estimate=cost(2 * rows * D * 2 * HID * 2, 12 << 20),
        name="mlp_backward",
    )(*operands, middle, slope, vecs, weights)


def attention_backward(
    grad_ref,
    own_ref,
    got_ref,
    mid_ref,
    hid_ref,
    qkv_ref,
    lse_ref,
    vecs,
    kept,
    weights,
    gm_ref,
    gb_ref,
    gp_ref,
    part_ref,
    sums_ref,
    _,
):
    rows = grad_ref.shape[0]
    centre, rstd = stats(mid_ref[...])
    grad_two = own_ref[...].astype(F32) + got_ref[...].astype(F32)
    grad_middle = grad_ref[...].astype(F32) + norm_back(
        grad_two, centre * rstd, rstd, vecs[4:5, :]
    )
    gm_ref[...] = grad_middle
    gb = grad_middle.astype(BF)
    gb_ref[...] = gb
    sums_ref[...] = jnp.zeros_like(sums_ref)
    sums_ref[3:4, :] = jnp.sum(gb.astype(F32), axis=0, keepdims=True)
    grad_att = (
        dot_nt(gb[:, 0:WID], weights[D : D + WID, WID:D])
        + dot_nt(gb[:, WID:D], weights[D + WID : 2 * D, WID:D])
    ).astype(BF)
    bias = key_bias(kept[0:1, :], rows)
    lane = lax.broadcasted_iota(jnp.int32, (rows, BLK), 1)
    for pair in range(WID // BLK):
        cols = slice(pair * BLK, (pair + 1) * BLK)
        key_cols = slice(WID + pair * BLK, WID + (pair + 1) * BLK)
        value_cols = slice(2 * WID + pair * BLK, 2 * WID + (pair + 1) * BLK)
        q = qkv_ref[:, cols] * jnp.asarray(0.125, BF)
        k = qkv_ref[:, key_cols]
        v = qkv_ref[:, value_cols]
        g = grad_att[:, cols]
        got = []
        for half in range(2):
            head = 2 * pair + half
            scores = dot_nt(lane_half(q, half), k) + bias
            att = jnp.exp(scores - lse_ref[:, head : head + 1])
            grad_a = dot_nt(lane_half(g, half), v)
            inner = jnp.sum(att * grad_a, axis=-1, keepdims=True)
            grad_s = (att * (grad_a - inner)).astype(BF)
            got.append((dot(grad_s, k) * 0.125, dot_tn(grad_s, q), dot_tn(att.astype(BF), g)))
        for at, where in enumerate((cols, key_cols, value_cols)):
            gp_ref[:, where] = jnp.where(lane < HEAD_DIM, got[0][at], got[1][at]).astype(BF)
    sums_ref[2:3, 0:WID] = jnp.sum(gp_ref[:, 0:WID].astype(F32), axis=0, keepdims=True)
    sums_ref[2:3, WID:D] = jnp.sum(gp_ref[:, 2 * WID :].astype(F32), axis=0, keepdims=True)
    grad = (
        dot_nt(gp_ref[:, 0:WID], weights[0:D, 0:WID])
        + dot_nt(gp_ref[:, WID : 2 * WID], weights[0:D, WID:D])
        + dot_nt(gp_ref[:, 2 * WID :], weights[D : 2 * D, 0:WID])
    )
    part_ref[...] = grad.astype(BF)
    centre, rstd = stats(hid_ref[...].astype(F32))
    sums_ref[0:1, :] = jnp.sum(grad * (centre * rstd), axis=0, keepdims=True)
    sums_ref[1:2, :] = jnp.sum(grad, axis=0, keepdims=True)


def call_attention_backward(*args):
    rows = args[0].shape[0]
    outs = [
        jax.ShapeDtypeStruct((rows, D), F32),
        jax.ShapeDtypeStruct((rows, D), BF),
        jax.ShapeDtypeStruct((rows, 3 * WID), BF),
        jax.ShapeDtypeStruct((rows, D), BF),
        jax.ShapeDtypeStruct((8, D), F32),
    ]
    return pl.pallas_call(
        attention_backward,
        grid=(1,),
        out_shape=outs + [jax.ShapeDtypeStruct(args[-1].shape, BF)],
        input_output_aliases={len(args) - 1: len(outs)},
        in_specs=[full(*a.shape) for a in args[:-1]] + [VMEM],
        out_specs=[full(*o.shape) for o in outs] + [VMEM],
        compiler_params=params(),
        cost_estimate=cost(2 * rows * D * 4 * WID * 3, 8 << 20),
        name="attention_backward",
    )(*args)


def mlp_grads(slot_own, slot_par, *refs):
    acts, gds, n2s, gus = refs[0:2], refs[2:4], refs[4:6], refs[6:8]
    own_ref, par_ref, down_buf, up_buf, sems = refs[8:]
    step = pl.program_id(0)
    at = lax.rem(step, 2)
    tiles = STEP_HID // 2 // BLK

    def start(of_step):
        part = lax.rem(of_step, 2)
        first = lax.rem(of_step, STEPS) * tiles

        def send(slots, out):
            def one(index, carry):
                tile = lax.div(index, 8)
                block = lax.rem(index, 8)
                down_row = pl.multiple_of(slots[128 + (first + tile) * 8 + block] * BLK, BLK)
                up_row = pl.multiple_of(slots[64 + block * 8 + first + tile] * BLK, BLK)
                tile_row = pl.multiple_of(tile * BLK, BLK)
                block_row = pl.multiple_of(block * BLK, BLK)
                pltpu.make_async_copy(
                    down_buf.at[part, pl.ds(tile_row, BLK), pl.ds(block_row, BLK)],
                    out.at[pl.ds(down_row, BLK), :],
                    sems.at[part],
                ).start()
                pltpu.make_async_copy(
                    up_buf.at[part, pl.ds(block_row, BLK), pl.ds(tile_row, BLK)],
                    out.at[pl.ds(up_row, BLK), :],
                    sems.at[part],
                ).start()
                return carry

            lax.fori_loop(0, tiles * 8, one, 0)

        pl.when(of_step < STEPS)(lambda: send(slot_own, own_ref))
        pl.when(of_step >= STEPS)(lambda: send(slot_par, par_ref))

    def wait(of_step):
        part = lax.rem(of_step, 2)
        for buf in (down_buf, up_buf):
            pltpu.make_async_copy(buf.at[part], buf.at[part], sems.at[part]).wait()

    @pl.when(step >= 2)
    def _():
        wait(step - 2)

    down_buf[at] = sum(dot_tn(a[...], g[...]) for a, g in zip(acts, gds)).astype(BF)
    up_buf[at] = sum(dot_tn(n[...], g[...]) for n, g in zip(n2s, gus)).astype(BF)
    start(step)

    @pl.when(step == 2 * STEPS - 1)
    def _():
        wait(step - 1)
        wait(step)


def call_mlp_grads(slots, acts, gds, n2s, gus):
    rows = gds[0].shape[0]
    wide = STEP_HID // 2
    by_hidden = pl.BlockSpec((rows, wide), lambda s, a, b: (0, s))
    whole = pl.BlockSpec((rows, D), lambda s, a, b: (0, 0))
    buffer = jax.ShapeDtypeStruct((SHARE_TILES * BLK, BLK), BF)
    return pl.pallas_call(
        mlp_grads,
        grid_spec=pltpu.PrefetchScalarGridSpec(
            num_scalar_prefetch=2,
            grid=(2 * STEPS,),
            in_specs=[by_hidden] * 2 + [whole] * 4 + [by_hidden] * 2,
            out_specs=[ANY, ANY],
            scratch_shapes=[
                pltpu.VMEM((2, wide, D), BF),
                pltpu.VMEM((2, D, wide), BF),
                pltpu.SemaphoreType.DMA((2,)),
            ],
        ),
        out_shape=[buffer, buffer],
        compiler_params=params(),
        cost_estimate=cost(2 * 2 * rows * D * 2 * HID * 2, 16 << 20),
        name="mlp_grads",
    )(*slots, *acts, *gds, *n2s, *gus)


def attention_grads(slot_own, slot_par, *refs):
    atts, gbs, n1s, gqs, gks, gvs = (refs[2 * i : 2 * i + 2] for i in range(6))
    own_ref, par_ref, out_buf, qkv_buf, sems = refs[14:]
    step = at = pl.program_id(0)
    per_share = D // NARROW // BLK

    def start(of_step):
        part = of_step

        def send(slots, out):
            def one(block, carry):
                block_row = pl.multiple_of(block * BLK, BLK)
                for column in range(per_share):
                    cols = pl.ds(column * BLK, BLK)
                    row = pl.multiple_of(slots[48 + column * 8 + block] * BLK, BLK)
                    pltpu.make_async_copy(
                        out_buf.at[part, cols, pl.ds(block_row, BLK)],
                        out.at[pl.ds(row, BLK), :],
                        sems.at[part],
                    ).start()
                    for third in range(3):
                        tile = block * 6 + third * 2 + column
                        row = pl.multiple_of(slots[tile] * BLK, BLK)
                        pltpu.make_async_copy(
                            qkv_buf.at[part, third, pl.ds(block_row, BLK), cols],
                            out.at[pl.ds(row, BLK), :],
                            sems.at[part],
                        ).start()
                return carry

            lax.fori_loop(0, 8, one, 0)

        pl.when(of_step == 0)(lambda: send(slot_own, own_ref))
        pl.when(of_step == 1)(lambda: send(slot_par, par_ref))

    def wait(part):
        for buf in (out_buf, qkv_buf):
            pltpu.make_async_copy(buf.at[part], buf.at[part], sems.at[part]).wait()

    out_buf[at] = sum(dot_tn(a[...], g[...]) for a, g in zip(atts, gbs)).astype(BF)
    for third, grads in enumerate((gqs, gks, gvs)):
        qkv_buf[at, third] = sum(dot_tn(n[...], g[...]) for n, g in zip(n1s, grads)).astype(BF)
    start(step)

    @pl.when(step == 1)
    def _():
        wait(0)
        wait(1)


def call_attention_grads(slots, atts, gbs, n1s, gps, own, par):
    rows = gbs[0].shape[0]
    width = WID // 2
    whole = pl.BlockSpec((rows, D), lambda s, a, b: (0, 0))

    def by_column(third):
        return pl.BlockSpec((rows, width), lambda s, a, b: (0, third * 2 + s))

    return pl.pallas_call(
        attention_grads,
        grid_spec=pltpu.PrefetchScalarGridSpec(
            num_scalar_prefetch=2,
            grid=(2,),
            in_specs=[by_column(0)] * 2
            + [whole] * 4
            + [by_column(0)] * 2
            + [by_column(1)] * 2
            + [by_column(2)] * 2
            + [ANY, ANY],
            out_specs=[ANY, ANY],
            scratch_shapes=[
                pltpu.VMEM((2, width, D), BF),
                pltpu.VMEM((2, 3, D, width), BF),
                pltpu.SemaphoreType.DMA((2,)),
            ],
        ),
        out_shape=[jax.ShapeDtypeStruct(own.shape, BF)] * 2,
        input_output_aliases={14: 0, 15: 1},
        compiler_params=params(),
        cost_estimate=cost(2 * 2 * rows * D * 4 * WID, 8 << 20),
        name="attention_grads",
    )(*slots, *atts, *gbs, *n1s, *gps, *gps, *gps, own, par)


def place_of(tile, share):
    quarter = WID // 2
    block, rest = tile // 6, tile % 6
    third, column = rest // 2, rest % 2
    qkv_row = jnp.where(third == 2, D, 0) + block * BLK
    qkv_col = jnp.where(third == 1, WID, 0) + share * quarter + column * BLK
    out = tile - 48
    out_block, out_col = out // 8, out % 8
    out_row = D + jnp.where(out_col >= 4, WID, 0) + share * quarter + out_block * BLK
    out_col = WID + (out_col % 4) * BLK
    up = tile - 64
    up_row, up_col = 2 * D + share * D + (up // 8) * BLK, (up % 8) * BLK
    down = tile - 128
    down_row, down_col = 4 * D + share * D + (down // 8) * BLK, (down % 8) * BLK
    kind = (tile >= 48).astype(jnp.int32) + (tile >= 64) + (tile >= 128)
    row = jnp.select([kind == 0, kind == 1, kind == 2], [qkv_row, out_row, up_row], down_row)
    col = jnp.select([kind == 0, kind == 1, kind == 2], [qkv_col, out_col, up_col], down_col)
    return row, col


def assemble_kernel(plan, rows, cols, *refs):
    sources = refs[: len(plan)]
    out_ref, sem = refs[-2:]
    for source, (share, first, count) in zip(sources, plan):

        def one(i, carry, source=source, share=share, first=first):
            row = pl.multiple_of(rows[share, first + i], BLK)
            col = pl.multiple_of(cols[share, first + i], BLK)
            pltpu.make_async_copy(
                source.at[pl.ds(pl.multiple_of(i * BLK, BLK), BLK), :],
                out_ref.at[pl.ds(row, BLK), pl.ds(col, BLK)],
                sem,
            ).start()
            return carry

        lax.fori_loop(0, count, one, 0, unroll=4 if count % 4 == 0 else 1)
    for source, (_, _, count) in zip(sources, plan):
        tiles = source.at[pl.ds(0, count * BLK), :]
        pltpu.make_async_copy(tiles, tiles, sem).wait()


def assemble(table, pieces):
    plan = [piece[:3] for piece in pieces]
    args = list(table) + [piece[3] for piece in pieces]
    return pl.pallas_call(
        functools.partial(assemble_kernel, plan),
        out_shape=jax.ShapeDtypeStruct((6 * D, D), BF),
        in_specs=[SMEM, SMEM] + [ANY] * len(pieces),
        out_specs=ANY,
        scratch_shapes=[pltpu.SemaphoreType.DMA],
        compiler_params=params(),
        cost_estimate=cost(0, BLK),
        name="assemble",
    )(*args)


def ring(size):
    order = list(range(0, size, 2)) + list(range(size - 1, 0, -2))
    ahead = [(order[i], order[(i + 1) % size]) for i in range(size)]
    position = [order.index(i) for i in range(size)]
    return order, position, ahead, [(b, a) for a, b in ahead]


def after(value, *earlier):
    return lax.optimization_barrier((value, *earlier))[0]


def need_order(size):
    far = size // 2
    order = [far]
    for step in range(far - 1, 0, -1):
        order += [step, size - step]
    return order + [0]


class Gather:
    def __init__(self, unit, size, per_device):
        _, _, self.ahead, self.behind = ring(size)
        self.size, self.per_device, self.step_count = size, per_device, 0
        self.up = self.down = unit

    def step(self, *earlier):
        self.step_count += 1
        step, far, front = self.step_count, self.size // 2, self.per_device // 2
        up, down = self.up, self.down
        if step == far:
            up, down = up[: front * BLK], down[front * BLK :]
        up, down, *_ = lax.optimization_barrier((up, down, *earlier))
        self.sent = (up, down)
        self.up = lax.ppermute(up, "wide", self.ahead)
        self.down = lax.ppermute(down, "wide", self.behind)
        if step < far:
            return [
                (self.size - step, 0, self.per_device, self.up),
                (step, 0, self.per_device, self.down),
            ]
        return [
            (far, 0, front, self.up),
            (far, front, self.per_device - front, self.down),
        ]


class Scatter:
    def __init__(self, unit_of, size, cut):
        _, _, self.ahead, self.behind = ring(size)
        self.unit_of, self.size, self.cut, self.left = unit_of, size, cut, size // 2

    def step(self, *earlier):
        cut = self.cut
        if self.left == self.size // 2:
            last = self.unit_of(self.left)
            up, down = last[:cut], last[cut:]
        else:
            up, down = self.unit_of(self.left), self.unit_of(self.size - self.left)
            got_up, got_down = self.up.astype(F32), self.down.astype(F32)
            if self.left == self.size // 2 - 1:
                up = jnp.concatenate([up[:cut] + got_up, up[cut:]])
                down = jnp.concatenate([down[:cut], down[cut:] + got_down])
            else:
                up, down = up + got_up, down + got_down
        up, down = up.astype(BF), down.astype(BF)
        up, down, *_ = lax.optimization_barrier((up, down, *earlier))
        self.sent = (up, down)
        self.up = lax.ppermute(up, "wide", self.ahead)
        self.down = lax.ppermute(down, "wide", self.behind)
        self.left -= 1

    def result(self):
        return self.unit_of(0) + self.up.astype(F32) + self.down.astype(F32)


def mesh_bits():
    out, base = [], 1
    for axis in ("narrow", "wide"):
        size, bit = lax.axis_size(axis), 1
        while bit < size:
            out.append((base * bit, axis, [(i, i ^ bit) for i in range(size)]))
            bit *= 2
        base *= size
    return out


def tile_ids(share):
    tile_rows = D // BLK
    shard_cols = D // (NARROW * BLK)
    shard_hidden = FF // (NARROW * BLK)
    count_qkv = tile_rows * 3 * tile_rows
    start_up = count_qkv + tile_rows * tile_rows
    start_down = start_up + tile_rows * (FF // BLK)
    row_part = jnp.arange(tile_rows)[:, None, None]
    third = jnp.arange(3)[None, :, None]
    column_part = jnp.arange(shard_cols)[None, None, :]
    qkv_ids = (
        row_part * 3 * tile_rows + third * tile_rows + share * shard_cols + column_part
    ).reshape(-1)
    out_ids = (
        count_qkv
        + (share * shard_cols + jnp.arange(shard_cols)[:, None]) * tile_rows
        + jnp.arange(tile_rows)[None, :]
    ).reshape(-1)
    up_ids = (
        start_up
        + jnp.arange(tile_rows)[:, None] * (FF // BLK)
        + share * shard_hidden
        + jnp.arange(shard_hidden)[None, :]
    ).reshape(-1)
    down_ids = (
        start_down
        + (share * shard_hidden + jnp.arange(shard_hidden)[:, None]) * tile_rows
        + jnp.arange(tile_rows)[None, :]
    ).reshape(-1)
    return jnp.concatenate([qkv_ids, out_ids, up_ids, down_ids])


def share_vectors(small_all, me):
    pieces = [small_all[i * D : (i + 1) * D] for i in range(8)]
    bias_up = small_all[8 * D :]

    def both(vector, width):
        own = lax.dynamic_slice_in_dim(vector, me * width, width)
        par = lax.dynamic_slice_in_dim(vector, (me ^ 1) * width, width)
        return jnp.concatenate([own, par])

    quarter = D // NARROW
    heads = jnp.concatenate([both(pieces[2], quarter), both(pieces[3], quarter)])
    rows = [pieces[0], pieces[1], heads, pieces[4], pieces[5], pieces[6], pieces[7]]
    up = both(bias_up, FF // NARROW)
    rows = rows + [up[0:D], up[D:]]
    return jnp.pad(jnp.stack(rows), ((0, 7), (0, 0)))


def small_vector(mlp_sums, att_sums, me):
    half = me // 2
    mine = [(half == t).astype(F32) for t in range(2)]
    mlp = mlp_sums[0] + mlp_sums[1]
    att = att_sums[0] + att_sums[1]
    bias_down = mine[0] * mlp_sums[0][2] + mine[1] * mlp_sums[1][2]
    bias_out = mine[0] * att_sums[0][3] + mine[1] * att_sums[1][3]
    odd = (me % 2) == 1

    def spread(own, par):
        placed = jnp.where(odd, jnp.concatenate([par, own]), jnp.concatenate([own, par]))
        return [jnp.where(half == 0, placed, 0.0), jnp.where(half == 1, placed, 0.0)]

    quarter = D // NARROW
    heads = att[2]
    return jnp.concatenate(
        [att[0], att[1]]
        + spread(heads[0:quarter], heads[quarter : 2 * quarter])
        + spread(heads[2 * quarter : 3 * quarter], heads[3 * quarter :])
        + [bias_out, mlp[0], mlp[1], bias_down]
        + spread(mlp[3], mlp[4])
    )


def total_over_mesh(value):
    value = jnp.broadcast_to(value.reshape(1, 1), (8, BLK))
    for _, axis, perm in mesh_bits():
        value = value + lax.ppermute(value, axis, perm)
    return value[0, 0]


def update_kernel(clip_ref, grad0, grad1, left, right, first, second, master, *outs):
    new_first, new_second, new_master, new_weights = outs
    step = pl.program_id(0)
    half = pl.num_programs(0) // 2
    clip = clip_ref[0]
    grads = (grad0, grad1)
    count = left.shape[1]
    for base in range(0, count, 4):
        blocks = range(base, min(base + 4, count))
        lefts = [left[0, b].astype(BF) for b in blocks]
        rights = [right[0, b].astype(BF) for b in blocks]
        terms = [
            jnp.where(step < half, *(g[b * BLK : (b + 1) * BLK, :] for g in grads)).astype(BF)
            for b in blocks
        ]
        terms = [dot_tn(a, x).astype(BF) for a, x in zip(lefts, terms)]
        terms = [clip * dot(x, b) for x, b in zip(terms, rights)]
        ones = [0.5 * first[0, b] + 0.5 * x for b, x in zip(blocks, terms)]
        twos = [0.5 * second[0, b] + 0.5 * x * x for b, x in zip(blocks, terms)]
        terms = [(a / (jnp.sqrt(b) + 1e-08)).astype(BF) for a, b in zip(ones, twos)]
        terms = [dot(a, x).astype(BF) for a, x in zip(lefts, terms)]
        terms = [dot_nt(x, b) for x, b in zip(terms, rights)]
        for b, one, two, turned in zip(blocks, ones, twos, terms):
            new_first[0, b] = one
            new_second[0, b] = two
            weights = master[0, b] - 0.02 * turned
            new_master[0, b] = weights
            new_weights[0, b] = weights.astype(BF)


def update(clip, grads, left, right, first, second, master):
    count = left.shape[1]
    group = 8 if count % 8 == 0 else 1
    steps = count // group
    spec = pl.BlockSpec((1, group, BLK, BLK), lambda i: (i // steps, i % steps, 0, 0))
    low = pl.BlockSpec((group * BLK, BLK), lambda i: (jnp.minimum(i, steps - 1), 0))
    high = pl.BlockSpec((group * BLK, BLK), lambda i: (jnp.maximum(i - steps, 0), 0))
    shape = jax.ShapeDtypeStruct(master.shape, F32)
    return pl.pallas_call(
        update_kernel,
        grid=(2 * steps,),
        out_shape=[shape, shape, shape, jax.ShapeDtypeStruct(master.shape, BF)],
        in_specs=[SMEM, low, high] + [spec] * 5,
        out_specs=[spec] * 4,
        compiler_params=params(56),
        cost_estimate=cost(count * 16 * BLK**3, count * BLK * BLK * 2 * 38),
        name="update",
    )(clip, *grads, left, right, first, second, master)


def shards(
    images,
    cotangent,
    kept_tokens,
    owner_slots,
    master_blocks,
    small_params,
    left_basis,
    right_basis,
    first_moment,
    second_moment,
    small_first,
    small_second,
):
    me = lax.axis_index("narrow")
    half, core = me // 2, me % 2
    wide = lax.axis_size("wide")
    per_device = master_blocks.shape[1]
    own_small = small_params.shape[1]
    own_images = images.shape[0]
    rows = own_images * S

    device = lax.axis_index("wide") * NARROW + me
    by_distance = jnp.arange(wide * NARROW) ^ device

    def chunks(own):
        other = lax.ppermute(own, "narrow", ACROSS)
        return [jnp.where(half == t, own, other) for t in range(2)]

    kept = [
        lax.dynamic_slice_in_dim(kept_tokens, (2 * t + core) * own_images, own_images, 0)
        .T.reshape(1, rows)
        .astype(F32)
        for t in range(2)
    ]

    order, position, _, _ = ring(wide)
    place = jnp.take(jnp.asarray(position, jnp.int32), lax.axis_index("wide"))
    around = jnp.take(jnp.asarray(order, jnp.int32), (place + jnp.arange(wide)) % wide)

    needed = need_order(wide)
    turns = [needed.index(distance) for distance in range(wide)]
    slots, tables = [], []
    for layer in range(LAYERS):
        owners = owner_slots[layer]
        layer_slots, layer_rows, layer_cols = [], [], []
        for at, share in enumerate((me, me ^ 1)):
            slot = jnp.take(owners, tile_ids(share))
            at_wide, at_pos = slot // per_device // NARROW, slot % per_device
            distance = (jnp.take(jnp.asarray(position, jnp.int32), at_wide) - place) % wide
            relative = distance * per_device + at_pos
            turn = jnp.take(jnp.asarray(turns, jnp.int32), distance)
            layer_slots.append(turn * per_device + at_pos)
            here = relative[None, :] == jnp.arange(SHARE_TILES)[:, None]
            tile = jnp.sum(jnp.where(here, jnp.arange(SHARE_TILES)[None, :], 0), axis=1)
            row, col = place_of(tile, at)
            layer_rows.append(row)
            layer_cols.append(col)
        slots.append(layer_slots)
        tables.append((jnp.stack(layer_rows), jnp.stack(layer_cols)))

    def by_token(value):
        return value.transpose(1, 0, 2).reshape(rows, D)

    def by_image(value):
        return value.reshape(S, own_images, D).transpose(1, 0, 2)

    def core_swap(value):
        return lax.ppermute(value, "narrow", CORE)

    def exchange(part):
        return lax.ppermute(part, "narrow", ACROSS)

    units = [
        master_blocks[layer].astype(BF).reshape(per_device * BLK, BLK) for layer in range(LAYERS)
    ]

    def swapped(pieces):
        return [piece + (core_swap(piece[3]),) for piece in pieces]

    def place_pieces(layer, pieces):
        group = [
            (share, distance * per_device + first, count, pair[share])
            for distance, first, count, *pair in pieces
            for share in range(2)
        ]
        return assemble(tables[layer], group)

    steps = wide // 2
    own_small_rows = small_params.astype(BF).reshape(1, -1)
    small_rows = own_small_rows
    bits = mesh_bits()
    near_bits, far_bits = bits[:2], bits[2:]
    per_window = -(-len(far_bits) // max(steps - 1, 1))

    def grow(rows, some_bits):
        for _, axis, perm in some_bits:
            rows = jnp.concatenate([rows, lax.ppermute(rows, axis, perm)])
        return rows

    gather = Gather(units[0], wide, per_device)
    arrived = [(0, 0, per_device, units[0])] + gather.step()
    small_rows = grow(small_rows, near_bits)
    inputs = [by_token(images), by_token(cotangent)]
    placed, extra = [], [small_rows]
    brought = []
    for step in range(2, steps + 1):
        latest = swapped(arrived)
        arrived = gather.step(*extra)
        placed += latest
        extra = [piece[4] for piece in latest]
        if step == 2:
            brought = chunks(after(inputs[0], *gather.sent))
            extra += brought
        elif step == 3:
            late = exchange(after(inputs[1], *gather.sent))
        at = (step - 2) * per_window
        small_rows = grow(small_rows, far_bits[at : at + per_window])
        if step < steps:
            extra.append(small_rows)
    hidden_in = brought
    next_unit = after(units[1], gather.up, gather.down, late)
    gather_next = Gather(next_unit, wide, per_device)
    arrived_next = [(0, 0, per_device, next_unit)] + gather_next.step()
    last = [piece[:3] + (after(piece[3], *gather_next.sent),) for piece in arrived]
    weights = [place_pieces(0, placed + swapped(last))]
    cot = [jnp.where(half == t, inputs[1], late) for t in range(2)]

    in_order = jnp.take(small_rows, by_distance, axis=0).astype(F32)
    small_all = in_order.reshape(-1, LAYERS, own_small).transpose(1, 0, 2).reshape(LAYERS, -1)
    vecs = [share_vectors(small_all[layer], me) for layer in range(LAYERS)]

    saved = []
    state = None
    for layer in range(LAYERS):
        kept_layer = []
        for t in range(2):
            if layer == 0:
                hidden = hidden_in[t]
                if t == 1:
                    placed = swapped(arrived_next)
                    arrived_next = gather_next.step(part)
                    hidden = after(hidden, *gather_next.sent)
                *out, weights[layer] = call_attention_forward(
                    True, (hidden,), vecs[0], kept[t], weights[layer]
                )
            else:
                hidden, *out, weights[layer] = call_attention_forward(
                    False, state[t] + (vecs[layer - 1],), vecs[layer], kept[t], weights[layer]
                )
            n1, qkv, lse, att, part = out
            kept_layer.append([hidden, n1, qkv, lse, att, part, exchange(part)])
        kept_layer[0][5] = after(kept_layer[0][5], kept_layer[1][5])
        state = []
        for t in range(2):
            hidden, n1, qkv, lse, att, part, got = kept_layer[t]
            if layer == 0 and t == 1:
                placed += swapped(arrived_next)
                arrived_next = gather_next.step(down_part)
                part = after(part, *gather_next.sent, *vecs[1:])
            middle, n2, act, slope, down_part, weights[layer] = call_mlp_forward(
                hidden, part, got, vecs[layer], weights[layer]
            )
            kept_layer[t] = (hidden, n1, qkv, lse, att, middle, n2, act, slope)
            if layer < LAYERS - 1:
                state.append((middle, down_part, exchange(down_part)))
            else:
                state.append((middle, down_part))
        saved.append(kept_layer)
        if layer == 0:
            gates = [down_part]
            for step in range(4, steps + 1):
                latest = swapped(arrived_next)
                arrived_next = gather_next.step(*gates)
                placed += latest
                gates = [piece[4] for piece in latest]
            weights.append(place_pieces(1, placed + swapped(arrived_next)))

    def mine(pair):
        return jnp.where(half == 0, pair[0], pair[1])

    def theirs(pair):
        return jnp.where(half == 0, pair[1], pair[0])

    down_parts = [state[t][1] for t in range(2)]
    middles = [state[t][0] for t in range(2)]
    upstream = None
    reduced = [None] * LAYERS
    small_terms = [None] * LAYERS
    pending = None
    for layer in reversed(range(LAYERS)):
        kept_layer = saved[layer]
        top = layer == LAYERS - 1
        work = []
        for t in range(2):
            hidden, n1, qkv, lse, att, middle, n2, act, slope = kept_layer[t]
            if top:
                grad = cot[t]
                gd, gu, part, sums, weights[layer] = call_mlp_backward(
                    True, (grad,), middle, slope, vecs[layer], weights[layer]
                )
            else:
                state = upstream[t]
                state = (after(state[0], *pending.sent),) + state[1:]
                grad, gd, gu, part, sums, weights[layer] = call_mlp_backward(
                    False, state + (vecs[layer + 1],), middle, slope, vecs[layer], weights[layer]
                )
                if t == 0:
                    pending.step(part)
            work.append([grad, gd, gu, part, sums, exchange(part)])
        gds = [w[1] for w in work]
        if pending is not None:
            gds[0] = after(gds[0], *pending.sent)
        own, par = call_mlp_grads(
            slots[layer],
            [k[7] for k in kept_layer],
            gds,
            [k[6] for k in kept_layer],
            [w[2] for w in work],
        )
        if pending is not None:
            pending.step(own)
        back = []
        for t in range(2):
            hidden, n1, qkv, lse, att, middle, n2, act, slope = kept_layer[t]
            grad, gd, gu, part, sums, got = work[t]
            if pending is not None:
                part = after(part, *pending.sent)
            gm, gb, gp, att_part, att_sums, weights[layer] = call_attention_backward(
                grad, part, got, middle, hidden, qkv, lse, vecs[layer], kept[t], weights[layer]
            )
            back.append((gm, gb, gp, att_part, att_sums))
        if pending is not None:
            pending.step(back[1][3])
            while pending.left > 0:
                pending.step()
            own = after(own, *pending.sent)
        if layer > 0:
            got = [exchange(back[t][3]) for t in range(2)]
            own = after(own, got[0])
            upstream = [
                (after(back[0][0], got[1]), back[0][3], got[0], kept_layer[0][0]),
                (back[1][0], back[1][3], got[1], kept_layer[1][0]),
            ]
        own, par = call_attention_grads(
            slots[layer],
            [k[4] for k in kept_layer],
            [b[1] for b in back],
            [k[1] for k in kept_layer],
            [b[2] for b in back],
            own,
            par,
        )
        terms = small_vector([w[4] for w in work], [b[4] for b in back], me)
        small_terms[layer] = terms.reshape(-1, own_small)
        unit_len = per_device * BLK

        first_got = core_swap(par[:unit_len])
        earlier = pending
        pending = Scatter(None, wide, (per_device // 2) * BLK)

        def first_unit(distance, own=own, got=first_got, unit_len=unit_len):
            return own[:unit_len].astype(F32) + got.astype(F32)

        pending.unit_of = first_unit
        pending.step()
        rest = core_swap(after(par, *pending.sent))
        if earlier is not None:
            earlier.up = after(earlier.up, *pending.sent)
            reduced[layer + 1] = earlier.result()

        def unit_of(distance, own=own, rest=rest, unit_len=unit_len):
            at = turns[distance] * unit_len
            return own[at : at + unit_len].astype(F32) + rest[at : at + unit_len].astype(F32)

        pending.unit_of = unit_of

    final = mine(middles) + (
        mine(down_parts).astype(F32)
        + exchange(after(theirs(down_parts), rest)).astype(F32)
        + vecs[LAYERS - 1][6]
    )
    block_output = by_image(final.astype(BF))
    parts = [b[3] for b in back]
    last_part = exchange(after(theirs(parts), rest)).astype(F32)
    small_rows = jnp.take(jnp.concatenate(small_terms, axis=1), by_distance, axis=0)
    small_rows = after(small_rows, rest)
    backward_bits = mesh_bits()[::-1]
    local_sum = input_grad = None
    while pending.left > 0:
        for bit, axis, perm in backward_bits[:per_window]:
            small_rows = small_rows[:bit] + lax.ppermute(small_rows[bit:], axis, perm)
        backward_bits = backward_bits[per_window:]
        pending.step(small_rows)
        early = list(pending.sent)
        if local_sum is None:
            upper = [after(grads, *pending.sent) for grads in reduced[1:]]
            local_sum = sum(jnp.sum(grads * grads) for grads in upper)
            early.append(local_sum)
        elif input_grad is None:
            hidden = mine([k[0] for k in saved[0]]).astype(F32)
            centre, rstd = stats(hidden)
            lower = norm_back(
                mine(parts).astype(F32) + after(last_part, *pending.sent),
                centre * rstd,
                rstd,
                vecs[0][0:1],
            )
            input_grad = by_image(mine([b[0] for b in back]) + lower)
            early += [input_grad, block_output]
        small_rows = after(small_rows, *early)
    for bit, axis, perm in backward_bits:
        small_rows = small_rows[:bit] + lax.ppermute(small_rows[bit:], axis, perm)
    reduced[0] = pending.result()
    grad_small = small_rows.reshape(LAYERS, own_small)
    local_sum = local_sum + jnp.sum(grad_small * grad_small) + jnp.sum(reduced[0] * reduced[0])
    grad_norm = jnp.sqrt(total_over_mesh(local_sum))
    clip_factor = 1.0 / jnp.maximum(grad_norm, 1.0)
    new_first, new_second, new_master, new_weights = update(
        clip_factor.reshape(1),
        reduced,
        left_basis,
        right_basis,
        first_moment,
        second_moment,
        master_blocks,
    )
    clipped_small = clip_factor * grad_small
    new_small_first = 0.5 * small_first + 0.5 * clipped_small
    new_small_second = 0.5 * small_second + 0.5 * clipped_small * clipped_small
    new_small = small_params - 0.3 * new_small_first / (jnp.sqrt(new_small_second) + 1e-08)
    return (
        block_output,
        input_grad,
        grad_norm.reshape(1),
        new_first,
        new_second,
        new_master,
        new_weights,
        new_small_first,
        new_small_second,
        new_small,
        new_small.astype(BF),
    )


def solution(mesh):
    both = ("wide", "narrow")
    rows = P(both, None, None)
    blocks = P(None, both, None, None)
    small = P(None, both)
    in_specs = (
        rows,
        rows,
        P("wide", None),
        P(),
        blocks,
        small,
        blocks,
        blocks,
        blocks,
        blocks,
        small,
        small,
    )
    out_specs = (rows, rows, P(), blocks, blocks, blocks, blocks, small, small, small, small)
    return jax.shard_map(shards, mesh=mesh, in_specs=in_specs, out_specs=out_specs, check_vma=False)
```

```python
import functools

import jax
import jax.numpy as jnp
from jax import lax
from jax.experimental import pallas as pl
from jax.experimental.pallas import tpu as pltpu
from jax.sharding import PartitionSpec as P

D = 1024
HEAD_DIM = 64
FF = 4096
S = 50
LAYERS = 2
BLK = 128
NARROW = 4

BF = jnp.bfloat16
F32 = jnp.float32

WID = D // 2
HID = FF // 2
SHARE_TILES = 192
ATT_ROWS = 2 * D
MLP_ROWS = 4 * D

CORE = [(j, j ^ 1) for j in range(NARROW)]
ACROSS = [(j, j ^ 2) for j in range(NARROW)]
ANY = pl.BlockSpec(memory_space=pl.ANY)
SMEM = pl.BlockSpec(memory_space=pltpu.SMEM)
VMEM = pl.BlockSpec(memory_space=pltpu.VMEM)


def params(mib=16):
    return pltpu.CompilerParams(vmem_limit_bytes=mib << 20)


def cost(flops, nbytes):
    return pl.CostEstimate(flops=flops, bytes_accessed=nbytes, transcendentals=0)


def output(in_hbm, *shape, dtype=BF):
    return (pltpu.HBM if in_hbm else jax.ShapeDtypeStruct)(shape, dtype)


def dot(a, b):
    return jnp.dot(a, b, preferred_element_type=F32)


def dot_nt(a, b):
    return lax.dot_general(a, b, (((1,), (1,)), ((), ())), preferred_element_type=F32)


def dot_tn(a, b):
    return lax.dot_general(a, b, (((0,), (0,)), ((), ())), preferred_element_type=F32)


def stats(x):
    centre = x - jnp.mean(x, axis=-1, keepdims=True)
    spread = jnp.mean(centre * centre, axis=-1, keepdims=True)
    return centre, lax.rsqrt(spread + 1e-06)


def norm_back(grad, xhat, rstd, gain):
    gn = grad * gain
    return rstd * (
        gn
        - jnp.mean(gn, axis=-1, keepdims=True)
        - xhat * jnp.mean(gn * xhat, axis=-1, keepdims=True)
    )


def key_bias(kept_row, rows):
    def image_of(dim):
        return lax.rem(lax.broadcasted_iota(jnp.int32, (rows, rows), dim), rows // S)

    allowed = (image_of(0) == image_of(1)) & (kept_row > 0.0)
    return jnp.where(allowed, 0.0, -1e30)


def lane_half(x, half):
    lane = lax.broadcasted_iota(jnp.int32, x.shape, 1)
    keep = (lane < HEAD_DIM) if half == 0 else (lane >= HEAD_DIM)
    return jnp.where(keep, x, jnp.zeros_like(x))


def attention_forward(first, *refs):
    if first:
        x_ref, vecs, kept, weights, n1_ref, qkv_ref, lse_ref, att_ref, part_ref, _ = refs
        hidden = x_ref[...].astype(F32)
    else:
        (mid_ref, own_ref, got_ref, prev, vecs, kept, weights) = refs[:7]
        hidden_ref, n1_ref, qkv_ref, lse_ref, att_ref, part_ref, _ = refs[7:]
        hidden = mid_ref[...] + (
            own_ref[...].astype(F32) + got_ref[...].astype(F32) + prev[6:7, :]
        )
        hidden_ref[...] = hidden
    rows = hidden.shape[0]
    centre, rstd = stats(hidden)
    n1 = (centre * rstd * vecs[0:1, :] + vecs[1:2, :]).astype(BF)
    n1_ref[...] = n1
    qkv_ref[:, 0:WID] = (dot(n1, weights[0:D, 0:WID]) + vecs[2:3, 0:WID]).astype(BF)
    qkv_ref[:, WID : 2 * WID] = dot(n1, weights[0:D, WID:D]).astype(BF)
    qkv_ref[:, 2 * WID :] = (dot(n1, weights[D : 2 * D, 0:WID]) + vecs[2:3, WID:D]).astype(BF)
    bias = key_bias(kept[0:1, :], rows)
    lane = lax.broadcasted_iota(jnp.int32, (rows, BLK), 1)
    lse_all = jnp.zeros((rows, BLK), F32)
    for pair in range(WID // BLK):
        cols = slice(pair * BLK, (pair + 1) * BLK)
        q = qkv_ref[:, cols] * jnp.asarray(0.125, BF)
        k = qkv_ref[:, WID + pair * BLK : WID + (pair + 1) * BLK]
        v = qkv_ref[:, 2 * WID + pair * BLK : 2 * WID + (pair + 1) * BLK]
        outs = []
        for half in range(2):
            scores = dot_nt(lane_half(q, half), k) + bias
            top = jnp.max(scores, axis=-1, keepdims=True)
            raised = jnp.exp(scores - top)
            total = jnp.sum(raised, axis=-1, keepdims=True)
            outs.append(dot((raised * (1.0 / total)).astype(BF), v))
            lse_all = jnp.where(lane == 2 * pair + half, top + jnp.log(total), lse_all)
        att_ref[:, cols] = jnp.where(lane < HEAD_DIM, outs[0], outs[1]).astype(BF)
    lse_ref[...] = lse_all
    att = att_ref[...]
    part_ref[:, 0:WID] = dot(att, weights[D : D + WID, WID:D]).astype(BF)
    part_ref[:, WID:D] = dot(att, weights[D + WID : 2 * D, WID:D]).astype(BF)


def call_attention_forward(first, operands, vecs, kept, weights):
    rows = operands[0].shape[0]
    outs = [
        output(first, rows, D),
        output(first, rows, 3 * WID),
        output(first, rows, BLK, dtype=F32),
        output(first, rows, WID),
        jax.ShapeDtypeStruct((rows, D), BF),
    ]
    if not first:
        outs = [jax.ShapeDtypeStruct((rows, D), F32)] + outs
    args = list(operands) + [vecs, kept, weights]
    return pl.pallas_call(
        functools.partial(attention_forward, first),
        out_shape=outs + [jax.ShapeDtypeStruct(weights.shape, BF)],
        grid=(1,),
        in_specs=[full(*a.shape) for a in args[:-1]] + [VMEM],
        out_specs=[full(*o.shape) for o in outs] + [VMEM],
        input_output_aliases={len(args) - 1: len(outs)},
        compiler_params=params(),
        cost_estimate=cost(2 * rows * D * 4 * WID * 2, 6 << 20),
        name="attention_forward",
    )(*args)


STEPS = 4
STEP_HID = HID // STEPS


def mlp_forward(hid_ref, own_ref, got_ref, vecs, weights, *rest):
    mid_ref, n2_ref, act_ref, slope_ref, part_ref, _, total = rest
    step = pl.program_id(0)

    @pl.when(step == 0)
    def _():
        middle = hid_ref[...].astype(F32) + (
            own_ref[...].astype(F32) + got_ref[...].astype(F32) + vecs[3:4, :]
        )
        mid_ref[...] = middle
        centre, rstd = stats(middle)
        n2_ref[...] = (centre * rstd * vecs[4:5, :] + vecs[5:6, :]).astype(BF)

    row = 7 + step // 2
    bias = jnp.where(
        step % 2 == 0, vecs[pl.ds(row, 1), 0:STEP_HID], vecs[pl.ds(row, 1), STEP_HID:D]
    )
    upward = dot(n2_ref[...], up_part(weights, step)) + bias
    cdf = 0.5 + 0.5 * lax.erf(upward * 0.7071067811865476)
    act = (upward * cdf).astype(BF)
    act_ref[...] = act
    slope_ref[...] = (
        cdf + upward * (jnp.exp(-0.5 * upward * upward) * 0.3989422804014327)
    ).astype(BF)
    term = dot(act, down_part(weights, step))

    @pl.when(step == 0)
    def _():
        total[...] = term

    @pl.when((step > 0) & (step < STEPS - 1))
    def _():
        total[...] += term

    @pl.when(step == STEPS - 1)
    def _():
        part_ref[...] = (total[...] + term).astype(BF)


def full(rows, cols):
    return pl.BlockSpec((rows, cols), lambda s: (0, 0))


def up_part(weights, step):
    rows = pl.ds(pl.multiple_of(2 * D + step // 2 * D, D), D)
    return weights[rows, pl.ds(pl.multiple_of(step % 2 * STEP_HID, STEP_HID), STEP_HID)]


def down_part(weights, step):
    return weights[pl.ds(pl.multiple_of(4 * D + step * STEP_HID, STEP_HID), STEP_HID), :]


def call_mlp_forward(first, hidden, own, got, vecs, weights):
    rows = hidden.shape[0]
    return pl.pallas_call(
        mlp_forward,
        grid=(STEPS,),
        out_shape=[
            jax.ShapeDtypeStruct((rows, D), F32),
            output(first, rows, D),
            output(first, rows, HID),
            output(first, rows, HID),
            jax.ShapeDtypeStruct((rows, D), BF),
            jax.ShapeDtypeStruct(weights.shape, BF),
        ],
        input_output_aliases={4: 5},
        in_specs=[full(rows, D), full(rows, D), full(rows, D), full(16, D), VMEM],
        out_specs=[
            full(rows, D),
            full(rows, D),
            pl.BlockSpec((rows, STEP_HID), lambda s: (0, s)),
            pl.BlockSpec((rows, STEP_HID), lambda s: (0, s)),
            full(rows, D),
            VMEM,
        ],
        scratch_shapes=[pltpu.VMEM((rows, D), F32)],
        compiler_params=params(),
        cost_estimate=cost(2 * rows * D * 2 * HID * 2, 12 << 20),
        name="mlp_forward",
    )(hidden, own, got, vecs, weights)


def mlp_backward(first, *refs):
    if first:
        grad_ref, mid_ref, slope_ref, vecs, weights = refs[:5]
        gd_ref, gu_ref, part_ref, sums_ref, _, total = refs[5:]
    else:
        (gm_ref, own_ref, got_ref, hid_ref, above) = refs[:5]
        mid_ref, slope_ref, vecs, weights = refs[5:9]
        grad_out_ref, gd_ref, gu_ref, part_ref, sums_ref, _, total = refs[9:]
    step = pl.program_id(0)

    @pl.when(step == 0)
    def _():
        if first:
            gd_ref[...] = grad_ref[...]
        else:
            centre, rstd = stats(hid_ref[...])
            grad = own_ref[...].astype(F32) + got_ref[...].astype(F32)
            grad_hidden = gm_ref[...] + norm_back(grad, centre * rstd, rstd, above[0:1, :])
            grad_out_ref[...] = grad_hidden
            gd_ref[...] = grad_hidden.astype(BF)
        sums_ref[...] = jnp.zeros_like(sums_ref)
        sums_ref[2:3, :] = jnp.sum(gd_ref[...].astype(F32), axis=0, keepdims=True)

    grad_up = (slope_ref[...].astype(F32) * dot_nt(gd_ref[...], down_part(weights, step))).astype(BF)
    gu_ref[...] = grad_up
    sums = jnp.sum(grad_up.astype(F32), axis=0, keepdims=True)
    for at in range(STEPS):

        @pl.when(step == at)
        def _():
            sums_ref[3 + at // 2 : 4 + at // 2, (at % 2) * STEP_HID : (at % 2 + 1) * STEP_HID] = (
                sums
            )

    term = dot_nt(grad_up, up_part(weights, step))

    @pl.when(step == 0)
    def _():
        total[...] = term

    @pl.when((step > 0) & (step < STEPS - 1))
    def _():
        total[...] += term

    @pl.when(step == STEPS - 1)
    def _():
        grad = total[...] + term
        part_ref[...] = grad.astype(BF)
        centre, rstd = stats(mid_ref[...])
        sums_ref[0:1, :] = jnp.sum(grad * (centre * rstd), axis=0, keepdims=True)
        sums_ref[1:2, :] = jnp.sum(grad, axis=0, keepdims=True)


def call_mlp_backward(first, operands, middle, slope, vecs, weights):
    rows = middle.shape[0]
    specs = [full(rows, D)] if first else [full(rows, D)] * 4 + [full(16, D)]
    outs = [
        jax.ShapeDtypeStruct((rows, D), BF),
        jax.ShapeDtypeStruct((rows, HID), BF),
        jax.ShapeDtypeStruct((rows, D), BF),
        jax.ShapeDtypeStruct((8, D), F32),
    ]
    out_specs = [
        full(rows, D),
        pl.BlockSpec((rows, STEP_HID), lambda s: (0, s)),
        full(rows, D),
        full(8, D),
    ]
    if not first:
        outs = [jax.ShapeDtypeStruct((rows, D), F32)] + outs
        out_specs = [full(rows, D)] + out_specs
    return pl.pallas_call(
        functools.partial(mlp_backward, first),
        grid=(STEPS,),
        out_shape=outs + [jax.ShapeDtypeStruct(weights.shape, BF)],
        input_output_aliases={len(specs) + 3: len(outs)},
        in_specs=specs
        + [full(rows, D), pl.BlockSpec((rows, STEP_HID), lambda s: (0, s)), full(16, D), VMEM],
        out_specs=out_specs + [VMEM],
        scratch_shapes=[pltpu.VMEM((rows, D), F32)],
        compiler_params=params(),
        cost_estimate=cost(2 * rows * D * 2 * HID * 2, 12 << 20),
        name="mlp_backward",
    )(*operands, middle, slope, vecs, weights)


def attention_backward(
    grad_ref,
    own_ref,
    got_ref,
    mid_ref,
    hid_ref,
    qkv_ref,
    lse_ref,
    vecs,
    kept,
    weights,
    gm_ref,
    gb_ref,
    gp_ref,
    part_ref,
    sums_ref,
    _,
):
    rows = grad_ref.shape[0]
    centre, rstd = stats(mid_ref[...])
    grad_two = own_ref[...].astype(F32) + got_ref[...].astype(F32)
    grad_middle = grad_ref[...].astype(F32) + norm_back(
        grad_two, centre * rstd, rstd, vecs[4:5, :]
    )
    gm_ref[...] = grad_middle
    gb = grad_middle.astype(BF)
    gb_ref[...] = gb
    sums_ref[...] = jnp.zeros_like(sums_ref)
    sums_ref[3:4, :] = jnp.sum(gb.astype(F32), axis=0, keepdims=True)
    grad_att = (
        dot_nt(gb[:, 0:WID], weights[D : D + WID, WID:D])
        + dot_nt(gb[:, WID:D], weights[D + WID : 2 * D, WID:D])
    ).astype(BF)
    bias = key_bias(kept[0:1, :], rows)
    lane = lax.broadcasted_iota(jnp.int32, (rows, BLK), 1)
    for pair in range(WID // BLK):
        cols = slice(pair * BLK, (pair + 1) * BLK)
        key_cols = slice(WID + pair * BLK, WID + (pair + 1) * BLK)
        value_cols = slice(2 * WID + pair * BLK, 2 * WID + (pair + 1) * BLK)
        q = qkv_ref[:, cols] * jnp.asarray(0.125, BF)
        k = qkv_ref[:, key_cols]
        v = qkv_ref[:, value_cols]
        g = grad_att[:, cols]
        got = []
        for half in range(2):
            head = 2 * pair + half
            scores = dot_nt(lane_half(q, half), k) + bias
            att = jnp.exp(scores - lse_ref[:, head : head + 1])
            grad_a = dot_nt(lane_half(g, half), v)
            inner = jnp.sum(att * grad_a, axis=-1, keepdims=True)
            grad_s = (att * (grad_a - inner)).astype(BF)
            got.append((dot(grad_s, k) * 0.125, dot_tn(grad_s, q), dot_tn(att.astype(BF), g)))
        for at, where in enumerate((cols, key_cols, value_cols)):
            gp_ref[:, where] = jnp.where(lane < HEAD_DIM, got[0][at], got[1][at]).astype(BF)
    sums_ref[2:3, 0:WID] = jnp.sum(gp_ref[:, 0:WID].astype(F32), axis=0, keepdims=True)
    sums_ref[2:3, WID:D] = jnp.sum(gp_ref[:, 2 * WID :].astype(F32), axis=0, keepdims=True)
    grad = (
        dot_nt(gp_ref[:, 0:WID], weights[0:D, 0:WID])
        + dot_nt(gp_ref[:, WID : 2 * WID], weights[0:D, WID:D])
        + dot_nt(gp_ref[:, 2 * WID :], weights[D : 2 * D, 0:WID])
    )
    part_ref[...] = grad.astype(BF)
    centre, rstd = stats(hid_ref[...].astype(F32))
    sums_ref[0:1, :] = jnp.sum(grad * (centre * rstd), axis=0, keepdims=True)
    sums_ref[1:2, :] = jnp.sum(grad, axis=0, keepdims=True)


def call_attention_backward(*args):
    rows = args[0].shape[0]
    outs = [
        jax.ShapeDtypeStruct((rows, D), F32),
        jax.ShapeDtypeStruct((rows, D), BF),
        jax.ShapeDtypeStruct((rows, 3 * WID), BF),
        jax.ShapeDtypeStruct((rows, D), BF),
        jax.ShapeDtypeStruct((8, D), F32),
    ]
    return pl.pallas_call(
        attention_backward,
        grid=(1,),
        out_shape=outs + [jax.ShapeDtypeStruct(args[-1].shape, BF)],
        input_output_aliases={len(args) - 1: len(outs)},
        in_specs=[full(*a.shape) for a in args[:-1]] + [VMEM],
        out_specs=[full(*o.shape) for o in outs] + [VMEM],
        compiler_params=params(),
        cost_estimate=cost(2 * rows * D * 4 * WID * 3, 8 << 20),
        name="attention_backward",
    )(*args)


def mlp_grads(slot_own, slot_par, *refs):
    acts, gds, n2s, gus = refs[0:2], refs[2:4], refs[4:6], refs[6:8]
    own_ref, par_ref, down_buf, up_buf, sems = refs[8:]
    step = pl.program_id(0)
    at = lax.rem(step, 2)
    tiles = STEP_HID // 2 // BLK

    def start(of_step):
        part = lax.rem(of_step, 2)
        first = lax.rem(of_step, STEPS) * tiles

        def send(slots, out):
            def one(index, carry):
                tile = lax.div(index, 8)
                block = lax.rem(index, 8)
                down_row = pl.multiple_of(slots[128 + (first + tile) * 8 + block] * BLK, BLK)
                up_row = pl.multiple_of(slots[64 + block * 8 + first + tile] * BLK, BLK)
                tile_row = pl.multiple_of(tile * BLK, BLK)
                block_row = pl.multiple_of(block * BLK, BLK)
                pltpu.make_async_copy(
                    down_buf.at[part, pl.ds(tile_row, BLK), pl.ds(block_row, BLK)],
                    out.at[pl.ds(down_row, BLK), :],
                    sems.at[part],
                ).start()
                pltpu.make_async_copy(
                    up_buf.at[part, pl.ds(block_row, BLK), pl.ds(tile_row, BLK)],
                    out.at[pl.ds(up_row, BLK), :],
                    sems.at[part],
                ).start()
                return carry

            lax.fori_loop(0, tiles * 8, one, 0)

        pl.when(of_step < STEPS)(lambda: send(slot_own, own_ref))
        pl.when(of_step >= STEPS)(lambda: send(slot_par, par_ref))

    def wait(of_step):
        part = lax.rem(of_step, 2)
        for buf in (down_buf, up_buf):
            pltpu.make_async_copy(buf.at[part], buf.at[part], sems.at[part]).wait()

    @pl.when(step >= 2)
    def _():
        wait(step - 2)

    down_buf[at] = sum(dot_tn(a[...], g[...]) for a, g in zip(acts, gds)).astype(BF)
    up_buf[at] = sum(dot_tn(n[...], g[...]) for n, g in zip(n2s, gus)).astype(BF)
    start(step)

    @pl.when(step == 2 * STEPS - 1)
    def _():
        wait(step - 1)
        wait(step)


def call_mlp_grads(slots, acts, gds, n2s, gus):
    rows = gds[0].shape[0]
    wide = STEP_HID // 2
    by_hidden = pl.BlockSpec((rows, wide), lambda s, a, b: (0, s))
    whole = pl.BlockSpec((rows, D), lambda s, a, b: (0, 0))
    buffer = pltpu.HBM((SHARE_TILES * BLK, BLK), BF)
    return pl.pallas_call(
        mlp_grads,
        grid_spec=pltpu.PrefetchScalarGridSpec(
            num_scalar_prefetch=2,
            grid=(2 * STEPS,),
            in_specs=[by_hidden] * 2 + [whole] * 4 + [by_hidden] * 2,
            out_specs=[ANY, ANY],
            scratch_shapes=[
                pltpu.VMEM((2, wide, D), BF),
                pltpu.VMEM((2, D, wide), BF),
                pltpu.SemaphoreType.DMA((2,)),
            ],
        ),
        out_shape=[buffer, buffer],
        compiler_params=params(),
        cost_estimate=cost(2 * 2 * rows * D * 2 * HID * 2, 16 << 20),
        name="mlp_grads",
    )(*slots, *acts, *gds, *n2s, *gus)


def attention_grads(slot_own, slot_par, *refs):
    atts, gbs, n1s, gqs, gks, gvs = (refs[2 * i : 2 * i + 2] for i in range(6))
    own_ref, par_ref, out_buf, qkv_buf, sems = refs[14:]
    step = at = pl.program_id(0)
    per_share = D // NARROW // BLK

    def start(of_step):
        part = of_step

        def send(slots, out):
            def one(block, carry):
                block_row = pl.multiple_of(block * BLK, BLK)
                for column in range(per_share):
                    cols = pl.ds(column * BLK, BLK)
                    row = pl.multiple_of(slots[48 + column * 8 + block] * BLK, BLK)
                    pltpu.make_async_copy(
                        out_buf.at[part, cols, pl.ds(block_row, BLK)],
                        out.at[pl.ds(row, BLK), :],
                        sems.at[part],
                    ).start()
                    for third in range(3):
                        tile = block * 6 + third * 2 + column
                        row = pl.multiple_of(slots[tile] * BLK, BLK)
                        pltpu.make_async_copy(
                            qkv_buf.at[part, third, pl.ds(block_row, BLK), cols],
                            out.at[pl.ds(row, BLK), :],
                            sems.at[part],
                        ).start()
                return carry

            lax.fori_loop(0, 8, one, 0)

        pl.when(of_step == 0)(lambda: send(slot_own, own_ref))
        pl.when(of_step == 1)(lambda: send(slot_par, par_ref))

    def wait(part):
        for buf in (out_buf, qkv_buf):
            pltpu.make_async_copy(buf.at[part], buf.at[part], sems.at[part]).wait()

    out_buf[at] = sum(dot_tn(a[...], g[...]) for a, g in zip(atts, gbs)).astype(BF)
    for third, grads in enumerate((gqs, gks, gvs)):
        qkv_buf[at, third] = sum(dot_tn(n[...], g[...]) for n, g in zip(n1s, grads)).astype(BF)
    start(step)

    @pl.when(step == 1)
    def _():
        wait(0)
        wait(1)


def call_attention_grads(slots, atts, gbs, n1s, gps, own, par):
    rows = gbs[0].shape[0]
    width = WID // 2
    whole = pl.BlockSpec((rows, D), lambda s, a, b: (0, 0))

    def by_column(third):
        return pl.BlockSpec((rows, width), lambda s, a, b: (0, third * 2 + s))

    return pl.pallas_call(
        attention_grads,
        grid_spec=pltpu.PrefetchScalarGridSpec(
            num_scalar_prefetch=2,
            grid=(2,),
            in_specs=[by_column(0)] * 2
            + [whole] * 4
            + [by_column(0)] * 2
            + [by_column(1)] * 2
            + [by_column(2)] * 2
            + [ANY, ANY],
            out_specs=[ANY, ANY],
            scratch_shapes=[
                pltpu.VMEM((2, width, D), BF),
                pltpu.VMEM((2, 3, D, width), BF),
                pltpu.SemaphoreType.DMA((2,)),
            ],
        ),
        out_shape=[pltpu.HBM(own.shape, BF)] * 2,
        input_output_aliases={14: 0, 15: 1},
        compiler_params=params(),
        cost_estimate=cost(2 * 2 * rows * D * 4 * WID, 8 << 20),
        name="attention_grads",
    )(*slots, *atts, *gbs, *n1s, *gps, *gps, *gps, own, par)


def place_of(tile, share):
    quarter = WID // 2
    block, rest = tile // 6, tile % 6
    third, column = rest // 2, rest % 2
    qkv_row = jnp.where(third == 2, D, 0) + block * BLK
    qkv_col = jnp.where(third == 1, WID, 0) + share * quarter + column * BLK
    out = tile - 48
    out_block, out_col = out // 8, out % 8
    out_row = D + jnp.where(out_col >= 4, WID, 0) + share * quarter + out_block * BLK
    out_col = WID + (out_col % 4) * BLK
    up = tile - 64
    up_row, up_col = 2 * D + share * D + (up // 8) * BLK, (up % 8) * BLK
    down = tile - 128
    down_row, down_col = 4 * D + share * D + (down // 8) * BLK, (down % 8) * BLK
    kind = (tile >= 48).astype(jnp.int32) + (tile >= 64) + (tile >= 128)
    row = jnp.select([kind == 0, kind == 1, kind == 2], [qkv_row, out_row, up_row], down_row)
    col = jnp.select([kind == 0, kind == 1, kind == 2], [qkv_col, out_col, up_col], down_col)
    return row, col


def assemble_kernel(plan, rows, cols, *refs):
    sources = refs[: len(plan)]
    out_ref, sem = refs[-2:]
    for source, (share, first, count) in zip(sources, plan):

        def one(i, carry, source=source, share=share, first=first):
            row = pl.multiple_of(rows[share, first + i], BLK)
            col = pl.multiple_of(cols[share, first + i], BLK)
            pltpu.make_async_copy(
                source.at[pl.ds(pl.multiple_of(i * BLK, BLK), BLK), :],
                out_ref.at[pl.ds(row, BLK), pl.ds(col, BLK)],
                sem,
            ).start()
            return carry

        lax.fori_loop(0, count, one, 0, unroll=4 if count % 4 == 0 else 1)
    for source, (_, _, count) in zip(sources, plan):
        tiles = source.at[pl.ds(0, count * BLK), :]
        pltpu.make_async_copy(tiles, tiles, sem).wait()


def assemble(table, pieces):
    plan = [piece[:3] for piece in pieces]
    args = list(table) + [pltpu.with_memory_space_constraint(p[3], pltpu.HBM) for p in pieces]
    return pl.pallas_call(
        functools.partial(assemble_kernel, plan),
        out_shape=jax.ShapeDtypeStruct((6 * D, D), BF),
        in_specs=[SMEM, SMEM] + [ANY] * len(pieces),
        out_specs=ANY,
        scratch_shapes=[pltpu.SemaphoreType.DMA],
        compiler_params=params(),
        cost_estimate=cost(0, BLK),
        name="assemble",
    )(*args)


def ring(size):
    order = list(range(0, size, 2)) + list(range(size - 1, 0, -2))
    ahead = [(order[i], order[(i + 1) % size]) for i in range(size)]
    position = [order.index(i) for i in range(size)]
    return order, position, ahead, [(b, a) for a, b in ahead]


def after(value, *earlier):
    return lax.optimization_barrier((value, *earlier))[0]


def need_order(size):
    far = size // 2
    order = [far]
    for step in range(far - 1, 0, -1):
        order += [step, size - step]
    return order + [0]


class Gather:
    def __init__(self, unit, size, per_device):
        _, _, self.ahead, self.behind = ring(size)
        self.size, self.per_device, self.step_count = size, per_device, 0
        self.up = self.down = unit

    def step(self, *earlier):
        self.step_count += 1
        step, far, front = self.step_count, self.size // 2, self.per_device // 2
        up, down = self.up, self.down
        if step == far:
            up, down = up[: front * BLK], down[front * BLK :]
        up, down, *_ = lax.optimization_barrier((up, down, *earlier))
        self.sent = (up, down)
        self.up = lax.ppermute(up, "wide", self.ahead)
        self.down = lax.ppermute(down, "wide", self.behind)
        if step < far:
            return [
                (self.size - step, 0, self.per_device, self.up),
                (step, 0, self.per_device, self.down),
            ]
        return [
            (far, 0, front, self.up),
            (far, front, self.per_device - front, self.down),
        ]


class Scatter:
    def __init__(self, unit_of, size, cut):
        _, _, self.ahead, self.behind = ring(size)
        self.unit_of, self.size, self.cut, self.left = unit_of, size, cut, size // 2

    def step(self, *earlier):
        cut = self.cut
        if self.left == self.size // 2:
            last = self.unit_of(self.left)
            up, down = last[:cut], last[cut:]
        else:
            up, down = self.unit_of(self.left), self.unit_of(self.size - self.left)
            got_up, got_down = self.up.astype(F32), self.down.astype(F32)
            if self.left == self.size // 2 - 1:
                up = jnp.concatenate([up[:cut] + got_up, up[cut:]])
                down = jnp.concatenate([down[:cut], down[cut:] + got_down])
            else:
                up, down = up + got_up, down + got_down
        up, down = up.astype(BF), down.astype(BF)
        up, down, *_ = lax.optimization_barrier((up, down, *earlier))
        self.sent = (up, down)
        self.up = lax.ppermute(up, "wide", self.ahead)
        self.down = lax.ppermute(down, "wide", self.behind)
        self.left -= 1

    def result(self):
        return self.unit_of(0) + self.up.astype(F32) + self.down.astype(F32)


def mesh_bits():
    out, base = [], 1
    for axis in ("narrow", "wide"):
        size, bit = lax.axis_size(axis), 1
        while bit < size:
            out.append((base * bit, axis, [(i, i ^ bit) for i in range(size)]))
            bit *= 2
        base *= size
    return out


def tile_ids(share):
    tile_rows = D // BLK
    shard_cols = D // (NARROW * BLK)
    shard_hidden = FF // (NARROW * BLK)
    count_qkv = tile_rows * 3 * tile_rows
    start_up = count_qkv + tile_rows * tile_rows
    start_down = start_up + tile_rows * (FF // BLK)
    row_part = jnp.arange(tile_rows)[:, None, None]
    third = jnp.arange(3)[None, :, None]
    column_part = jnp.arange(shard_cols)[None, None, :]
    qkv_ids = (
        row_part * 3 * tile_rows + third * tile_rows + share * shard_cols + column_part
    ).reshape(-1)
    out_ids = (
        count_qkv
        + (share * shard_cols + jnp.arange(shard_cols)[:, None]) * tile_rows
        + jnp.arange(tile_rows)[None, :]
    ).reshape(-1)
    up_ids = (
        start_up
        + jnp.arange(tile_rows)[:, None] * (FF // BLK)
        + share * shard_hidden
        + jnp.arange(shard_hidden)[None, :]
    ).reshape(-1)
    down_ids = (
        start_down
        + (share * shard_hidden + jnp.arange(shard_hidden)[:, None]) * tile_rows
        + jnp.arange(tile_rows)[None, :]
    ).reshape(-1)
    return jnp.concatenate([qkv_ids, out_ids, up_ids, down_ids])


def share_vectors(small_all, me):
    pieces = [small_all[i * D : (i + 1) * D] for i in range(8)]
    bias_up = small_all[8 * D :]

    def both(vector, width):
        own = lax.dynamic_slice_in_dim(vector, me * width, width)
        par = lax.dynamic_slice_in_dim(vector, (me ^ 1) * width, width)
        return jnp.concatenate([own, par])

    quarter = D // NARROW
    heads = jnp.concatenate([both(pieces[2], quarter), both(pieces[3], quarter)])
    rows = [pieces[0], pieces[1], heads, pieces[4], pieces[5], pieces[6], pieces[7]]
    up = both(bias_up, FF // NARROW)
    rows = rows + [up[0:D], up[D:]]
    return jnp.pad(jnp.stack(rows), ((0, 7), (0, 0)))


def small_vector(mlp_sums, att_sums, me):
    half = me // 2
    mine = [(half == t).astype(F32) for t in range(2)]
    mlp = mlp_sums[0] + mlp_sums[1]
    att = att_sums[0] + att_sums[1]
    bias_down = mine[0] * mlp_sums[0][2] + mine[1] * mlp_sums[1][2]
    bias_out = mine[0] * att_sums[0][3] + mine[1] * att_sums[1][3]
    odd = (me % 2) == 1

    def spread(own, par):
        placed = jnp.where(odd, jnp.concatenate([par, own]), jnp.concatenate([own, par]))
        return [jnp.where(half == 0, placed, 0.0), jnp.where(half == 1, placed, 0.0)]

    quarter = D // NARROW
    heads = att[2]
    return jnp.concatenate(
        [att[0], att[1]]
        + spread(heads[0:quarter], heads[quarter : 2 * quarter])
        + spread(heads[2 * quarter : 3 * quarter], heads[3 * quarter :])
        + [bias_out, mlp[0], mlp[1], bias_down]
        + spread(mlp[3], mlp[4])
    )


def total_over_mesh(value):
    value = jnp.broadcast_to(value.reshape(1, 1), (8, BLK))
    for axis in ("narrow", "wide"):
        size, bit = lax.axis_size(axis), 1

        def swap(flip, value=None, axis=axis, size=size):
            return lax.ppermute(value, axis, [(i, i ^ flip) for i in range(size)])

        while bit < size:
            if 2 * bit < size:
                near, far, both = (swap(bit * k, value) for k in (1, 2, 3))
                value = (value + near) + (far + both)
            else:
                value = value + swap(bit, value)
            bit *= 4
    return value[0, 0]


def update_kernel(clip_ref, grad0, grad1, left, right, first, second, master, *outs):
    new_first, new_second, new_master, new_weights = outs
    step = pl.program_id(0)
    half = pl.num_programs(0) // 2
    clip = clip_ref[0]
    grads = (grad0, grad1)
    count = left.shape[1]
    for base in range(0, count, 4):
        blocks = range(base, min(base + 4, count))
        lefts = [left[0, b].astype(BF) for b in blocks]
        rights = [right[0, b].astype(BF) for b in blocks]
        terms = [
            jnp.where(step < half, *(g[b * BLK : (b + 1) * BLK, :] for g in grads)).astype(BF)
            for b in blocks
        ]
        terms = [dot_tn(a, x).astype(BF) for a, x in zip(lefts, terms)]
        terms = [clip * dot(x, b) for x, b in zip(terms, rights)]
        ones = [0.5 * first[0, b] + 0.5 * x for b, x in zip(blocks, terms)]
        twos = [0.5 * second[0, b] + 0.5 * x * x for b, x in zip(blocks, terms)]
        terms = [(a / (jnp.sqrt(b) + 1e-08)).astype(BF) for a, b in zip(ones, twos)]
        terms = [dot(a, x).astype(BF) for a, x in zip(lefts, terms)]
        terms = [dot_nt(x, b) for x, b in zip(terms, rights)]
        for b, one, two, turned in zip(blocks, ones, twos, terms):
            new_first[0, b] = one
            new_second[0, b] = two
            weights = master[0, b] - 0.02 * turned
            new_master[0, b] = weights
            new_weights[0, b] = weights.astype(BF)


def update(clip, grads, left, right, first, second, master):
    count = left.shape[1]
    group = 8 if count % 8 == 0 else 1
    steps = count // group
    spec = pl.BlockSpec((1, group, BLK, BLK), lambda i: (i // steps, i % steps, 0, 0))
    low = pl.BlockSpec((group * BLK, BLK), lambda i: (jnp.minimum(i, steps - 1), 0))
    high = pl.BlockSpec((group * BLK, BLK), lambda i: (jnp.maximum(i - steps, 0), 0))
    shape = jax.ShapeDtypeStruct(master.shape, F32)
    return pl.pallas_call(
        update_kernel,
        grid=(2 * steps,),
        out_shape=[shape, shape, shape, jax.ShapeDtypeStruct(master.shape, BF)],
        in_specs=[SMEM, low, high] + [spec] * 5,
        out_specs=[spec] * 4,
        compiler_params=params(56),
        cost_estimate=cost(count * 16 * BLK**3, count * BLK * BLK * 2 * 38),
        name="update",
    )(clip, *grads, left, right, first, second, master)


def shards(
    images,
    cotangent,
    kept_tokens,
    owner_slots,
    master_blocks,
    small_params,
    left_basis,
    right_basis,
    first_moment,
    second_moment,
    small_first,
    small_second,
):
    me = lax.axis_index("narrow")
    half, core = me // 2, me % 2
    wide = lax.axis_size("wide")
    per_device = master_blocks.shape[1]
    own_small = small_params.shape[1]
    own_images = images.shape[0]
    rows = own_images * S

    device = lax.axis_index("wide") * NARROW + me
    by_distance = jnp.arange(wide * NARROW) ^ device

    def chunks(own):
        other = lax.ppermute(own, "narrow", ACROSS)
        return [jnp.where(half == t, own, other) for t in range(2)]

    kept = [
        lax.dynamic_slice_in_dim(kept_tokens, (2 * t + core) * own_images, own_images, 0)
        .T.reshape(1, rows)
        .astype(F32)
        for t in range(2)
    ]

    order, position, _, _ = ring(wide)
    place = jnp.take(jnp.asarray(position, jnp.int32), lax.axis_index("wide"))
    around = jnp.take(jnp.asarray(order, jnp.int32), (place + jnp.arange(wide)) % wide)

    needed = need_order(wide)
    turns = [needed.index(distance) for distance in range(wide)]
    slots, tables = [], []
    for layer in range(LAYERS):
        owners = owner_slots[layer]
        layer_slots, layer_rows, layer_cols = [], [], []
        for at, share in enumerate((me, me ^ 1)):
            slot = jnp.take(owners, tile_ids(share))
            at_wide, at_pos = slot // per_device // NARROW, slot % per_device
            distance = (jnp.take(jnp.asarray(position, jnp.int32), at_wide) - place) % wide
            relative = distance * per_device + at_pos
            turn = jnp.take(jnp.asarray(turns, jnp.int32), distance)
            layer_slots.append(turn * per_device + at_pos)
            here = relative[None, :] == jnp.arange(SHARE_TILES)[:, None]
            tile = jnp.sum(jnp.where(here, jnp.arange(SHARE_TILES)[None, :], 0), axis=1)
            row, col = place_of(tile, at)
            layer_rows.append(row)
            layer_cols.append(col)
        slots.append(layer_slots)
        tables.append((jnp.stack(layer_rows), jnp.stack(layer_cols)))

    def by_token(value):
        return value.transpose(1, 0, 2).reshape(rows, D)

    def by_image(value):
        return value.reshape(S, own_images, D).transpose(1, 0, 2)

    def core_swap(value):
        return lax.ppermute(value, "narrow", CORE)

    def exchange(part):
        return lax.ppermute(part, "narrow", ACROSS)

    units = [
        master_blocks[layer].astype(BF).reshape(per_device * BLK, BLK) for layer in range(LAYERS)
    ]

    def swapped(pieces):
        return [piece + (core_swap(piece[3]),) for piece in pieces]

    def place_pieces(layer, pieces):
        group = [
            (share, distance * per_device + first, count, pair[share])
            for distance, first, count, *pair in pieces
            for share in range(2)
        ]
        return assemble(tables[layer], group)

    steps = wide // 2
    own_small_rows = small_params.astype(BF).reshape(1, -1)
    small_rows = own_small_rows
    bits = mesh_bits()
    near_bits, far_bits = bits[:2], bits[2:]
    per_window = -(-len(far_bits) // max(steps - 1, 1))

    def grow(rows, some_bits):
        for _, axis, perm in some_bits:
            rows = jnp.concatenate([rows, lax.ppermute(rows, axis, perm)])
        return rows

    gather = Gather(units[0], wide, per_device)
    arrived = [(0, 0, per_device, units[0])] + gather.step()
    small_rows = grow(small_rows, near_bits)
    inputs = [by_token(images), by_token(cotangent)]
    placed, extra = [], [small_rows]
    brought = []
    for step in range(2, steps + 1):
        latest = swapped(arrived)
        arrived = gather.step(*extra)
        placed += latest
        extra = [piece[4] for piece in latest]
        if step == 2:
            brought = chunks(after(inputs[0], *gather.sent))
            extra += brought + [inputs[1]]
        elif step == 3:
            late = exchange(after(inputs[1], *gather.sent))
        at = (step - 2) * per_window
        small_rows = grow(small_rows, far_bits[at : at + per_window])
        if step < steps:
            extra.append(small_rows)
    hidden_in = brought
    next_unit = after(units[1], gather.up, gather.down, late)
    gather_next = Gather(next_unit, wide, per_device)
    arrived_next = [(0, 0, per_device, next_unit)] + gather_next.step()
    last = [piece[:3] + (after(piece[3], *gather_next.sent),) for piece in arrived]
    weights = [place_pieces(0, placed + swapped(last))]
    cot = [jnp.where(half == t, inputs[1], late) for t in range(2)]

    in_order = jnp.take(small_rows, by_distance, axis=0).astype(F32)
    small_all = in_order.reshape(-1, LAYERS, own_small).transpose(1, 0, 2).reshape(LAYERS, -1)
    vecs = [share_vectors(small_all[layer], me) for layer in range(LAYERS)]

    saved = []
    state = None
    for layer in range(LAYERS):
        kept_layer = []
        for t in range(2):
            if layer == 0:
                hidden = hidden_in[t]
                if t == 1:
                    placed = swapped(arrived_next)
                    arrived_next = gather_next.step(part)
                    hidden = after(hidden, *gather_next.sent)
                *out, weights[layer] = call_attention_forward(
                    True, (hidden,), vecs[0], kept[t], weights[layer]
                )
            else:
                hidden, *out, weights[layer] = call_attention_forward(
                    False, state[t] + (vecs[layer - 1],), vecs[layer], kept[t], weights[layer]
                )
            n1, qkv, lse, att, part = out
            kept_layer.append([hidden, n1, qkv, lse, att, part, exchange(part)])
        kept_layer[0][5] = after(kept_layer[0][5], kept_layer[1][5])
        state = []
        for t in range(2):
            hidden, n1, qkv, lse, att, part, got = kept_layer[t]
            if layer == 0 and t == 1:
                placed += swapped(arrived_next)
                arrived_next = gather_next.step(down_part)
                placed += swapped(arrived_next)
                arrived_next = gather_next.step()
                part = after(part, *gather_next.sent, *vecs[1:])
            middle, n2, act, slope, down_part, weights[layer] = call_mlp_forward(
                layer == 0, hidden, part, got, vecs[layer], weights[layer]
            )
            kept_layer[t] = (hidden, n1, qkv, lse, att, middle, n2, act, slope)
            if layer < LAYERS - 1:
                state.append((middle, down_part, exchange(down_part)))
            else:
                state.append((middle, down_part))
        saved.append(kept_layer)
        if layer == 0:
            for _ in range(5, steps + 1):
                placed += swapped(arrived_next)
                arrived_next = gather_next.step()
            weights.append(place_pieces(1, placed + swapped(arrived_next)))

    def mine(pair):
        return jnp.where(half == 0, pair[0], pair[1])

    def theirs(pair):
        return jnp.where(half == 0, pair[1], pair[0])

    down_parts = [state[t][1] for t in range(2)]
    middles = [state[t][0] for t in range(2)]
    upstream = None
    reduced = [None] * LAYERS
    small_terms = [None] * LAYERS
    pending = None
    for layer in reversed(range(LAYERS)):
        kept_layer = saved[layer]
        top = layer == LAYERS - 1
        work = []
        for t in range(2):
            hidden, n1, qkv, lse, att, middle, n2, act, slope = kept_layer[t]
            if top:
                grad = cot[t]
                gd, gu, part, sums, weights[layer] = call_mlp_backward(
                    True, (grad,), middle, slope, vecs[layer], weights[layer]
                )
            else:
                state = upstream[t]
                state = (after(state[0], *pending.sent),) + state[1:]
                grad, gd, gu, part, sums, weights[layer] = call_mlp_backward(
                    False, state + (vecs[layer + 1],), middle, slope, vecs[layer], weights[layer]
                )
                if t == 0:
                    pending.step(part)
            work.append([grad, gd, gu, part, sums, exchange(part)])
        gds = [w[1] for w in work]
        if pending is not None:
            gds[0] = after(gds[0], *pending.sent)
        own, par = call_mlp_grads(
            slots[layer],
            [k[7] for k in kept_layer],
            gds,
            [k[6] for k in kept_layer],
            [w[2] for w in work],
        )
        if pending is not None:
            pending.step(own)
        back = []
        for t in range(2):
            hidden, n1, qkv, lse, att, middle, n2, act, slope = kept_layer[t]
            grad, gd, gu, part, sums, got = work[t]
            if pending is not None:
                part = after(part, *pending.sent)
            gm, gb, gp, att_part, att_sums, weights[layer] = call_attention_backward(
                grad, part, got, middle, hidden, qkv, lse, vecs[layer], kept[t], weights[layer]
            )
            back.append((gm, gb, gp, att_part, att_sums))
        if pending is not None:
            pending.step(back[1][3])
            while pending.left > 0:
                pending.step()
            own = after(own, *pending.sent)
        if layer > 0:
            got = [exchange(back[t][3]) for t in range(2)]
            own = after(own, got[0])
            upstream = [
                (back[0][0], back[0][3], got[0], kept_layer[0][0]),
                (back[1][0], back[1][3], got[1], kept_layer[1][0]),
            ]
        own, par = call_attention_grads(
            slots[layer],
            [k[4] for k in kept_layer],
            [b[1] for b in back],
            [k[1] for k in kept_layer],
            [b[2] for b in back],
            own,
            par,
        )
        if pending is not None:
            own = after(own, pending.up, pending.down)
        terms = small_vector([w[4] for w in work], [b[4] for b in back], me)
        small_terms[layer] = terms.reshape(-1, own_small)
        unit_len = per_device * BLK

        first_got = core_swap(par[:unit_len])
        earlier = pending
        pending = Scatter(None, wide, (per_device // 2) * BLK)

        def first_unit(distance, own=own, got=first_got, unit_len=unit_len):
            return own[:unit_len].astype(F32) + got.astype(F32)

        pending.unit_of = first_unit
        pending.step()
        rest = core_swap(after(par, *pending.sent))
        if earlier is not None:
            earlier.up = after(earlier.up, *pending.sent)
            reduced[layer + 1] = earlier.result()

        def unit_of(distance, own=own, rest=rest, unit_len=unit_len):
            at = turns[distance] * unit_len
            return own[at : at + unit_len].astype(F32) + rest[at : at + unit_len].astype(F32)

        pending.unit_of = unit_of

    final = mine(middles) + (
        mine(down_parts).astype(F32)
        + exchange(after(theirs(down_parts), rest)).astype(F32)
        + vecs[LAYERS - 1][6]
    )
    block_output = by_image(final.astype(BF))
    parts = [b[3] for b in back]
    last_part = exchange(after(theirs(parts), rest)).astype(F32)
    small_rows = jnp.take(jnp.concatenate(small_terms, axis=1), by_distance, axis=0)
    small_rows = after(small_rows, rest)
    backward_bits = mesh_bits()[::-1]
    local_sum = input_grad = None
    while pending.left > 0:
        for bit, axis, perm in backward_bits[:per_window]:
            small_rows = small_rows[:bit] + lax.ppermute(small_rows[bit:], axis, perm)
        backward_bits = backward_bits[per_window:]
        pending.step(small_rows)
        early = list(pending.sent)
        if local_sum is None:
            upper = [after(grads, *pending.sent) for grads in reduced[1:]]
            local_sum = sum(jnp.sum(grads * grads) for grads in upper)
            early.append(local_sum)
        elif input_grad is None:
            hidden = mine([k[0] for k in saved[0]]).astype(F32)
            centre, rstd = stats(hidden)
            lower = norm_back(
                mine(parts).astype(F32) + after(last_part, *pending.sent),
                centre * rstd,
                rstd,
                vecs[0][0:1],
            )
            input_grad = by_image(mine([b[0] for b in back]) + lower)
            early += [input_grad, block_output]
        small_rows = after(small_rows, *early)
    for bit, axis, perm in backward_bits:
        small_rows = small_rows[:bit] + lax.ppermute(small_rows[bit:], axis, perm)
    reduced[0] = pending.result()
    grad_small = small_rows.reshape(LAYERS, own_small)
    local_sum = local_sum + jnp.sum(grad_small * grad_small) + jnp.sum(reduced[0] * reduced[0])
    grad_norm = jnp.sqrt(total_over_mesh(local_sum))
    clip_factor = 1.0 / jnp.maximum(grad_norm, 1.0)
    new_first, new_second, new_master, new_weights = update(
        clip_factor.reshape(1),
        reduced,
        left_basis,
        right_basis,
        first_moment,
        second_moment,
        master_blocks,
    )
    clipped_small = clip_factor * grad_small
    new_small_first = 0.5 * small_first + 0.5 * clipped_small
    new_small_second = 0.5 * small_second + 0.5 * clipped_small * clipped_small
    new_small = small_params - 0.3 * new_small_first / (jnp.sqrt(new_small_second) + 1e-08)
    return (
        block_output,
        input_grad,
        grad_norm.reshape(1),
        new_first,
        new_second,
        new_master,
        new_weights,
        new_small_first,
        new_small_second,
        new_small,
        new_small.astype(BF),
    )


def solution(mesh):
    both = ("wide", "narrow")
    rows = P(both, None, None)
    blocks = P(None, both, None, None)
    small = P(None, both)
    in_specs = (
        rows,
        rows,
        P("wide", None),
        P(),
        blocks,
        small,
        blocks,
        blocks,
        blocks,
        blocks,
        small,
        small,
    )
    out_specs = (rows, rows, P(), blocks, blocks, blocks, blocks, small, small, small, small)
    return jax.shard_map(shards, mesh=mesh, in_specs=in_specs, out_specs=out_specs, check_vma=False)
```

```python
import functools

import jax
import jax.numpy as jnp
from jax import lax
from jax.experimental import pallas as pl
from jax.experimental.pallas import tpu as pltpu
from jax.sharding import PartitionSpec as P

D = 1024
HEAD_DIM = 64
FF = 4096
S = 50
LAYERS = 2
BLK = 128
NARROW = 4

BF = jnp.bfloat16
F32 = jnp.float32

WID = D // 2
HID = FF // 2
SHARE_TILES = 192
ATT_ROWS = 2 * D
MLP_ROWS = 4 * D

CORE = [(j, j ^ 1) for j in range(NARROW)]
ACROSS = [(j, j ^ 2) for j in range(NARROW)]
ANY = pl.BlockSpec(memory_space=pl.ANY)
SMEM = pl.BlockSpec(memory_space=pltpu.SMEM)
VMEM = pl.BlockSpec(memory_space=pltpu.VMEM)


def params(mib=16):
    return pltpu.CompilerParams(vmem_limit_bytes=mib << 20)


def cost(flops, nbytes):
    return pl.CostEstimate(flops=flops, bytes_accessed=nbytes, transcendentals=0)


def output(in_hbm, *shape, dtype=BF):
    return (pltpu.HBM if in_hbm else jax.ShapeDtypeStruct)(shape, dtype)


def dot(a, b):
    return jnp.dot(a, b, preferred_element_type=F32)


def dot_nt(a, b):
    return lax.dot_general(a, b, (((1,), (1,)), ((), ())), preferred_element_type=F32)


def dot_tn(a, b):
    return lax.dot_general(a, b, (((0,), (0,)), ((), ())), preferred_element_type=F32)


def stats(x):
    centre = x - jnp.mean(x, axis=-1, keepdims=True)
    spread = jnp.mean(centre * centre, axis=-1, keepdims=True)
    return centre, lax.rsqrt(spread + 1e-06)


def norm_back(grad, xhat, rstd, gain):
    gn = grad * gain
    return rstd * (
        gn
        - jnp.mean(gn, axis=-1, keepdims=True)
        - xhat * jnp.mean(gn * xhat, axis=-1, keepdims=True)
    )


def key_bias(kept_row, rows):
    def image_of(dim):
        return lax.rem(lax.broadcasted_iota(jnp.int32, (rows, rows), dim), rows // S)

    allowed = (image_of(0) == image_of(1)) & (kept_row > 0.0)
    return jnp.where(allowed, 0.0, -1e30)


def lane_half(x, half):
    lane = lax.broadcasted_iota(jnp.int32, x.shape, 1)
    keep = (lane < HEAD_DIM) if half == 0 else (lane >= HEAD_DIM)
    return jnp.where(keep, x, jnp.zeros_like(x))


def attention_forward(first, *refs):
    if first:
        x_ref, vecs, kept, weights, n1_ref, qkv_ref, lse_ref, att_ref, part_ref, _ = refs
        hidden = x_ref[...].astype(F32)
    else:
        (mid_ref, own_ref, got_ref, prev, vecs, kept, weights) = refs[:7]
        hidden_ref, n1_ref, qkv_ref, lse_ref, att_ref, part_ref, _ = refs[7:]
        hidden = mid_ref[...] + (
            own_ref[...].astype(F32) + got_ref[...].astype(F32) + prev[6:7, :]
        )
        hidden_ref[...] = hidden
    rows = hidden.shape[0]
    centre, rstd = stats(hidden)
    n1 = (centre * rstd * vecs[0:1, :] + vecs[1:2, :]).astype(BF)
    n1_ref[...] = n1
    qkv_ref[:, 0:WID] = (dot(n1, weights[0:D, 0:WID]) + vecs[2:3, 0:WID]).astype(BF)
    qkv_ref[:, WID : 2 * WID] = dot(n1, weights[0:D, WID:D]).astype(BF)
    qkv_ref[:, 2 * WID :] = (dot(n1, weights[D : 2 * D, 0:WID]) + vecs[2:3, WID:D]).astype(BF)
    bias = key_bias(kept[0:1, :], rows)
    lane = lax.broadcasted_iota(jnp.int32, (rows, BLK), 1)
    lse_all = jnp.zeros((rows, BLK), F32)
    for pair in range(WID // BLK):
        cols = slice(pair * BLK, (pair + 1) * BLK)
        q = qkv_ref[:, cols] * jnp.asarray(0.125, BF)
        k = qkv_ref[:, WID + pair * BLK : WID + (pair + 1) * BLK]
        v = qkv_ref[:, 2 * WID + pair * BLK : 2 * WID + (pair + 1) * BLK]
        outs = []
        for half in range(2):
            scores = dot_nt(lane_half(q, half), k) + bias
            top = jnp.max(scores, axis=-1, keepdims=True)
            raised = jnp.exp(scores - top)
            total = jnp.sum(raised, axis=-1, keepdims=True)
            outs.append(dot((raised * (1.0 / total)).astype(BF), v))
            lse_all = jnp.where(lane == 2 * pair + half, top + jnp.log(total), lse_all)
        att_ref[:, cols] = jnp.where(lane < HEAD_DIM, outs[0], outs[1]).astype(BF)
    lse_ref[...] = lse_all
    att = att_ref[...]
    part_ref[:, 0:WID] = dot(att, weights[D : D + WID, WID:D]).astype(BF)
    part_ref[:, WID:D] = dot(att, weights[D + WID : 2 * D, WID:D]).astype(BF)


def call_attention_forward(first, operands, vecs, kept, weights):
    rows = operands[0].shape[0]
    outs = [
        output(first, rows, D),
        output(first, rows, 3 * WID),
        output(first, rows, BLK, dtype=F32),
        output(first, rows, WID),
        jax.ShapeDtypeStruct((rows, D), BF),
    ]
    if not first:
        outs = [jax.ShapeDtypeStruct((rows, D), F32)] + outs
    args = list(operands) + [vecs, kept, weights]
    return pl.pallas_call(
        functools.partial(attention_forward, first),
        out_shape=outs + [jax.ShapeDtypeStruct(weights.shape, BF)],
        grid=(1,),
        in_specs=[full(*a.shape) for a in args[:-1]] + [VMEM],
        out_specs=[full(*o.shape) for o in outs] + [VMEM],
        input_output_aliases={len(args) - 1: len(outs)},
        compiler_params=params(),
        cost_estimate=cost(2 * rows * D * 4 * WID * 2, 6 << 20),
        name="attention_forward",
    )(*args)


STEPS = 4
STEP_HID = HID // STEPS


def mlp_forward(hid_ref, own_ref, got_ref, vecs, weights, *rest):
    mid_ref, n2_ref, act_ref, slope_ref, part_ref, _, total = rest
    step = pl.program_id(0)

    @pl.when(step == 0)
    def _():
        middle = hid_ref[...].astype(F32) + (
            own_ref[...].astype(F32) + got_ref[...].astype(F32) + vecs[3:4, :]
        )
        mid_ref[...] = middle
        centre, rstd = stats(middle)
        n2_ref[...] = (centre * rstd * vecs[4:5, :] + vecs[5:6, :]).astype(BF)

    row = 7 + step // 2
    bias = jnp.where(
        step % 2 == 0, vecs[pl.ds(row, 1), 0:STEP_HID], vecs[pl.ds(row, 1), STEP_HID:D]
    )
    upward = dot(n2_ref[...], up_part(weights, step)) + bias
    cdf = 0.5 + 0.5 * lax.erf(upward * 0.7071067811865476)
    act = (upward * cdf).astype(BF)
    act_ref[...] = act
    slope_ref[...] = (
        cdf + upward * (jnp.exp(-0.5 * upward * upward) * 0.3989422804014327)
    ).astype(BF)
    term = dot(act, down_part(weights, step))

    @pl.when(step == 0)
    def _():
        total[...] = term

    @pl.when((step > 0) & (step < STEPS - 1))
    def _():
        total[...] += term

    @pl.when(step == STEPS - 1)
    def _():
        part_ref[...] = (total[...] + term).astype(BF)


def full(rows, cols):
    return pl.BlockSpec((rows, cols), lambda s: (0, 0))


def up_part(weights, step):
    rows = pl.ds(pl.multiple_of(2 * D + step // 2 * D, D), D)
    return weights[rows, pl.ds(pl.multiple_of(step % 2 * STEP_HID, STEP_HID), STEP_HID)]


def down_part(weights, step):
    return weights[pl.ds(pl.multiple_of(4 * D + step * STEP_HID, STEP_HID), STEP_HID), :]


def call_mlp_forward(first, hidden, own, got, vecs, weights):
    rows = hidden.shape[0]
    return pl.pallas_call(
        mlp_forward,
        grid=(STEPS,),
        out_shape=[
            jax.ShapeDtypeStruct((rows, D), F32),
            output(first, rows, D),
            output(first, rows, HID),
            output(first, rows, HID),
            jax.ShapeDtypeStruct((rows, D), BF),
            jax.ShapeDtypeStruct(weights.shape, BF),
        ],
        input_output_aliases={4: 5},
        in_specs=[full(rows, D), full(rows, D), full(rows, D), full(16, D), VMEM],
        out_specs=[
            full(rows, D),
            full(rows, D),
            pl.BlockSpec((rows, STEP_HID), lambda s: (0, s)),
            pl.BlockSpec((rows, STEP_HID), lambda s: (0, s)),
            full(rows, D),
            VMEM,
        ],
        scratch_shapes=[pltpu.VMEM((rows, D), F32)],
        compiler_params=params(),
        cost_estimate=cost(2 * rows * D * 2 * HID * 2, 12 << 20),
        name="mlp_forward",
    )(hidden, own, got, vecs, weights)


def mlp_backward(first, *refs):
    if first:
        grad_ref, mid_ref, slope_ref, vecs, weights = refs[:5]
        gd_ref, gu_ref, part_ref, sums_ref, _, total = refs[5:]
    else:
        (gm_ref, own_ref, got_ref, hid_ref, above) = refs[:5]
        mid_ref, slope_ref, vecs, weights = refs[5:9]
        grad_out_ref, gd_ref, gu_ref, part_ref, sums_ref, _, total = refs[9:]
    step = pl.program_id(0)

    @pl.when(step == 0)
    def _():
        if first:
            gd_ref[...] = grad_ref[...]
        else:
            centre, rstd = stats(hid_ref[...])
            grad = own_ref[...].astype(F32) + got_ref[...].astype(F32)
            grad_hidden = gm_ref[...] + norm_back(grad, centre * rstd, rstd, above[0:1, :])
            grad_out_ref[...] = grad_hidden
            gd_ref[...] = grad_hidden.astype(BF)
        sums_ref[...] = jnp.zeros_like(sums_ref)
        sums_ref[2:3, :] = jnp.sum(gd_ref[...].astype(F32), axis=0, keepdims=True)

    grad_up = (slope_ref[...].astype(F32) * dot_nt(gd_ref[...], down_part(weights, step))).astype(BF)
    gu_ref[...] = grad_up
    sums = jnp.sum(grad_up.astype(F32), axis=0, keepdims=True)
    for at in range(STEPS):

        @pl.when(step == at)
        def _():
            sums_ref[3 + at // 2 : 4 + at // 2, (at % 2) * STEP_HID : (at % 2 + 1) * STEP_HID] = (
                sums
            )

    term = dot_nt(grad_up, up_part(weights, step))

    @pl.when(step == 0)
    def _():
        total[...] = term

    @pl.when((step > 0) & (step < STEPS - 1))
    def _():
        total[...] += term

    @pl.when(step == STEPS - 1)
    def _():
        grad = total[...] + term
        part_ref[...] = grad.astype(BF)
        centre, rstd = stats(mid_ref[...])
        sums_ref[0:1, :] = jnp.sum(grad * (centre * rstd), axis=0, keepdims=True)
        sums_ref[1:2, :] = jnp.sum(grad, axis=0, keepdims=True)


def call_mlp_backward(first, operands, middle, slope, vecs, weights):
    rows = middle.shape[0]
    specs = [full(rows, D)] if first else [full(rows, D)] * 4 + [full(16, D)]
    outs = [
        jax.ShapeDtypeStruct((rows, D), BF),
        jax.ShapeDtypeStruct((rows, HID), BF),
        jax.ShapeDtypeStruct((rows, D), BF),
        jax.ShapeDtypeStruct((8, D), F32),
    ]
    out_specs = [
        full(rows, D),
        pl.BlockSpec((rows, STEP_HID), lambda s: (0, s)),
        full(rows, D),
        full(8, D),
    ]
    if not first:
        outs = [jax.ShapeDtypeStruct((rows, D), F32)] + outs
        out_specs = [full(rows, D)] + out_specs
    return pl.pallas_call(
        functools.partial(mlp_backward, first),
        grid=(STEPS,),
        out_shape=outs + [jax.ShapeDtypeStruct(weights.shape, BF)],
        input_output_aliases={len(specs) + 3: len(outs)},
        in_specs=specs
        + [full(rows, D), pl.BlockSpec((rows, STEP_HID), lambda s: (0, s)), full(16, D), VMEM],
        out_specs=out_specs + [VMEM],
        scratch_shapes=[pltpu.VMEM((rows, D), F32)],
        compiler_params=params(),
        cost_estimate=cost(2 * rows * D * 2 * HID * 2, 12 << 20),
        name="mlp_backward",
    )(*operands, middle, slope, vecs, weights)


def attention_backward(
    grad_ref,
    own_ref,
    got_ref,
    mid_ref,
    hid_ref,
    qkv_ref,
    lse_ref,
    vecs,
    kept,
    weights,
    gm_ref,
    gb_ref,
    gp_ref,
    part_ref,
    sums_ref,
    _,
):
    rows = grad_ref.shape[0]
    centre, rstd = stats(mid_ref[...])
    grad_two = own_ref[...].astype(F32) + got_ref[...].astype(F32)
    grad_middle = grad_ref[...].astype(F32) + norm_back(
        grad_two, centre * rstd, rstd, vecs[4:5, :]
    )
    gm_ref[...] = grad_middle
    gb = grad_middle.astype(BF)
    gb_ref[...] = gb
    sums_ref[...] = jnp.zeros_like(sums_ref)
    sums_ref[3:4, :] = jnp.sum(gb.astype(F32), axis=0, keepdims=True)
    grad_att = (
        dot_nt(gb[:, 0:WID], weights[D : D + WID, WID:D])
        + dot_nt(gb[:, WID:D], weights[D + WID : 2 * D, WID:D])
    ).astype(BF)
    bias = key_bias(kept[0:1, :], rows)
    lane = lax.broadcasted_iota(jnp.int32, (rows, BLK), 1)
    for pair in range(WID // BLK):
        cols = slice(pair * BLK, (pair + 1) * BLK)
        key_cols = slice(WID + pair * BLK, WID + (pair + 1) * BLK)
        value_cols = slice(2 * WID + pair * BLK, 2 * WID + (pair + 1) * BLK)
        q = qkv_ref[:, cols] * jnp.asarray(0.125, BF)
        k = qkv_ref[:, key_cols]
        v = qkv_ref[:, value_cols]
        g = grad_att[:, cols]
        got = []
        for half in range(2):
            head = 2 * pair + half
            scores = dot_nt(lane_half(q, half), k) + bias
            att = jnp.exp(scores - lse_ref[:, head : head + 1])
            grad_a = dot_nt(lane_half(g, half), v)
            inner = jnp.sum(att * grad_a, axis=-1, keepdims=True)
            grad_s = (att * (grad_a - inner)).astype(BF)
            got.append((dot(grad_s, k) * 0.125, dot_tn(grad_s, q), dot_tn(att.astype(BF), g)))
        for at, where in enumerate((cols, key_cols, value_cols)):
            gp_ref[:, where] = jnp.where(lane < HEAD_DIM, got[0][at], got[1][at]).astype(BF)
    sums_ref[2:3, 0:WID] = jnp.sum(gp_ref[:, 0:WID].astype(F32), axis=0, keepdims=True)
    sums_ref[2:3, WID:D] = jnp.sum(gp_ref[:, 2 * WID :].astype(F32), axis=0, keepdims=True)
    grad = (
        dot_nt(gp_ref[:, 0:WID], weights[0:D, 0:WID])
        + dot_nt(gp_ref[:, WID : 2 * WID], weights[0:D, WID:D])
        + dot_nt(gp_ref[:, 2 * WID :], weights[D : 2 * D, 0:WID])
    )
    part_ref[...] = grad.astype(BF)
    centre, rstd = stats(hid_ref[...].astype(F32))
    sums_ref[0:1, :] = jnp.sum(grad * (centre * rstd), axis=0, keepdims=True)
    sums_ref[1:2, :] = jnp.sum(grad, axis=0, keepdims=True)


def call_attention_backward(*args):
    rows = args[0].shape[0]
    outs = [
        jax.ShapeDtypeStruct((rows, D), F32),
        jax.ShapeDtypeStruct((rows, D), BF),
        jax.ShapeDtypeStruct((rows, 3 * WID), BF),
        jax.ShapeDtypeStruct((rows, D), BF),
        jax.ShapeDtypeStruct((8, D), F32),
    ]
    return pl.pallas_call(
        attention_backward,
        grid=(1,),
        out_shape=outs + [jax.ShapeDtypeStruct(args[-1].shape, BF)],
        input_output_aliases={len(args) - 1: len(outs)},
        in_specs=[full(*a.shape) for a in args[:-1]] + [VMEM],
        out_specs=[full(*o.shape) for o in outs] + [VMEM],
        compiler_params=params(),
        cost_estimate=cost(2 * rows * D * 4 * WID * 3, 8 << 20),
        name="attention_backward",
    )(*args)


def mlp_grads(slot_own, slot_par, *refs):
    acts, gds, n2s, gus = refs[0:2], refs[2:4], refs[4:6], refs[6:8]
    own_ref, par_ref, down_buf, up_buf, sems = refs[8:]
    step = pl.program_id(0)
    at = lax.rem(step, 2)
    tiles = STEP_HID // 2 // BLK

    def start(of_step):
        part = lax.rem(of_step, 2)
        first = lax.rem(of_step, STEPS) * tiles

        def send(slots, out):
            def one(index, carry):
                tile = lax.div(index, 8)
                block = lax.rem(index, 8)
                down_row = pl.multiple_of(slots[128 + (first + tile) * 8 + block] * BLK, BLK)
                up_row = pl.multiple_of(slots[64 + block * 8 + first + tile] * BLK, BLK)
                tile_row = pl.multiple_of(tile * BLK, BLK)
                block_row = pl.multiple_of(block * BLK, BLK)
                pltpu.make_async_copy(
                    down_buf.at[part, pl.ds(tile_row, BLK), pl.ds(block_row, BLK)],
                    out.at[pl.ds(down_row, BLK), :],
                    sems.at[part],
                ).start()
                pltpu.make_async_copy(
                    up_buf.at[part, pl.ds(block_row, BLK), pl.ds(tile_row, BLK)],
                    out.at[pl.ds(up_row, BLK), :],
                    sems.at[part],
                ).start()
                return carry

            lax.fori_loop(0, tiles * 8, one, 0)

        pl.when(of_step < STEPS)(lambda: send(slot_own, own_ref))
        pl.when(of_step >= STEPS)(lambda: send(slot_par, par_ref))

    def wait(of_step):
        part = lax.rem(of_step, 2)
        for buf in (down_buf, up_buf):
            pltpu.make_async_copy(buf.at[part], buf.at[part], sems.at[part]).wait()

    @pl.when(step >= 2)
    def _():
        wait(step - 2)

    down_buf[at] = sum(dot_tn(a[...], g[...]) for a, g in zip(acts, gds)).astype(BF)
    up_buf[at] = sum(dot_tn(n[...], g[...]) for n, g in zip(n2s, gus)).astype(BF)
    start(step)

    @pl.when(step == 2 * STEPS - 1)
    def _():
        wait(step - 1)
        wait(step)


def call_mlp_grads(slots, acts, gds, n2s, gus):
    rows = gds[0].shape[0]
    wide = STEP_HID // 2
    by_hidden = pl.BlockSpec((rows, wide), lambda s, a, b: (0, s))
    whole = pl.BlockSpec((rows, D), lambda s, a, b: (0, 0))
    buffer = pltpu.HBM((SHARE_TILES * BLK, BLK), BF)
    return pl.pallas_call(
        mlp_grads,
        grid_spec=pltpu.PrefetchScalarGridSpec(
            num_scalar_prefetch=2,
            grid=(2 * STEPS,),
            in_specs=[by_hidden] * 2 + [whole] * 4 + [by_hidden] * 2,
            out_specs=[ANY, ANY],
            scratch_shapes=[
                pltpu.VMEM((2, wide, D), BF),
                pltpu.VMEM((2, D, wide), BF),
                pltpu.SemaphoreType.DMA((2,)),
            ],
        ),
        out_shape=[buffer, buffer],
        compiler_params=params(),
        cost_estimate=cost(2 * 2 * rows * D * 2 * HID * 2, 16 << 20),
        name="mlp_grads",
    )(*slots, *acts, *gds, *n2s, *gus)


def attention_grads(slot_own, slot_par, *refs):
    atts, gbs, n1s, gqs, gks, gvs = (refs[2 * i : 2 * i + 2] for i in range(6))
    own_ref, par_ref, out_buf, qkv_buf, sems = refs[14:]
    step = at = pl.program_id(0)
    per_share = D // NARROW // BLK

    def start(of_step):
        part = of_step

        def send(slots, out):
            def one(block, carry):
                block_row = pl.multiple_of(block * BLK, BLK)
                for column in range(per_share):
                    cols = pl.ds(column * BLK, BLK)
                    row = pl.multiple_of(slots[48 + column * 8 + block] * BLK, BLK)
                    pltpu.make_async_copy(
                        out_buf.at[part, cols, pl.ds(block_row, BLK)],
                        out.at[pl.ds(row, BLK), :],
                        sems.at[part],
                    ).start()
                    for third in range(3):
                        tile = block * 6 + third * 2 + column
                        row = pl.multiple_of(slots[tile] * BLK, BLK)
                        pltpu.make_async_copy(
                            qkv_buf.at[part, third, pl.ds(block_row, BLK), cols],
                            out.at[pl.ds(row, BLK), :],
                            sems.at[part],
                        ).start()
                return carry

            lax.fori_loop(0, 8, one, 0)

        pl.when(of_step == 0)(lambda: send(slot_own, own_ref))
        pl.when(of_step == 1)(lambda: send(slot_par, par_ref))

    def wait(part):
        for buf in (out_buf, qkv_buf):
            pltpu.make_async_copy(buf.at[part], buf.at[part], sems.at[part]).wait()

    out_buf[at] = sum(dot_tn(a[...], g[...]) for a, g in zip(atts, gbs)).astype(BF)
    for third, grads in enumerate((gqs, gks, gvs)):
        qkv_buf[at, third] = sum(dot_tn(n[...], g[...]) for n, g in zip(n1s, grads)).astype(BF)
    start(step)

    @pl.when(step == 1)
    def _():
        wait(0)
        wait(1)


def call_attention_grads(slots, atts, gbs, n1s, gps, own, par):
    rows = gbs[0].shape[0]
    width = WID // 2
    whole = pl.BlockSpec((rows, D), lambda s, a, b: (0, 0))

    def by_column(third):
        return pl.BlockSpec((rows, width), lambda s, a, b: (0, third * 2 + s))

    return pl.pallas_call(
        attention_grads,
        grid_spec=pltpu.PrefetchScalarGridSpec(
            num_scalar_prefetch=2,
            grid=(2,),
            in_specs=[by_column(0)] * 2
            + [whole] * 4
            + [by_column(0)] * 2
            + [by_column(1)] * 2
            + [by_column(2)] * 2
            + [ANY, ANY],
            out_specs=[ANY, ANY],
            scratch_shapes=[
                pltpu.VMEM((2, width, D), BF),
                pltpu.VMEM((2, 3, D, width), BF),
                pltpu.SemaphoreType.DMA((2,)),
            ],
        ),
        out_shape=[pltpu.HBM(own.shape, BF)] * 2,
        input_output_aliases={14: 0, 15: 1},
        compiler_params=params(),
        cost_estimate=cost(2 * 2 * rows * D * 4 * WID, 8 << 20),
        name="attention_grads",
    )(*slots, *atts, *gbs, *n1s, *gps, *gps, *gps, own, par)


def place_of(tile, share):
    quarter = WID // 2
    block, rest = tile // 6, tile % 6
    third, column = rest // 2, rest % 2
    qkv_row = jnp.where(third == 2, D, 0) + block * BLK
    qkv_col = jnp.where(third == 1, WID, 0) + share * quarter + column * BLK
    out = tile - 48
    out_block, out_col = out // 8, out % 8
    out_row = D + jnp.where(out_col >= 4, WID, 0) + share * quarter + out_block * BLK
    out_col = WID + (out_col % 4) * BLK
    up = tile - 64
    up_row, up_col = 2 * D + share * D + (up // 8) * BLK, (up % 8) * BLK
    down = tile - 128
    down_row, down_col = 4 * D + share * D + (down // 8) * BLK, (down % 8) * BLK
    kind = (tile >= 48).astype(jnp.int32) + (tile >= 64) + (tile >= 128)
    row = jnp.select([kind == 0, kind == 1, kind == 2], [qkv_row, out_row, up_row], down_row)
    col = jnp.select([kind == 0, kind == 1, kind == 2], [qkv_col, out_col, up_col], down_col)
    return row, col


def assemble_kernel(plan, rows, cols, *refs):
    sources = refs[: len(plan)]
    out_ref, sem = refs[-2:]
    for source, (share, first, count) in zip(sources, plan):

        def one(i, carry, source=source, share=share, first=first):
            row = pl.multiple_of(rows[share, first + i], BLK)
            col = pl.multiple_of(cols[share, first + i], BLK)
            pltpu.make_async_copy(
                source.at[pl.ds(pl.multiple_of(i * BLK, BLK), BLK), :],
                out_ref.at[pl.ds(row, BLK), pl.ds(col, BLK)],
                sem,
            ).start()
            return carry

        lax.fori_loop(0, count, one, 0, unroll=4 if count % 4 == 0 else 1)
    for source, (_, _, count) in zip(sources, plan):
        tiles = source.at[pl.ds(0, count * BLK), :]
        pltpu.make_async_copy(tiles, tiles, sem).wait()


def assemble(table, pieces):
    plan = [piece[:3] for piece in pieces]
    args = list(table) + [pltpu.with_memory_space_constraint(p[3], pltpu.HBM) for p in pieces]
    return pl.pallas_call(
        functools.partial(assemble_kernel, plan),
        out_shape=jax.ShapeDtypeStruct((6 * D, D), BF),
        in_specs=[SMEM, SMEM] + [ANY] * len(pieces),
        out_specs=ANY,
        scratch_shapes=[pltpu.SemaphoreType.DMA],
        compiler_params=params(),
        cost_estimate=cost(0, BLK),
        name="assemble",
    )(*args)


def ring(size):
    order = list(range(0, size, 2)) + list(range(size - 1, 0, -2))
    ahead = [(order[i], order[(i + 1) % size]) for i in range(size)]
    position = [order.index(i) for i in range(size)]
    return order, position, ahead, [(b, a) for a, b in ahead]


def after(value, *earlier):
    return lax.optimization_barrier((value, *earlier))[0]


def need_order(size):
    far = size // 2
    order = [far]
    for step in range(far - 1, 0, -1):
        order += [step, size - step]
    return order + [0]


class Gather:
    def __init__(self, unit, size, per_device):
        _, _, self.ahead, self.behind = ring(size)
        self.size, self.per_device, self.step_count = size, per_device, 0
        self.up = self.down = unit

    def step(self, *earlier):
        self.step_count += 1
        step, far, front = self.step_count, self.size // 2, self.per_device // 2
        up, down = self.up, self.down
        if step == far:
            up, down = up[: front * BLK], down[front * BLK :]
        up, down, *_ = lax.optimization_barrier((up, down, *earlier))
        self.sent = (up, down)
        self.up = lax.ppermute(up, "wide", self.ahead)
        self.down = lax.ppermute(down, "wide", self.behind)
        if step < far:
            return [
                (self.size - step, 0, self.per_device, self.up),
                (step, 0, self.per_device, self.down),
            ]
        return [
            (far, 0, front, self.up),
            (far, front, self.per_device - front, self.down),
        ]


class Scatter:
    def __init__(self, unit_of, size, cut):
        _, _, self.ahead, self.behind = ring(size)
        self.unit_of, self.size, self.cut, self.left = unit_of, size, cut, size // 2

    def step(self, *earlier):
        cut = self.cut
        if self.left == self.size // 2:
            last = self.unit_of(self.left)
            up, down = last[:cut], last[cut:]
        else:
            up, down = self.unit_of(self.left), self.unit_of(self.size - self.left)
            got_up, got_down = self.up.astype(F32), self.down.astype(F32)
            if self.left == self.size // 2 - 1:
                up = jnp.concatenate([up[:cut] + got_up, up[cut:]])
                down = jnp.concatenate([down[:cut], down[cut:] + got_down])
            else:
                up, down = up + got_up, down + got_down
        up, down = up.astype(BF), down.astype(BF)
        up, down, *_ = lax.optimization_barrier((up, down, *earlier))
        self.sent = (up, down)
        self.up = lax.ppermute(up, "wide", self.ahead)
        self.down = lax.ppermute(down, "wide", self.behind)
        self.left -= 1

    def result(self):
        return self.unit_of(0) + self.up.astype(F32) + self.down.astype(F32)


def mesh_bits():
    out, base = [], 1
    for axis in ("narrow", "wide"):
        size, bit = lax.axis_size(axis), 1
        while bit < size:
            out.append((base * bit, axis, [(i, i ^ bit) for i in range(size)]))
            bit *= 2
        base *= size
    return out


def tile_ids(share):
    tile_rows = D // BLK
    shard_cols = D // (NARROW * BLK)
    shard_hidden = FF // (NARROW * BLK)
    count_qkv = tile_rows * 3 * tile_rows
    start_up = count_qkv + tile_rows * tile_rows
    start_down = start_up + tile_rows * (FF // BLK)
    row_part = jnp.arange(tile_rows)[:, None, None]
    third = jnp.arange(3)[None, :, None]
    column_part = jnp.arange(shard_cols)[None, None, :]
    qkv_ids = (
        row_part * 3 * tile_rows + third * tile_rows + share * shard_cols + column_part
    ).reshape(-1)
    out_ids = (
        count_qkv
        + (share * shard_cols + jnp.arange(shard_cols)[:, None]) * tile_rows
        + jnp.arange(tile_rows)[None, :]
    ).reshape(-1)
    up_ids = (
        start_up
        + jnp.arange(tile_rows)[:, None] * (FF // BLK)
        + share * shard_hidden
        + jnp.arange(shard_hidden)[None, :]
    ).reshape(-1)
    down_ids = (
        start_down
        + (share * shard_hidden + jnp.arange(shard_hidden)[:, None]) * tile_rows
        + jnp.arange(tile_rows)[None, :]
    ).reshape(-1)
    return jnp.concatenate([qkv_ids, out_ids, up_ids, down_ids])


def share_vectors(small_all, me):
    pieces = [small_all[i * D : (i + 1) * D] for i in range(8)]
    bias_up = small_all[8 * D :]

    def both(vector, width):
        own = lax.dynamic_slice_in_dim(vector, me * width, width)
        par = lax.dynamic_slice_in_dim(vector, (me ^ 1) * width, width)
        return jnp.concatenate([own, par])

    quarter = D // NARROW
    heads = jnp.concatenate([both(pieces[2], quarter), both(pieces[3], quarter)])
    rows = [pieces[0], pieces[1], heads, pieces[4], pieces[5], pieces[6], pieces[7]]
    up = both(bias_up, FF // NARROW)
    rows = rows + [up[0:D], up[D:]]
    return jnp.pad(jnp.stack(rows), ((0, 7), (0, 0)))


def small_vector(mlp_sums, att_sums, me):
    half = me // 2
    mine = [(half == t).astype(F32) for t in range(2)]
    mlp = mlp_sums[0] + mlp_sums[1]
    att = att_sums[0] + att_sums[1]
    bias_down = mine[0] * mlp_sums[0][2] + mine[1] * mlp_sums[1][2]
    bias_out = mine[0] * att_sums[0][3] + mine[1] * att_sums[1][3]
    odd = (me % 2) == 1

    def spread(own, par):
        placed = jnp.where(odd, jnp.concatenate([par, own]), jnp.concatenate([own, par]))
        return [jnp.where(half == 0, placed, 0.0), jnp.where(half == 1, placed, 0.0)]

    quarter = D // NARROW
    heads = att[2]
    return jnp.concatenate(
        [att[0], att[1]]
        + spread(heads[0:quarter], heads[quarter : 2 * quarter])
        + spread(heads[2 * quarter : 3 * quarter], heads[3 * quarter :])
        + [bias_out, mlp[0], mlp[1], bias_down]
        + spread(mlp[3], mlp[4])
    )


def total_over_mesh(value):
    value = jnp.broadcast_to(value.reshape(1, 1), (8, BLK))
    for axis in ("narrow", "wide"):
        size, bit = lax.axis_size(axis), 1

        def swap(flip, value=None, axis=axis, size=size):
            return lax.ppermute(value, axis, [(i, i ^ flip) for i in range(size)])

        while bit < size:
            if 2 * bit < size:
                near, far, both = (swap(bit * k, value) for k in (1, 2, 3))
                value = (value + near) + (far + both)
            else:
                value = value + swap(bit, value)
            bit *= 4
    return value[0, 0]


def update_kernel(clip_ref, grad0, grad1, left, right, first, second, master, *outs):
    new_first, new_second, new_master, new_weights = outs
    step = pl.program_id(0)
    half = pl.num_programs(0) // 2
    clip = clip_ref[0]
    grads = (grad0, grad1)
    count = left.shape[1]
    for base in range(0, count, 4):
        blocks = range(base, min(base + 4, count))
        lefts = [left[0, b].astype(BF) for b in blocks]
        rights = [right[0, b].astype(BF) for b in blocks]
        terms = [
            jnp.where(step < half, *(g[b * BLK : (b + 1) * BLK, :] for g in grads)).astype(BF)
            for b in blocks
        ]
        terms = [dot_tn(a, x).astype(BF) for a, x in zip(lefts, terms)]
        terms = [clip * dot(x, b) for x, b in zip(terms, rights)]
        ones = [0.5 * first[0, b] + 0.5 * x for b, x in zip(blocks, terms)]
        twos = [0.5 * second[0, b] + 0.5 * x * x for b, x in zip(blocks, terms)]
        terms = [(a / (jnp.sqrt(b) + 1e-08)).astype(BF) for a, b in zip(ones, twos)]
        terms = [dot(a, x).astype(BF) for a, x in zip(lefts, terms)]
        terms = [dot_nt(x, b) for x, b in zip(terms, rights)]
        for b, one, two, turned in zip(blocks, ones, twos, terms):
            new_first[0, b] = one
            new_second[0, b] = two
            weights = master[0, b] - 0.02 * turned
            new_master[0, b] = weights
            new_weights[0, b] = weights.astype(BF)


def update(clip, grads, left, right, first, second, master):
    count = left.shape[1]
    group = 8 if count % 8 == 0 else 1
    steps = count // group
    spec = pl.BlockSpec((1, group, BLK, BLK), lambda i: (i // steps, i % steps, 0, 0))
    low = pl.BlockSpec((group * BLK, BLK), lambda i: (jnp.minimum(i, steps - 1), 0))
    high = pl.BlockSpec((group * BLK, BLK), lambda i: (jnp.maximum(i - steps, 0), 0))
    shape = jax.ShapeDtypeStruct(master.shape, F32)
    return pl.pallas_call(
        update_kernel,
        grid=(2 * steps,),
        out_shape=[shape, shape, shape, jax.ShapeDtypeStruct(master.shape, BF)],
        in_specs=[SMEM, low, high] + [spec] * 5,
        out_specs=[spec] * 4,
        compiler_params=params(56),
        cost_estimate=cost(count * 16 * BLK**3, count * BLK * BLK * 2 * 38),
        name="update",
    )(clip, *grads, left, right, first, second, master)


def shards(
    images,
    cotangent,
    kept_tokens,
    owner_slots,
    master_blocks,
    small_params,
    left_basis,
    right_basis,
    first_moment,
    second_moment,
    small_first,
    small_second,
):
    me = lax.axis_index("narrow")
    half, core = me // 2, me % 2
    wide = lax.axis_size("wide")
    per_device = master_blocks.shape[1]
    own_small = small_params.shape[1]
    own_images = images.shape[0]
    rows = own_images * S

    device = lax.axis_index("wide") * NARROW + me
    by_distance = jnp.arange(wide * NARROW) ^ device

    def chunks(own):
        other = lax.ppermute(own, "narrow", ACROSS)
        return [jnp.where(half == t, own, other) for t in range(2)]

    kept = [
        lax.dynamic_slice_in_dim(kept_tokens, (2 * t + core) * own_images, own_images, 0)
        .T.reshape(1, rows)
        .astype(F32)
        for t in range(2)
    ]

    order, position, _, _ = ring(wide)
    place = jnp.take(jnp.asarray(position, jnp.int32), lax.axis_index("wide"))
    around = jnp.take(jnp.asarray(order, jnp.int32), (place + jnp.arange(wide)) % wide)

    needed = need_order(wide)
    turns = [needed.index(distance) for distance in range(wide)]
    slots, tables = [], []
    for layer in range(LAYERS):
        owners = owner_slots[layer]
        layer_slots, layer_rows, layer_cols = [], [], []
        for at, share in enumerate((me, me ^ 1)):
            slot = jnp.take(owners, tile_ids(share))
            at_wide, at_pos = slot // per_device // NARROW, slot % per_device
            distance = (jnp.take(jnp.asarray(position, jnp.int32), at_wide) - place) % wide
            relative = distance * per_device + at_pos
            turn = jnp.take(jnp.asarray(turns, jnp.int32), distance)
            layer_slots.append(turn * per_device + at_pos)
            here = relative[None, :] == jnp.arange(SHARE_TILES)[:, None]
            tile = jnp.sum(jnp.where(here, jnp.arange(SHARE_TILES)[None, :], 0), axis=1)
            row, col = place_of(tile, at)
            layer_rows.append(row)
            layer_cols.append(col)
        slots.append(layer_slots)
        tables.append((jnp.stack(layer_rows), jnp.stack(layer_cols)))

    def by_token(value):
        return value.transpose(1, 0, 2).reshape(rows, D)

    def by_image(value):
        return value.reshape(S, own_images, D).transpose(1, 0, 2)

    def core_swap(value):
        return lax.ppermute(value, "narrow", CORE)

    def exchange(part):
        return lax.ppermute(part, "narrow", ACROSS)

    units = [
        master_blocks[layer].astype(BF).reshape(per_device * BLK, BLK) for layer in range(LAYERS)
    ]

    def swapped(pieces):
        return [piece + (core_swap(piece[3]),) for piece in pieces]

    def place_pieces(layer, pieces):
        group = [
            (share, distance * per_device + first, count, pair[share])
            for distance, first, count, *pair in pieces
            for share in range(2)
        ]
        return assemble(tables[layer], group)

    steps = wide // 2
    own_small_rows = small_params.astype(BF).reshape(1, -1)
    small_rows = own_small_rows
    bits = mesh_bits()
    near_bits, far_bits = bits[:2], bits[2:]
    per_window = -(-len(far_bits) // max(steps - 1, 1))

    def grow(rows, some_bits):
        for _, axis, perm in some_bits:
            rows = jnp.concatenate([rows, lax.ppermute(rows, axis, perm)])
        return rows

    gather = Gather(units[0], wide, per_device)
    arrived = [(0, 0, per_device, units[0])] + gather.step()
    small_rows = grow(small_rows, near_bits)
    inputs = [by_token(images), by_token(cotangent)]
    placed, extra = [], [small_rows]
    brought = []
    for step in range(2, steps + 1):
        latest = swapped(arrived)
        arrived = gather.step(*extra)
        placed += latest
        extra = [piece[4] for piece in latest]
        if step == 2:
            brought = chunks(after(inputs[0], *gather.sent))
            extra += brought + [inputs[1]]
        elif step == 3:
            late = exchange(after(inputs[1], *gather.sent))
        at = (step - 2) * per_window
        small_rows = grow(small_rows, far_bits[at : at + per_window])
        if step < steps:
            extra.append(small_rows)
    hidden_in = brought
    next_unit = after(units[1], gather.up, gather.down, late)
    gather_next = Gather(next_unit, wide, per_device)
    arrived_next = [(0, 0, per_device, next_unit)] + gather_next.step()
    last = [piece[:3] + (after(piece[3], *gather_next.sent),) for piece in arrived]
    weights = [place_pieces(0, placed + swapped(last))]
    cot = [jnp.where(half == t, inputs[1], late) for t in range(2)]

    in_order = jnp.take(small_rows, by_distance, axis=0).astype(F32)
    small_all = in_order.reshape(-1, LAYERS, own_small).transpose(1, 0, 2).reshape(LAYERS, -1)
    vecs = [share_vectors(small_all[layer], me) for layer in range(LAYERS)]

    saved = []
    state = None
    for layer in range(LAYERS):
        kept_layer = []
        for t in range(2):
            if layer == 0:
                hidden = hidden_in[t]
                if t == 1:
                    placed = swapped(arrived_next)
                    arrived_next = gather_next.step(part)
                    hidden = after(hidden, *gather_next.sent)
                *out, weights[layer] = call_attention_forward(
                    True, (hidden,), vecs[0], kept[t], weights[layer]
                )
            else:
                hidden, *out, weights[layer] = call_attention_forward(
                    False, state[t] + (vecs[layer - 1],), vecs[layer], kept[t], weights[layer]
                )
            n1, qkv, lse, att, part = out
            kept_layer.append([hidden, n1, qkv, lse, att, part, exchange(part)])
        kept_layer[0][5] = after(kept_layer[0][5], kept_layer[1][5])
        state = []
        for t in range(2):
            hidden, n1, qkv, lse, att, part, got = kept_layer[t]
            if layer == 0 and t == 1:
                placed += swapped(arrived_next)
                arrived_next = gather_next.step(down_part)
                placed += swapped(arrived_next)
                arrived_next = gather_next.step()
                part = after(part, *gather_next.sent, *vecs[1:])
            middle, n2, act, slope, down_part, weights[layer] = call_mlp_forward(
                layer == 0, hidden, part, got, vecs[layer], weights[layer]
            )
            kept_layer[t] = (hidden, n1, qkv, lse, att, middle, n2, act, slope)
            if layer < LAYERS - 1:
                state.append((middle, down_part, exchange(down_part)))
            else:
                state.append((middle, down_part))
        saved.append(kept_layer)
        if layer == 0:
            for _ in range(5, steps + 1):
                placed += swapped(arrived_next)
                arrived_next = gather_next.step()
            weights.append(place_pieces(1, placed + swapped(arrived_next)))

    def mine(pair):
        return jnp.where(half == 0, pair[0], pair[1])

    def theirs(pair):
        return jnp.where(half == 0, pair[1], pair[0])

    down_parts = [state[t][1] for t in range(2)]
    middles = [state[t][0] for t in range(2)]
    upstream = None
    reduced = [None] * LAYERS
    small_terms = [None] * LAYERS
    pending = None
    for layer in reversed(range(LAYERS)):
        kept_layer = saved[layer]
        top = layer == LAYERS - 1
        work = []
        for t in range(2):
            hidden, n1, qkv, lse, att, middle, n2, act, slope = kept_layer[t]
            if top:
                grad = cot[t]
                gd, gu, part, sums, weights[layer] = call_mlp_backward(
                    True, (grad,), middle, slope, vecs[layer], weights[layer]
                )
            else:
                state = upstream[t]
                state = (after(state[0], *pending.sent),) + state[1:]
                grad, gd, gu, part, sums, weights[layer] = call_mlp_backward(
                    False, state + (vecs[layer + 1],), middle, slope, vecs[layer], weights[layer]
                )
                if t == 0:
                    pending.step(part)
            work.append([grad, gd, gu, part, sums, exchange(part)])
        gds = [w[1] for w in work]
        if pending is not None:
            gds[0] = after(gds[0], *pending.sent)
        own, par = call_mlp_grads(
            slots[layer],
            [k[7] for k in kept_layer],
            gds,
            [k[6] for k in kept_layer],
            [w[2] for w in work],
        )
        if pending is not None:
            pending.step(own)
        back = []
        for t in range(2):
            hidden, n1, qkv, lse, att, middle, n2, act, slope = kept_layer[t]
            grad, gd, gu, part, sums, got = work[t]
            if pending is not None:
                part = after(part, *pending.sent)
            gm, gb, gp, att_part, att_sums, weights[layer] = call_attention_backward(
                grad, part, got, middle, hidden, qkv, lse, vecs[layer], kept[t], weights[layer]
            )
            back.append((gm, gb, gp, att_part, att_sums))
        if pending is not None:
            pending.step(back[1][3])
            while pending.left > 0:
                pending.step()
            own = after(own, *pending.sent)
        if layer > 0:
            got = [exchange(back[t][3]) for t in range(2)]
            own = after(own, got[0])
            upstream = [
                (back[0][0], back[0][3], got[0], kept_layer[0][0]),
                (back[1][0], back[1][3], got[1], kept_layer[1][0]),
            ]
        own, par = call_attention_grads(
            slots[layer],
            [k[4] for k in kept_layer],
            [b[1] for b in back],
            [k[1] for k in kept_layer],
            [b[2] for b in back],
            own,
            par,
        )
        if pending is not None:
            own = after(own, pending.up, pending.down)
        terms = small_vector([w[4] for w in work], [b[4] for b in back], me)
        small_terms[layer] = terms.reshape(-1, own_small)
        unit_len = per_device * BLK

        first_got = core_swap(par[:unit_len])
        earlier = pending
        pending = Scatter(None, wide, (per_device // 2) * BLK)

        def first_unit(distance, own=own, got=first_got, unit_len=unit_len):
            return own[:unit_len].astype(F32) + got.astype(F32)

        pending.unit_of = first_unit
        if layer == 0:
            backward_bits = mesh_bits()[::-1]
            small_rows = jnp.take(jnp.concatenate(small_terms, axis=1), by_distance, axis=0)
            for bit, axis, perm in backward_bits[:per_window]:
                small_rows = small_rows[:bit] + lax.ppermute(small_rows[bit:], axis, perm)
            backward_bits = backward_bits[per_window:]
            pending.step(small_rows)
        else:
            pending.step()
        rest = core_swap(after(par, *pending.sent))
        if earlier is not None:
            earlier.up = after(earlier.up, *pending.sent)
            reduced[layer + 1] = earlier.result()

        def unit_of(distance, own=own, rest=rest, unit_len=unit_len):
            at = turns[distance] * unit_len
            return own[at : at + unit_len].astype(F32) + rest[at : at + unit_len].astype(F32)

        pending.unit_of = unit_of

    final = mine(middles) + (
        mine(down_parts).astype(F32)
        + exchange(after(theirs(down_parts), rest)).astype(F32)
        + vecs[LAYERS - 1][6]
    )
    block_output = by_image(final.astype(BF))
    parts = [b[3] for b in back]
    last_part = exchange(after(theirs(parts), rest)).astype(F32)
    small_rows = after(small_rows, rest)
    local_sum = input_grad = None
    while pending.left > 0:
        if local_sum is None:
            pending.step()
        else:
            for bit, axis, perm in backward_bits[:per_window]:
                small_rows = small_rows[:bit] + lax.ppermute(small_rows[bit:], axis, perm)
            backward_bits = backward_bits[per_window:]
            pending.step(small_rows)
        early = list(pending.sent)
        if local_sum is None:
            upper = [after(grads, *pending.sent) for grads in reduced[1:]]
            local_sum = sum(jnp.sum(grads * grads) for grads in upper)
            early.append(local_sum)
        elif input_grad is None:
            hidden = mine([k[0] for k in saved[0]]).astype(F32)
            centre, rstd = stats(hidden)
            lower = norm_back(
                mine(parts).astype(F32) + after(last_part, *pending.sent),
                centre * rstd,
                rstd,
                vecs[0][0:1],
            )
            input_grad = by_image(mine([b[0] for b in back]) + lower)
            early += [input_grad, block_output]
        small_rows = after(small_rows, *early)
    for bit, axis, perm in backward_bits:
        small_rows = small_rows[:bit] + lax.ppermute(small_rows[bit:], axis, perm)
    reduced[0] = pending.result()
    grad_small = small_rows.reshape(LAYERS, own_small)
    local_sum = local_sum + jnp.sum(grad_small * grad_small) + jnp.sum(reduced[0] * reduced[0])
    grad_norm = jnp.sqrt(total_over_mesh(local_sum))
    clip_factor = 1.0 / jnp.maximum(grad_norm, 1.0)
    new_first, new_second, new_master, new_weights = update(
        clip_factor.reshape(1),
        reduced,
        left_basis,
        right_basis,
        first_moment,
        second_moment,
        master_blocks,
    )
    clipped_small = clip_factor * grad_small
    new_small_first = 0.5 * small_first + 0.5 * clipped_small
    new_small_second = 0.5 * small_second + 0.5 * clipped_small * clipped_small
    new_small = small_params - 0.3 * new_small_first / (jnp.sqrt(new_small_second) + 1e-08)
    return (
        block_output,
        input_grad,
        grad_norm.reshape(1),
        new_first,
        new_second,
        new_master,
        new_weights,
        new_small_first,
        new_small_second,
        new_small,
        new_small.astype(BF),
    )


def solution(mesh):
    both = ("wide", "narrow")
    rows = P(both, None, None)
    blocks = P(None, both, None, None)
    small = P(None, both)
    in_specs = (
        rows,
        rows,
        P("wide", None),
        P(),
        blocks,
        small,
        blocks,
        blocks,
        blocks,
        blocks,
        small,
        small,
    )
    out_specs = (rows, rows, P(), blocks, blocks, blocks, blocks, small, small, small, small)
    return jax.shard_map(shards, mesh=mesh, in_specs=in_specs, out_specs=out_specs, check_vma=False)
```
